32 devices in a mesh: rows: 16 (over z, x, core), seq: 2 (over y).
Axes of the slice: x: 2, y: 2, z: 4, core: 2. Of those that a mesh axis runs over, the one named last changes fastest.
Arguments:
- encoder_input: bfloat16 [32, 512, 768], P('rows', 'seq'), may hold values from -23 to 23
- decoder_input: bfloat16 [32, 128, 768], P('rows', 'seq'), may hold values from -23 to 23
- segment_lengths: int32 [32, 8], P('rows'), may hold values from 0 to 512, as said below
- target_lengths: int32 [32], P('rows'), may hold values from 32 to 128, as said below
- bucket_table: int32 [1023], replicated, may hold values from 0 to 31
- encoder_attention_gain: bfloat16 [768], P(('rows', 'seq')), may hold values from 0.5 to 1.5
- encoder_query: bfloat16 [768, 768], P(('rows', 'seq')), may hold values from -0.109375 to 0.109375
- encoder_key: bfloat16 [768, 768], P(('rows', 'seq')), may hold values from -0.109375 to 0.109375
- encoder_value: bfloat16 [768, 768], P(('rows', 'seq')), may hold values from -0.21875 to 0.21875
- encoder_outward: bfloat16 [768, 768], P(('rows', 'seq')), may hold values from -0.875 to 0.875
- encoder_position_bias: float32 [32, 12], replicated, may hold values from -4 to 4
- encoder_feedforward_gain: bfloat16 [768], P(('rows', 'seq')), may hold values from 0.5 to 1.5
- encoder_widen: bfloat16 [768, 3072], P(('rows', 'seq')), may hold values from -0.21875 to 0.21875
- encoder_narrow: bfloat16 [3072, 768], P(('rows', 'seq')), may hold values from -0.15625 to 0.15625
- encoder_final_gain: bfloat16 [768], P(('rows', 'seq')), may hold values from 0.5 to 1.5
- decoder_self_gain: bfloat16 [768], P(('rows', 'seq')), may hold values from 0.5 to 1.5
- decoder_query: bfloat16 [768, 768], P(('rows', 'seq')), may hold values from -0.109375 to 0.109375
- decoder_key: bfloat16 [768, 768], P(('rows', 'seq')), may hold values from -0.109375 to 0.109375
- decoder_value: bfloat16 [768, 768], P(('rows', 'seq')), may hold values from -0.21875 to 0.21875
- decoder_outward: bfloat16 [768, 768], P(('rows', 'seq')), may hold values from -0.875 to 0.875
- decoder_position_bias: float32 [32, 12], replicated, may hold values from -4 to 4
- decoder_cross_gain: bfloat16 [768], P(('rows', 'seq')), may hold values from 0.5 to 1.5
- cross_query: bfloat16 [768, 768], P(('rows', 'seq')), may hold values from -0.109375 to 0.109375
- cross_key: bfloat16 [768, 768], P(('rows', 'seq')), may hold values from -0.109375 to 0.109375
- cross_value: bfloat16 [768, 768], P(('rows', 'seq')), may hold values from -0.21875 to 0.21875
- cross_outward: bfloat16 [768, 768], P(('rows', 'seq')), may hold values from -0.875 to 0.875
- decoder_feedforward_gain: bfloat16 [768], P(('rows', 'seq')), may hold values from 0.5 to 1.5
- decoder_widen: bfloat16 [768, 3072], P(('rows', 'seq')), may hold values from -0.21875 to 0.21875
- decoder_narrow: bfloat16 [3072, 768], P(('rows', 'seq')), may hold values from -0.15625 to 0.15625
- encoder_cotangent: bfloat16 [32, 512, 768], P('rows', 'seq'), may hold values from -6 to 6
- decoder_cotangent: bfloat16 [32, 128, 768], P('rows', 'seq'), may hold values from -6 to 6
Outputs:
- encoder_output: float32 [32, 512, 768], P('rows', 'seq')
- decoder_output: float32 [32, 128, 768], P('rows', 'seq')
- encoder_input_grad: float32 [32, 512, 768], P('rows', 'seq')
- decoder_input_grad: float32 [32, 128, 768], P('rows', 'seq')
- encoder_attention_gain_grad: float32 [768], P(('rows', 'seq'))
- encoder_query_grad: float32 [768, 768], P(('rows', 'seq'))
- encoder_key_grad: float32 [768, 768], P(('rows', 'seq'))
- encoder_value_grad: float32 [768, 768], P(('rows', 'seq'))
- encoder_outward_grad: float32 [768, 768], P(('rows', 'seq'))
- encoder_position_bias_grad: float32 [32, 12], replicated
- encoder_feedforward_gain_grad: float32 [768], P(('rows', 'seq'))
- encoder_widen_grad: float32 [768, 3072], P(('rows', 'seq'))
- encoder_narrow_grad: float32 [3072, 768], P(('rows', 'seq'))
- encoder_final_gain_grad: float32 [768], P(('rows', 'seq'))
- decoder_self_gain_grad: float32 [768], P(('rows', 'seq'))
- decoder_query_grad: float32 [768, 768], P(('rows', 'seq'))
- decoder_key_grad: float32 [768, 768], P(('rows', 'seq'))
- decoder_value_grad: float32 [768, 768], P(('rows', 'seq'))
- decoder_outward_grad: float32 [768, 768], P(('rows', 'seq'))
- decoder_position_bias_grad: float32 [32, 12], replicated
- decoder_cross_gain_grad: float32 [768], P(('rows', 'seq'))
- cross_query_grad: float32 [768, 768], P(('rows', 'seq'))
- cross_key_grad: float32 [768, 768], P(('rows', 'seq'))
- cross_value_grad: float32 [768, 768], P(('rows', 'seq'))
- cross_outward_grad: float32 [768, 768], P(('rows', 'seq'))
- decoder_feedforward_gain_grad: float32 [768], P(('rows', 'seq'))
- decoder_widen_grad: float32 [768, 3072], P(('rows', 'seq'))
- decoder_narrow_grad: float32 [3072, 768], P(('rows', 'seq'))
- norm_statistics: float32 [4], replicated
The draws below stay inside these ranges and needn't reach their ends.
Inputs may be any that keep to these rules, and one draw needn't show every extreme that they name: `segment_lengths`: in each row either entry 0 alone is nonzero, above 256, or all 8 entries lie in 16 to 64; among the 2 rows of each index of rows one is a single input of 512 tokens. `target_lengths`: among the 2 rows of each index of rows one has length 128.
All inputs are finite; a program needn't handle non-finite values.
Results may differ from the reference program's by a relative error of at most 0.025.
The reference program's roundings to bfloat16 on the way count: a program that leaves them out, or rounds other values in their place, can miss the bound.
Values may be sent and summed in bfloat16 or wider, within the bound.
A program may use at most 384 MiB of HBM per device.

```python
import jax
import jax.numpy as jnp
from jax import lax

D = 768
HEADS = 12
HEAD = 64
FF = 3072
BUCKETS = 32
SEGS = 8
ENC_LEN = 512
DEC_LEN = 128
ROW_DEV = 2
ROWS = 32


def row_scales(key):
    row_index = jnp.arange(ROWS, dtype=jnp.float32)
    rising = jnp.exp(jnp.log(3.0) * row_index / max(ROWS - 1, 1))
    jitter = jnp.exp(jax.random.uniform(key, (ROWS,), jnp.float32, -0.4, 0.4))
    return rising * jitter


def activation_draw(key, length):
    scale_key, value_key = jax.random.split(key)
    scales = row_scales(scale_key)[:, None, None]
    values = jnp.clip(jax.random.normal(value_key, (ROWS, length, D), jnp.float32), -5.0, 5.0)
    return (values * scales).astype(jnp.bfloat16)


def chosen_rows(key):
    forced = jax.random.randint(key, (ROWS // ROW_DEV,), 0, ROW_DEV)
    row_index = jnp.arange(ROWS, dtype=jnp.int32)
    return row_index % ROW_DEV == jnp.repeat(forced, ROW_DEV)


def draw_encoder_input(key, part):
    return activation_draw(jax.random.fold_in(key, 3), ENC_LEN)


def draw_decoder_input(key, part):
    return activation_draw(jax.random.fold_in(key, 7), DEC_LEN)


def draw_segment_lengths(key, part):
    key_mode, key_single, key_packed, key_force = jax.random.split(jax.random.fold_in(key, 13), 4)
    slot_width = ENC_LEN // SEGS
    mode_flag = jax.random.randint(key_mode, (ROWS,), 0, 2)
    single = jax.random.randint(key_single, (ROWS,), ENC_LEN // 2 + 1, ENC_LEN + 1)
    packed = jax.random.randint(key_packed, (ROWS, SEGS), slot_width // 4, slot_width + 1)
    chosen = chosen_rows(key_force)
    single = jnp.where(chosen, ENC_LEN, single)
    mode_flag = jnp.where(chosen, 0, mode_flag)
    leading = jnp.where(mode_flag == 0, single, packed[:, 0])
    remaining = jnp.where(mode_flag[:, None] == 0, 0, packed[:, 1:])
    return jnp.concatenate([leading[:, None], remaining], axis=1).astype(jnp.int32)


def draw_target_lengths(key, part):
    key_length, key_force = jax.random.split(jax.random.fold_in(key, 17))
    lengths_drawn = jax.random.randint(key_length, (ROWS,), DEC_LEN // 4, DEC_LEN + 1)
    return jnp.where(chosen_rows(key_force), DEC_LEN, lengths_drawn).astype(jnp.int32)


def plant(values, stream_key, smallest, top_value):
    extent = values.shape
    place = [jax.random.randint(jax.random.fold_in(stream_key, axis), (), 0, extent[axis]) for axis in range(len(extent))]
    values = values.at[tuple(place)].set(smallest)
    longest = extent.index(max(extent))
    place[longest] = (place[longest] + 1) % extent[longest]
    return values.at[tuple(place)].set(top_value)


def steps_of(key, dims, shards, least, largest):
    level = 1.0
    for dim, shards_of in shards:
        steps = jax.random.uniform(jax.random.fold_in(jax.random.fold_in(key, 6), dim), (shards_of,), jnp.float32, least / len(shards), largest / len(shards))
        level = level * jnp.repeat(jnp.exp(steps), dims[dim] // shards_of).reshape((-1,) + (1,) * (len(dims) - 1 - dim))
    return level


def gaussian(stream_key, dims, deviation, bound, pieces=(), held_as=jnp.bfloat16):
    values = deviation * jax.random.normal(stream_key, dims, jnp.float32)
    if pieces:
        values = values * steps_of(stream_key, dims, pieces, -0.22, 0.18)
    return jnp.clip(values, -bound, bound).astype(held_as)


def setup_inputs(seed: int = 0) -> dict:
    splits = jax.random.split(jax.random.key(seed), 32)
    return {
        "encoder_input": draw_encoder_input(jax.random.fold_in(splits[31], 71), 0),
        "decoder_input": draw_decoder_input(jax.random.fold_in(splits[31], 71), 0),
        "segment_lengths": draw_segment_lengths(jax.random.fold_in(splits[31], 71), 0),
        "target_lengths": draw_target_lengths(jax.random.fold_in(splits[31], 71), 0),
        "bucket_table": plant(jax.random.randint(splits[4], (2 * ENC_LEN - 1,), 0, BUCKETS), jax.random.fold_in(splits[4], 1), 0, BUCKETS - 1).astype(jnp.int32),
        "encoder_attention_gain": jnp.clip(1.0 + 0.1 * jax.random.normal(splits[5], (D,), jnp.float32), 0.5, 1.5).astype(jnp.bfloat16),
        "encoder_query": gaussian(splits[6], (D, D), (4 * D) ** -0.5, 0.109375, ((0, 32),)),
        "encoder_key": gaussian(splits[7], (D, D), (4 * D) ** -0.5, 0.109375, ((0, 32),)),
        "encoder_value": gaussian(splits[8], (D, D), D ** -0.5, 0.21875, ((0, 32),)),
        "encoder_outward": gaussian(splits[9], (D, D), (D // 16) ** -0.5, 0.875, ((0, 32),)),
        "encoder_position_bias": gaussian(splits[10], (BUCKETS, HEADS), 1.0, 4.0, (), jnp.float32),
        "encoder_feedforward_gain": jnp.clip(1.0 + 0.1 * jax.random.normal(splits[11], (D,), jnp.float32), 0.5, 1.5).astype(jnp.bfloat16),
        "encoder_widen": gaussian(splits[12], (D, FF), D ** -0.5, 0.21875, ((0, 32),)),
        "encoder_narrow": gaussian(splits[13], (FF, D), (FF // 2) ** -0.5, 0.15625, ((0, 32),)),
        "encoder_final_gain": jnp.clip(1.0 + 0.1 * jax.random.normal(splits[14], (D,), jnp.float32), 0.5, 1.5).astype(jnp.bfloat16),
        "decoder_self_gain": jnp.clip(1.0 + 0.1 * jax.random.normal(splits[15], (D,), jnp.float32), 0.5, 1.5).astype(jnp.bfloat16),
        "decoder_query": gaussian(splits[16], (D, D), (4 * D) ** -0.5, 0.109375, ((0, 32),)),
        "decoder_key": gaussian(splits[17], (D, D), (4 * D) ** -0.5, 0.109375, ((0, 32),)),
        "decoder_value": gaussian(splits[18], (D, D), D ** -0.5, 0.21875, ((0, 32),)),
        "decoder_outward": gaussian(splits[19], (D, D), (D // 16) ** -0.5, 0.875, ((0, 32),)),
        "decoder_position_bias": gaussian(splits[20], (BUCKETS, HEADS), 1.0, 4.0, (), jnp.float32),
        "decoder_cross_gain": jnp.clip(1.0 + 0.1 * jax.random.normal(splits[21], (D,), jnp.float32), 0.5, 1.5).astype(jnp.bfloat16),
        "cross_query": gaussian(splits[22], (D, D), (4 * D) ** -0.5, 0.109375, ((0, 32),)),
        "cross_key": gaussian(splits[23], (D, D), (4 * D) ** -0.5, 0.109375, ((0, 32),)),
        "cross_value": gaussian(splits[24], (D, D), D ** -0.5, 0.21875, ((0, 32),)),
        "cross_outward": gaussian(splits[25], (D, D), (D // 16) ** -0.5, 0.875, ((0, 32),)),
        "decoder_feedforward_gain": jnp.clip(1.0 + 0.1 * jax.random.normal(splits[26], (D,), jnp.float32), 0.5, 1.5).astype(jnp.bfloat16),
        "decoder_widen": gaussian(splits[27], (D, FF), D ** -0.5, 0.21875, ((0, 32),)),
        "decoder_narrow": gaussian(splits[28], (FF, D), (FF // 2) ** -0.5, 0.15625, ((0, 32),)),
        "encoder_cotangent": gaussian(splits[29], (ROWS, ENC_LEN, D), 1.0, 6.0, ((0, 16), (1, 2))),
        "decoder_cotangent": gaussian(splits[30], (ROWS, DEC_LEN, D), 1.0, 6.0, ((0, 16), (1, 2))),
    }


EPSILON = 1e-06
NEGATIVE = -1e+30
HIGHEST_PRECISION = lax.Precision.HIGHEST

@jax.custom_vjp
def low(v):
    return lax.optimization_barrier(v.astype(jnp.bfloat16)).astype(jnp.float32)

@jax.custom_vjp
def low_back(v):
    return v

def low_keep(v):
    return (low(v), None)

def low_pass(kept, grad):
    return (grad,)

def back_keep(v):
    return (v, None)

def back_low(kept, grad):
    return (low(grad),)
low.defvjp(low_keep, low_pass)
low_back.defvjp(back_keep, back_low)

def matmul(left, right):
    return jnp.dot(left, right, precision=HIGHEST_PRECISION)

def rms_scale(values, gain_vec):
    return values * lax.rsqrt(lax.optimization_barrier(jnp.mean(values * values, axis=-1, keepdims=True)) + EPSILON) * gain_vec

def gelu_float(values):
    return jax.nn.gelu(values, approximate=True)

def position_bias(table_in, buckets, query_pos, key_pos, span):
    distance_table = jnp.dot(jax.nn.one_hot(buckets, BUCKETS, dtype=jnp.float32), table_in, precision=HIGHEST_PRECISION)
    distance_index = key_pos[None, :] - query_pos[:, None] + (span - 1)
    return jnp.transpose(jnp.take(distance_table, distance_index, axis=0), (2, 0, 1))

def attend(query_source, key_source, weights, rel_bias, key_mask):
    query_weight, key_weight, value_weight, outward = weights
    query_count = query_source.shape[0]
    key_count = key_source.shape[0]
    queries = low(low_back(matmul(query_source, query_weight))).reshape(query_count, HEADS, HEAD)
    keys_all = low(low_back(matmul(key_source, key_weight))).reshape(key_count, HEADS, HEAD)
    values_all = low(low_back(matmul(key_source, value_weight))).reshape(key_count, HEADS, HEAD)
    scores = jnp.einsum('qhd,khd->hqk', queries, keys_all, precision=HIGHEST_PRECISION) + rel_bias
    scores = jnp.where(key_mask[None], low_back(scores), NEGATIVE)
    row_maximum = lax.optimization_barrier(jnp.max(scores, axis=-1, keepdims=True))
    exponent = jnp.exp(scores - row_maximum)
    softmax_probs = low(exponent / lax.optimization_barrier(jnp.sum(exponent, axis=-1, keepdims=True)))
    attended = jnp.einsum('hqk,khd->qhd', softmax_probs, values_all, precision=HIGHEST_PRECISION)
    attended = low(low_back(attended.reshape(query_count, HEADS * HEAD)))
    return low_back(matmul(attended, outward))

def layer_row(row_items, params, enc_bias, dec_bias):
    encoder_row, decoder_row, lengths_row, target_length = row_items
    encoder_attention_gain, encoder_query, encoder_key, encoder_value, encoder_outward, encoder_position_bias, encoder_feedforward_gain, encoder_widen, encoder_narrow, encoder_final_gain, decoder_self_gain, decoder_query, decoder_key, decoder_value, decoder_outward, decoder_position_bias, decoder_cross_gain, cross_query, cross_key, cross_value, cross_outward, decoder_feedforward_gain, decoder_widen, decoder_narrow = params
    enc_positions = jnp.arange(ENC_LEN, dtype=jnp.int32)
    dec_positions = jnp.arange(DEC_LEN, dtype=jnp.int32)
    segment_ends = jnp.cumsum(lengths_row)
    segment = lax.optimization_barrier(jnp.sum((segment_ends[None, :] <= enc_positions[:, None]).astype(jnp.int32), axis=1))
    enc_mask = segment[:, None] == segment[None, :]
    enc_valid = enc_positions < segment_ends[-1]
    dec_valid = dec_positions < target_length
    dec_mask = (dec_positions[None, :] <= dec_positions[:, None]) & (dec_valid[:, None] == dec_valid[None, :])
    cross_mask = jnp.logical_not(dec_valid)[:, None] | enc_valid[None, :]
    normed_one = low(rms_scale(encoder_row, encoder_attention_gain))
    middle = encoder_row + attend(normed_one, normed_one, (encoder_query, encoder_key, encoder_value, encoder_outward), enc_bias, enc_mask)
    normed_two = low(rms_scale(middle, encoder_feedforward_gain))
    encoder_pre = low_back(matmul(normed_two, encoder_widen))
    encoder_branch = low_back(matmul(low(gelu_float(encoder_pre)), encoder_narrow))
    encoder_out = middle + encoder_branch
    memory = low(rms_scale(encoder_out, encoder_final_gain))
    normed_three = low(rms_scale(decoder_row, decoder_self_gain))
    target_middle = decoder_row + attend(normed_three, normed_three, (decoder_query, decoder_key, decoder_value, decoder_outward), dec_bias, dec_mask)
    normed_four = low(rms_scale(target_middle, decoder_cross_gain))
    target_crossed = target_middle + attend(normed_four, memory, (cross_query, cross_key, cross_value, cross_outward), 0.0, cross_mask)
    normed_five = low(rms_scale(target_crossed, decoder_feedforward_gain))
    decoder_pre = low_back(matmul(normed_five, decoder_widen))
    decoder_branch = low_back(matmul(low(gelu_float(decoder_pre)), decoder_narrow))
    decoder_out = target_crossed + decoder_branch
    return ((encoder_out, decoder_out), (encoder_branch, decoder_branch))

def reference(encoder_input, decoder_input, segment_lengths, target_lengths, bucket_table, encoder_attention_gain, encoder_query, encoder_key, encoder_value, encoder_outward, encoder_position_bias, encoder_feedforward_gain, encoder_widen, encoder_narrow, encoder_final_gain, decoder_self_gain, decoder_query, decoder_key, decoder_value, decoder_outward, decoder_position_bias, decoder_cross_gain, cross_query, cross_key, cross_value, cross_outward, decoder_feedforward_gain, decoder_widen, decoder_narrow, encoder_cotangent, decoder_cotangent):
    enc_positions = jnp.arange(ENC_LEN, dtype=jnp.int32)
    dec_positions = jnp.arange(DEC_LEN, dtype=jnp.int32)
    params = tuple((param_item.astype(jnp.float32) for param_item in (encoder_attention_gain, encoder_query, encoder_key, encoder_value, encoder_outward, encoder_position_bias, encoder_feedforward_gain, encoder_widen, encoder_narrow, encoder_final_gain, decoder_self_gain, decoder_query, decoder_key, decoder_value, decoder_outward, decoder_position_bias, decoder_cross_gain, cross_query, cross_key, cross_value, cross_outward, decoder_feedforward_gain, decoder_widen, decoder_narrow)))

    def forward(encoder_values, decoder_values, param_values):
        enc_bias = position_bias(param_values[5], bucket_table, enc_positions, enc_positions, ENC_LEN)
        dec_bias = position_bias(param_values[15], bucket_table, dec_positions, dec_positions, ENC_LEN)

        def one_row(row_items):
            return layer_row(row_items, param_values, enc_bias, dec_bias)
        return lax.map(jax.checkpoint(one_row), (encoder_values, decoder_values, segment_lengths, target_lengths))
    outputs, pullback, extras = jax.vjp(forward, encoder_input.astype(jnp.float32), decoder_input.astype(jnp.float32), params, has_aux=True)
    encoder_grad, decoder_grad, param_grads = pullback((encoder_cotangent.astype(jnp.float32), decoder_cotangent.astype(jnp.float32)))
    encoder_out, decoder_out = outputs
    encoder_branch, decoder_branch = extras
    segment_ends = jnp.cumsum(segment_lengths, axis=1)
    enc_valid = (enc_positions[None, :] < segment_ends[:, -1:])[:, :, None]
    dec_valid = (dec_positions[None, :] < target_lengths[:, None])[:, :, None]
    enc_count = jnp.sum(enc_valid.astype(jnp.float32)) * D
    dec_count = jnp.sum(dec_valid.astype(jnp.float32)) * D
    statistics = jnp.sqrt(jnp.stack([jnp.sum(jnp.where(enc_valid, encoder_out * encoder_out, 0.0)) / enc_count, jnp.sum(jnp.where(enc_valid, encoder_branch * encoder_branch, 0.0)) / enc_count, jnp.sum(jnp.where(dec_valid, decoder_out * decoder_out, 0.0)) / dec_count, jnp.sum(jnp.where(dec_valid, decoder_branch * decoder_branch, 0.0)) / dec_count]))
    return (encoder_out, decoder_out, encoder_grad, decoder_grad, param_grads[0], param_grads[1], param_grads[2], param_grads[3], param_grads[4], param_grads[5], param_grads[6], param_grads[7], param_grads[8], param_grads[9], param_grads[10], param_grads[11], param_grads[12], param_grads[13], param_grads[14], param_grads[15], param_grads[16], param_grads[17], param_grads[18], param_grads[19], param_grads[20], param_grads[21], param_grads[22], param_grads[23], statistics)
```

```python
import functools

import jax
import jax.numpy as jnp
from jax import lax
from jax.experimental import pallas as pl
from jax.experimental.pallas import tpu as pltpu
from jax.sharding import PartitionSpec as P

HEADS = 12
BUCKETS = 32
EPSILON = 1e-06
NEGATIVE = -1e30
HIGHEST_PRECISION = lax.Precision.HIGHEST
BOTH = ("rows", "seq")
CHAIN = 4

SPAN=1024
CONTRACT_LAST=(((1,),(1,)),((),()))
CONTRACT_FIRST=(((0,),(0,)),((),()))

def dotf(a,b,dims):
    return lax.dot_general(a,b,dims,preferred_element_type=jnp.float32)

def allowed_of(mode,qcode,kcode,shape):
    if mode=="segment":
        return qcode==kcode
    if mode=="causal":
        qi=lax.broadcasted_iota(jnp.int32,shape,0); ki=lax.broadcasted_iota(jnp.int32,shape,1)
        return (ki<=qi)&(qcode==kcode)
    return (qcode==0)|(kcode==1)

def probs_of(q,k,table_ref,h,allowed,half):
    s=dotf(q,k,CONTRACT_LAST)
    if table_ref is not None:
        row=jnp.broadcast_to(table_ref[0,h:h+1,:],(s.shape[0],SPAN))
        s=s+pltpu.roll(row,SPAN-half,1,stride=1,stride_axis=0)[:,:s.shape[1]]
    s=jnp.where(allowed,s,NEGATIVE)
    e=jnp.exp(s-jnp.max(s,axis=-1,keepdims=True))
    return e*(1.0/jnp.sum(e,axis=-1,keepdims=True))

def fwd_kernel(mode,half,*refs):
    if mode=="cross":
        q_ref,k_ref,v_ref,qc,kc,o_ref=refs; t_ref=None
    else:
        q_ref,k_ref,v_ref,qc,kc,t_ref,o_ref=refs
    allowed=allowed_of(mode,qc[...],kc[...],(q_ref.shape[0],k_ref.shape[0]))
    for h in range(2):
        sl=slice(64*h,64*h+64)
        p=probs_of(q_ref[:,sl],k_ref[:,sl],t_ref,h,allowed,half)
        o_ref[:,sl]=jnp.dot(p.astype(jnp.bfloat16),v_ref[:,sl],preferred_element_type=jnp.float32).astype(jnp.bfloat16)

def bwd_kernel(mode,half,*refs):
    if mode=="cross":
        q_ref,k_ref,v_ref,g_ref,qc,kc,dq_ref,dk_ref,dv_ref=refs; t_ref=None
    else:
        q_ref,k_ref,v_ref,g_ref,qc,kc,t_ref,dq_ref,dk_ref,dv_ref,dt_ref=refs
    allowed=allowed_of(mode,qc[...],kc[...],(q_ref.shape[0],k_ref.shape[0]))
    for h in range(2):
        sl=slice(64*h,64*h+64)
        q=q_ref[:,sl];k=k_ref[:,sl];v=v_ref[:,sl];g=g_ref[:,sl]
        p=probs_of(q,k,t_ref,h,allowed,half)
        dv_ref[:,sl]=dotf(p.astype(jnp.bfloat16),g,CONTRACT_FIRST).astype(jnp.bfloat16)
        dp=dotf(g,v,CONTRACT_LAST)
        ds=p*(dp-jnp.sum(dp*p,axis=-1,keepdims=True))
        dsb=ds.astype(jnp.bfloat16)
        dq_ref[:,sl]=jnp.dot(dsb,k,preferred_element_type=jnp.float32).astype(jnp.bfloat16)
        dk_ref[:,sl]=dotf(dsb,q,CONTRACT_FIRST).astype(jnp.bfloat16)
        if t_ref is not None:
            sq=ds.shape[0]
            flip=(lax.broadcasted_iota(jnp.int32,(sq,sq),0)+lax.broadcasted_iota(jnp.int32,(sq,sq),1)==sq-1).astype(jnp.bfloat16)
            flipped=jnp.dot(flip,dsb,preferred_element_type=jnp.float32)
            wide=jnp.concatenate([flipped,jnp.zeros((sq,SPAN-ds.shape[1]),jnp.float32)],axis=1)
            rolled=pltpu.roll(wide,half-(sq-1),1,stride=1,stride_axis=0)
            dt_ref[0,h:h+1,:]=jnp.sum(rolled,axis=0,keepdims=True)

def attn(kernel,mode,half,outs,q,k,v,extra,qc,kc,table):
    sq,width=q.shape; sk=k.shape[0]
    qs=pl.BlockSpec((sq,128),lambda i:(0,i)); ks=pl.BlockSpec((sk,128),lambda i:(0,i))
    ts=pl.BlockSpec((1,2,SPAN),lambda i:(i,0,0))
    ins=[q,k,v]+extra+[qc,kc]; specs=[qs,ks,ks]+[qs]*len(extra)+[pl.BlockSpec((sq,1),lambda i:(0,0)),pl.BlockSpec((1,sk),lambda i:(0,0))]
    if table is not None: ins.append(table); specs.append(ts)
    shapes={"q":(jax.ShapeDtypeStruct((sq,width),jnp.bfloat16),qs),"k":(jax.ShapeDtypeStruct((sk,width),jnp.bfloat16),ks),"t":(jax.ShapeDtypeStruct((width//128,2,SPAN),jnp.float32),ts)}
    return pl.pallas_call(functools.partial(kernel,mode,half),grid=(width//128,),in_specs=specs,
        out_shape=[shapes[o][0] for o in outs],out_specs=[shapes[o][1] for o in outs],
        compiler_params=pltpu.CompilerParams(vmem_limit_bytes=48*2**20))(*ins)

def attn_fwd(mode,half,q,k,v,qc,kc,table):
    return attn(fwd_kernel,mode,half,"q",q,k,v,[],qc,kc,table)[0]
def attn_bwd(mode,half,q,k,v,g,qc,kc,table):
    return attn(bwd_kernel,mode,half,"qkk"+("t" if table is not None else ""),q,k,v,[g],qc,kc,table)


def flat_index(z, x, core, y):
    return ((z * 2 + x) * 2 + core) * 2 + y


def every_device():
    return [(z, x, c, y) for z in range(CHAIN) for x in range(2) for c in range(2) for y in range(2)]


def swap(value, axis):
    pairs = []
    for place in every_device():
        other = list(place)
        other["zxcy".index(axis)] ^= 1
        pairs.append((flat_index(*place), flat_index(*other)))
    return lax.ppermute(value, BOTH, pairs)


def shift(value, step, reach):
    pairs = []
    for z, x, c, y in every_device():
        if 0 <= z + step < CHAIN and 0 <= z + reach < CHAIN:
            pairs.append((flat_index(z, x, c, y), flat_index(z + step, x, c, y)))
    return lax.ppermute(value, BOTH, pairs)


def hop(value, bit):
    size = 4 * CHAIN * 2
    return lax.ppermute(value, BOTH, [(i, i ^ bit) for i in range(size)])


def place_of():
    row = lax.axis_index("rows")
    return {"z": row // 4, "x": (row // 2) % 2, "c": row % 2, "y": lax.axis_index("seq")}


def assemble_kernel(count, shifts, *refs):
    pieces = refs[:8]
    outs = refs[8 : 8 + count]
    sem = refs[8 + count]
    row = lax.axis_index("rows")
    here = {"x": (row // 2) % 2, "c": row % 2, "y": lax.axis_index("seq")}
    copies = []
    for number, piece in enumerate(pieces):
        moved = shifts[number]
        slot = {a: here[a] + (1 - 2 * here[a]) * (1 if a in moved else 0) for a in "xcy"}
        index = slot["x"] * 4 + slot["c"] * 2 + slot["y"]
        for item in range(count):
            copy = pltpu.make_async_copy(
                piece.at[item], outs[item].at[:, index], sem.at[number, item]
            )
            copy.start()
            copies.append(copy)
    for copy in copies:
        copy.wait()


def assemble(pieces, shifts):
    count, chain, height, width = pieces[0].shape
    outs = pl.pallas_call(
        functools.partial(assemble_kernel, count, shifts),
        out_shape=[jax.ShapeDtypeStruct((chain, 8, height, width), pieces[0].dtype)] * count,
        in_specs=[pl.BlockSpec(memory_space=pl.ANY)] * 8,
        out_specs=[pl.BlockSpec(memory_space=pl.ANY)] * count,
        scratch_shapes=[pltpu.SemaphoreType.DMA((8, count))],
        cost_estimate=pl.CostEstimate(
            flops=0, bytes_accessed=2 * 8 * pieces[0].size * 2, transcendentals=0
        ),
    )(*pieces)
    return [out.reshape(chain * 8 * height, width) for out in outs]


def gather_group(shards, order):
    own = jnp.stack(shards)
    place = place_of()
    up, down = own, own
    ups, downs = {}, {}
    for step in range(1, CHAIN):
        up = shift(up, 1, 1 - step)
        down = shift(down, -1, step - 1)
        ups[step], downs[step] = up, down
    blocks = []
    for k in range(CHAIN):
        block = own
        for step in range(1, CHAIN):
            if k + step < CHAIN:
                block = jnp.where(place["z"] == k + step, ups[step], block)
            if k - step >= 0:
                block = jnp.where(place["z"] == k - step, downs[step], block)
        blocks.append(block)
    pieces = {"": jnp.stack(blocks, axis=1)}
    for axis in order:
        for name in list(pieces):
            pieces[name + axis] = swap(pieces[name], axis)
    names = list(pieces)
    return assemble([pieces[name] for name in names], names)


def reduce_group(grads, order):
    place = place_of()
    axes = ["z", "x", "c", "y"]
    parts = [
        grad.reshape(CHAIN, 2, 2, 2, grad.shape[0] // (8 * CHAIN), grad.shape[1]) for grad in grads
    ]
    held = None
    for axis in reversed(order):
        at = axes.index(axis)
        axes.remove(axis)
        mine = place[axis]
        if held is None:
            pick = lambda where: jnp.stack(
                [lax.dynamic_index_in_dim(part, where, at, keepdims=False) for part in parts]
            )
        else:
            pick = lambda where: lax.dynamic_index_in_dim(held, where, at + 1, keepdims=False)
        sent = swap(pick(1 - mine), axis)
        held = (pick(mine).astype(jnp.float32) + sent.astype(jnp.float32)).astype(jnp.bfloat16)
    pick = lambda where: lax.dynamic_index_in_dim(
        held, jnp.clip(where, 0, CHAIN - 1), 1, keepdims=False
    ).astype(jnp.float32)
    total = pick(place["z"])
    for sign in (1, -1):
        moving = None
        for step in range(CHAIN - 1, 0, -1):
            term = pick(place["z"] + sign * step)
            if moving is not None:
                term = term + moving.astype(jnp.float32)
            moving = shift(term.astype(jnp.bfloat16), sign, sign * step)
        total = total + moving.astype(jnp.float32)
    return [total[i] for i in range(len(grads))]


def sum_everywhere(value):
    for bit in (1, 2, 4, 8, 16):
        value = value + hop(value, bit)
    return value


def whole_row(halves):
    mine = lax.axis_index("seq")
    keep = lax.dynamic_index_in_dim(halves, mine, 0, keepdims=False)
    other = lax.ppermute(
        lax.dynamic_index_in_dim(halves, 1 - mine, 0, keepdims=False), "seq", [(0, 1), (1, 0)]
    )
    first = jnp.where(mine == 0, keep, other)
    second = jnp.where(mine == 0, other, keep)
    return jnp.concatenate([first, second], axis=0)


def own_slots(row):
    mine = lax.axis_index("seq")
    half = row.shape[0] // 2
    keep = lax.dynamic_slice_in_dim(row, mine * half, half, 0)
    sent = lax.dynamic_slice_in_dim(row, (1 - mine) * half, half, 0).astype(jnp.bfloat16)
    other = lax.ppermute(sent, "seq", [(0, 1), (1, 0)]).astype(row.dtype)
    return jnp.stack([jnp.where(mine == 0, keep, other), jnp.where(mine == 0, other, keep)])


def matmul(left, right):
    return jnp.dot(left, right, preferred_element_type=jnp.float32)


def matmul_back(grads, weight):
    return dotf(grads, weight, CONTRACT_LAST)


def weight_grad(inputs, grads):
    return dotf(inputs, grads, CONTRACT_FIRST).astype(jnp.bfloat16)


def rms_scale(values, gain_vec):
    return (
        values * lax.rsqrt(jnp.mean(values * values, axis=-1, keepdims=True) + EPSILON) * gain_vec
    )


def gelu_float(values):
    return jax.nn.gelu(values, approximate=True)


def norm_back(values, gain_vec, upstream):
    unused_value, pullback = jax.vjp(rms_scale, values, gain_vec)
    return pullback(upstream)


def low(values):
    return values.astype(jnp.bfloat16)


def feedforward_back(normed, pre_values, active, widen, narrow, upstream):
    branch_low = low(upstream)
    narrow_grad = weight_grad(active, branch_low)
    active_grad = matmul_back(branch_low, narrow)
    unused_value, gelu_pull = jax.vjp(gelu_float, pre_values)
    pre_low = low(gelu_pull(active_grad)[0])
    return (matmul_back(pre_low, widen), weight_grad(normed, pre_low), narrow_grad)


def distance_table(table_in, buckets):
    ids = jnp.arange(BUCKETS, dtype=jnp.int32)
    selector = (buckets[:, None] == ids[None, :]).astype(jnp.float32)
    by_distance = jnp.einsum("db,bh->hd", selector, table_in, precision=HIGHEST_PRECISION)
    padded = jnp.pad(by_distance, ((0, 0), (0, SPAN - by_distance.shape[1])))
    return padded.reshape(HEADS // 2, 2, SPAN), selector


def table_grad(selector, by_distance):
    flat = by_distance.reshape(HEADS, SPAN)[:, : selector.shape[0]]
    return jnp.einsum("db,hd->bh", selector, flat, precision=HIGHEST_PRECISION)


def layers(encoder_row, decoder_row, lengths_row, target_length, buckets, gains, weights, encoder_cotangent, decoder_cotangent, encoder_table_in, decoder_table_in):
    encoder_length, feature_count = encoder_row.shape
    decoder_length = decoder_row.shape[0]
    half = encoder_length - 1
    positions = jnp.arange(encoder_length, dtype=jnp.int32)
    target_positions = jnp.arange(decoder_length, dtype=jnp.int32)
    count = lengths_row.shape[0]
    order = jnp.arange(count, dtype=jnp.int32)
    ends = jnp.sum(jnp.where(order[None, :] <= order[:, None], lengths_row[None, :], 0), axis=1)
    segment = jnp.sum((ends[None, :] <= positions[:, None]).astype(jnp.int32), axis=1)
    valid = positions < jnp.sum(lengths_row)
    target_valid = target_positions < target_length
    column = lambda code: code.astype(jnp.int32)[:, None]
    line = lambda code: code.astype(jnp.int32)[None, :]
    encoder_codes = (column(segment), line(segment))
    self_codes = (column(target_valid), line(target_valid))
    cross_codes = (column(target_valid), line(valid))
    encoder_table, selector = distance_table(encoder_table_in, buckets)
    decoder_table, unused_selector = distance_table(decoder_table_in, buckets)
    (
        first_gain,
        second_gain,
        final_gain,
        self_gain,
        cross_gain,
        third_gain,
    ) = [gains[i] for i in range(6)]
    w = weights

    residual = encoder_row.astype(jnp.float32)
    first_normed = low(rms_scale(residual, first_gain))
    queries = low(matmul(first_normed, w["eq"]))
    keys = low(matmul(first_normed, w["ek"]))
    values = low(matmul(first_normed, w["ev"]))
    attended = attn_fwd("segment", half, queries, keys, values, *encoder_codes, encoder_table)
    middle = residual + matmul(attended, w["eo"])
    second_normed = low(rms_scale(middle, second_gain))
    pre = matmul(second_normed, w["ew"])
    active = low(gelu_float(pre))
    branch = matmul(active, w["en"])
    output = middle + branch
    memory = low(rms_scale(output, final_gain))

    target = decoder_row.astype(jnp.float32)
    self_normed = low(rms_scale(target, self_gain))
    self_queries = low(matmul(self_normed, w["dq"]))
    self_keys = low(matmul(self_normed, w["dk"]))
    self_values = low(matmul(self_normed, w["dv"]))
    self_attended = attn_fwd(
        "causal", half, self_queries, self_keys, self_values, *self_codes, decoder_table
    )
    target_middle = target + matmul(self_attended, w["do"])
    cross_normed = low(rms_scale(target_middle, cross_gain))
    cross_queries = low(matmul(cross_normed, w["cq"]))
    cross_keys = low(matmul(memory, w["ck"]))
    cross_values = low(matmul(memory, w["cv"]))
    cross_attended = attn_fwd(
        "cross", half, cross_queries, cross_keys, cross_values, *cross_codes, None
    )
    crossed = target_middle + matmul(cross_attended, w["co"])
    third_normed = low(rms_scale(crossed, third_gain))
    decoder_pre = matmul(third_normed, w["dw"])
    decoder_active = low(gelu_float(decoder_pre))
    decoder_branch = matmul(decoder_active, w["dn"])
    decoder_output = crossed + decoder_branch

    grads = {}
    upstream = decoder_cotangent.astype(jnp.float32)
    normed_grad, grads["dw"], grads["dn"] = feedforward_back(
        third_normed, decoder_pre, decoder_active, w["dw"], w["dn"], upstream
    )
    part, third_gain_grad = norm_back(crossed, third_gain, normed_grad)
    crossed_grad = upstream + part

    crossed_low = low(crossed_grad)
    grads["co"] = weight_grad(cross_attended, crossed_low)
    mixed_grad = low(matmul_back(crossed_low, w["co"]))
    query_low, key_low, value_low = attn_bwd(
        "cross", half, cross_queries, cross_keys, cross_values, mixed_grad, *cross_codes, None
    )
    grads["cq"] = weight_grad(cross_normed, query_low)
    grads["ck"] = weight_grad(memory, key_low)
    grads["cv"] = weight_grad(memory, value_low)
    memory_grad = matmul_back(key_low, w["ck"]) + matmul_back(value_low, w["cv"])
    part, cross_gain_grad = norm_back(target_middle, cross_gain, matmul_back(query_low, w["cq"]))
    middle_grad = crossed_grad + part

    middle_low = low(middle_grad)
    grads["do"] = weight_grad(self_attended, middle_low)
    mixed_grad = low(matmul_back(middle_low, w["do"]))
    query_low, key_low, value_low, decoder_distance = attn_bwd(
        "causal", half, self_queries, self_keys, self_values, mixed_grad, *self_codes, decoder_table
    )
    grads["dq"] = weight_grad(self_normed, query_low)
    grads["dk"] = weight_grad(self_normed, key_low)
    grads["dv"] = weight_grad(self_normed, value_low)
    normed_grad = (
        matmul_back(query_low, w["dq"])
        + matmul_back(key_low, w["dk"])
        + matmul_back(value_low, w["dv"])
    )
    part, self_gain_grad = norm_back(target, self_gain, normed_grad)
    decoder_input_grad = middle_grad + part

    part, final_gain_grad = norm_back(output, final_gain, memory_grad)
    output_grad = encoder_cotangent.astype(jnp.float32) + part
    normed_grad, grads["ew"], grads["en"] = feedforward_back(
        second_normed, pre, active, w["ew"], w["en"], output_grad
    )
    part, second_gain_grad = norm_back(middle, second_gain, normed_grad)
    encoder_middle_grad = output_grad + part

    middle_low = low(encoder_middle_grad)
    grads["eo"] = weight_grad(attended, middle_low)
    mixed_grad = low(matmul_back(middle_low, w["eo"]))
    query_low, key_low, value_low, encoder_distance = attn_bwd(
        "segment", half, queries, keys, values, mixed_grad, *encoder_codes, encoder_table
    )
    grads["eq"] = weight_grad(first_normed, query_low)
    grads["ek"] = weight_grad(first_normed, key_low)
    grads["ev"] = weight_grad(first_normed, value_low)
    normed_grad = (
        matmul_back(query_low, w["eq"])
        + matmul_back(key_low, w["ek"])
        + matmul_back(value_low, w["ev"])
    )
    part, first_gain_grad = norm_back(residual, first_gain, normed_grad)
    encoder_input_grad = encoder_middle_grad + part

    keep = valid[:, None]
    target_keep = target_valid[:, None]
    sums = jnp.stack(
        [
            jnp.sum(jnp.where(keep, output * output, 0.0)),
            jnp.sum(jnp.where(keep, branch * branch, 0.0)),
            jnp.sum(jnp.where(target_keep, decoder_output * decoder_output, 0.0)),
            jnp.sum(jnp.where(target_keep, decoder_branch * decoder_branch, 0.0)),
            jnp.sum(valid.astype(jnp.float32)),
            jnp.sum(target_valid.astype(jnp.float32)),
        ]
    )
    small = jnp.concatenate(
        [
            first_gain_grad,
            second_gain_grad,
            final_gain_grad,
            self_gain_grad,
            cross_gain_grad,
            third_gain_grad,
            table_grad(selector, encoder_distance).reshape(-1),
            table_grad(selector, decoder_distance).reshape(-1),
            sums,
        ]
    )
    return (output, decoder_output, encoder_input_grad, decoder_input_grad, grads, small)


GROUPS = (
    (("eq", "ek"), "xyc"),
    (("ev", "eo"), "yxc"),
    (("ew",), "xyc"),
    (("en",), "yxc"),
    (("dq", "dk", "dv", "do"), "xyc"),
    (("cq", "ck", "cv", "co"), "yxc"),
    (("dw",), "xyc"),
    (("dn",), "yxc"),
)
WEIGHT_ARGS = {
    "eq": 6, "ek": 7, "ev": 8, "eo": 9, "ew": 12, "en": 13, "dq": 16, "dk": 17, "dv": 18, "do": 19,
    "cq": 22, "ck": 23, "cv": 24, "co": 25, "dw": 27, "dn": 28,
}
GAIN_ARGS = (5, 11, 14, 15, 21, 26)
WEIGHT_OUTS = {
    "eq": 5, "ek": 6, "ev": 7, "eo": 8, "ew": 11, "en": 12, "dq": 15, "dk": 16, "dv": 17, "do": 18,
    "cq": 21, "ck": 22, "cv": 23, "co": 24, "dw": 26, "dn": 27,
}
GAIN_OUTS = (4, 10, 13, 14, 20, 25)


def body(near, *args):
    row_count = lax.axis_size("rows") * lax.axis_size("seq")
    me = lax.axis_index("rows") * lax.axis_size("seq") + lax.axis_index("seq")
    seq_index = lax.axis_index("seq")
    shards = {name: args[i] for name, i in WEIGHT_ARGS.items()}
    own_gains = jnp.stack([args[i] for i in GAIN_ARGS])
    weights = {}
    if near:
        spread = jnp.zeros((6, row_count * own_gains.shape[1]), jnp.bfloat16)
        spread = lax.dynamic_update_slice_in_dim(spread, own_gains, me * own_gains.shape[1], 1)
        gains = sum_everywhere(spread)
        for names, order in GROUPS:
            weights.update(zip(names, gather_group([shards[n] for n in names], order)))
    else:
        gains = lax.all_gather(own_gains, BOTH, axis=1, tiled=True)
        for name, shard in shards.items():
            weights[name] = lax.all_gather(shard, BOTH, axis=0, tiled=True)
    encoder_row = whole_row(args[0])
    decoder_row = whole_row(args[1])
    lengths_row = lax.dynamic_index_in_dim(args[2], seq_index, 0, keepdims=False)
    target_length = lax.dynamic_index_in_dim(args[3], seq_index, 0, keepdims=False)
    output, decoder_output, encoder_input_grad, decoder_input_grad, grads, small = layers(
        encoder_row,
        decoder_row,
        lengths_row,
        target_length,
        args[4],
        gains.astype(jnp.float32),
        weights,
        whole_row(args[29]),
        whole_row(args[30]),
        args[10],
        args[20],
    )
    outs = [None] * 29
    for i, value in enumerate((output, decoder_output, encoder_input_grad, decoder_input_grad)):
        outs[i] = own_slots(value)
    reduced = {}
    if near:
        for names, order in reversed(GROUPS):
            reduced.update(zip(names, reduce_group([grads[n] for n in names], order)))
        small = sum_everywhere(small)
    else:
        for name, grad in grads.items():
            reduced[name] = lax.psum_scatter(
                grad.astype(jnp.float32), BOTH, scatter_dimension=0, tiled=True
            )
        small = lax.psum(small, BOTH)
    for name, i in WEIGHT_OUTS.items():
        outs[i] = reduced[name]
    feature_count = args[0].shape[2]
    share = feature_count // row_count
    for number, i in enumerate(GAIN_OUTS):
        outs[i] = lax.dynamic_slice_in_dim(small, number * feature_count + me * share, share)
    offset = 6 * feature_count
    size = BUCKETS * HEADS
    outs[9] = small[offset : offset + size].reshape(BUCKETS, HEADS)
    outs[19] = small[offset + size : offset + 2 * size].reshape(BUCKETS, HEADS)
    sums = small[offset + 2 * size :]
    divisors = jnp.stack([sums[4], sums[4], sums[5], sums[5]]) * feature_count
    outs[28] = jnp.sqrt(sums[:4] / divisors)
    return tuple(outs)


def solution(mesh):
    row_spec = P("rows", "seq", None)
    matrix = P(BOTH, None)
    vector = P(BOTH)
    in_specs = [row_spec, row_spec, P("rows", None), P("rows"), P()] + [None] * 26
    in_specs[10] = in_specs[20] = P()
    in_specs[29] = in_specs[30] = row_spec
    for i in GAIN_ARGS:
        in_specs[i] = vector
    for i in WEIGHT_ARGS.values():
        in_specs[i] = matrix
    out_specs = [row_spec] * 4 + [None] * 25
    out_specs[9] = out_specs[19] = out_specs[28] = P()
    for i in GAIN_OUTS:
        out_specs[i] = vector
    for i in WEIGHT_OUTS.values():
        out_specs[i] = matrix
    near = mesh.shape["rows"] == 4 * CHAIN and mesh.shape["seq"] == 2
    return jax.shard_map(
        functools.partial(body, near),
        mesh=mesh,
        in_specs=tuple(in_specs),
        out_specs=tuple(out_specs),
        check_vma=False,
    )
```

```python
import functools

import jax
import jax.numpy as jnp
from jax import lax
from jax.experimental import pallas as pl
from jax.experimental.pallas import tpu as pltpu
from jax.sharding import PartitionSpec as P

HEADS = 12
BUCKETS = 32
EPSILON = 1e-06
NEGATIVE = -1e30
HIGHEST_PRECISION = lax.Precision.HIGHEST
BOTH = ("rows", "seq")
CHAIN = 4

SPAN=1024
CONTRACT_LAST=(((1,),(1,)),((),()))
CONTRACT_FIRST=(((0,),(0,)),((),()))

def dotf(a,b,dims):
    return lax.dot_general(a,b,dims,preferred_element_type=jnp.float32)

def allowed_of(mode,qcode,kcode,shape):
    if mode=="segment":
        return qcode==kcode
    if mode=="causal":
        qi=lax.broadcasted_iota(jnp.int32,shape,0); ki=lax.broadcasted_iota(jnp.int32,shape,1)
        return (ki<=qi)&(qcode==kcode)
    return (qcode==0)|(kcode==1)

def probs_of(q,k,table_ref,h,allowed,half):
    s=dotf(q,k,CONTRACT_LAST)
    if table_ref is not None:
        row=jnp.broadcast_to(table_ref[0,h:h+1,:],(s.shape[0],SPAN))
        s=s+pltpu.roll(row,SPAN-half,1,stride=1,stride_axis=0)[:,:s.shape[1]]
    s=jnp.where(allowed,s,NEGATIVE)
    e=jnp.exp(s-jnp.max(s,axis=-1,keepdims=True))
    return e*(1.0/jnp.sum(e,axis=-1,keepdims=True))

def fwd_kernel(mode,half,*refs):
    if mode=="cross":
        q_ref,k_ref,v_ref,qc,kc,o_ref=refs; t_ref=None
    else:
        q_ref,k_ref,v_ref,qc,kc,t_ref,o_ref=refs
    allowed=allowed_of(mode,qc[...],kc[...],(q_ref.shape[0],k_ref.shape[0]))
    for h in range(2):
        sl=slice(64*h,64*h+64)
        p=probs_of(q_ref[:,sl],k_ref[:,sl],t_ref,h,allowed,half)
        o_ref[:,sl]=jnp.dot(p.astype(jnp.bfloat16),v_ref[:,sl],preferred_element_type=jnp.float32).astype(jnp.bfloat16)

def bwd_kernel(mode,half,*refs):
    if mode=="cross":
        q_ref,k_ref,v_ref,g_ref,qc,kc,dq_ref,dk_ref,dv_ref=refs; t_ref=None
    else:
        q_ref,k_ref,v_ref,g_ref,qc,kc,t_ref,dq_ref,dk_ref,dv_ref,dt_ref=refs
    allowed=allowed_of(mode,qc[...],kc[...],(q_ref.shape[0],k_ref.shape[0]))
    for h in range(2):
        sl=slice(64*h,64*h+64)
        q=q_ref[:,sl];k=k_ref[:,sl];v=v_ref[:,sl];g=g_ref[:,sl]
        p=probs_of(q,k,t_ref,h,allowed,half)
        dv_ref[:,sl]=dotf(p.astype(jnp.bfloat16),g,CONTRACT_FIRST).astype(jnp.bfloat16)
        dp=dotf(g,v,CONTRACT_LAST)
        ds=p*(dp-jnp.sum(dp*p,axis=-1,keepdims=True))
        dsb=ds.astype(jnp.bfloat16)
        dq_ref[:,sl]=jnp.dot(dsb,k,preferred_element_type=jnp.float32).astype(jnp.bfloat16)
        dk_ref[:,sl]=dotf(dsb,q,CONTRACT_FIRST).astype(jnp.bfloat16)
        if t_ref is not None:
            sq=ds.shape[0]
            flip=(lax.broadcasted_iota(jnp.int32,(sq,sq),0)+lax.broadcasted_iota(jnp.int32,(sq,sq),1)==sq-1).astype(jnp.bfloat16)
            flipped=jnp.dot(flip,dsb,preferred_element_type=jnp.float32)
            wide=jnp.concatenate([flipped,jnp.zeros((sq,SPAN-ds.shape[1]),jnp.float32)],axis=1)
            rolled=pltpu.roll(wide,half-(sq-1),1,stride=1,stride_axis=0)
            dt_ref[0,h:h+1,:]=jnp.sum(rolled,axis=0,keepdims=True)

def attn(kernel,mode,half,outs,q,k,v,extra,qc,kc,table):
    sq,width=q.shape; sk=k.shape[0]
    qs=pl.BlockSpec((sq,128),lambda i:(0,i)); ks=pl.BlockSpec((sk,128),lambda i:(0,i))
    ts=pl.BlockSpec((1,2,SPAN),lambda i:(i,0,0))
    ins=[q,k,v]+extra+[qc,kc]; specs=[qs,ks,ks]+[qs]*len(extra)+[pl.BlockSpec((sq,1),lambda i:(0,0)),pl.BlockSpec((1,sk),lambda i:(0,0))]
    if table is not None: ins.append(table); specs.append(ts)
    shapes={"q":(jax.ShapeDtypeStruct((sq,width),jnp.bfloat16),qs),"k":(jax.ShapeDtypeStruct((sk,width),jnp.bfloat16),ks),"t":(jax.ShapeDtypeStruct((width//128,2,SPAN),jnp.float32),ts)}
    return pl.pallas_call(functools.partial(kernel,mode,half),grid=(width//128,),in_specs=specs,
        out_shape=[shapes[o][0] for o in outs],out_specs=[shapes[o][1] for o in outs],
        compiler_params=pltpu.CompilerParams(vmem_limit_bytes=48*2**20))(*ins)

def attn_fwd(mode,half,q,k,v,qc,kc,table):
    return attn(fwd_kernel,mode,half,"q",q,k,v,[],qc,kc,table)[0]
def attn_bwd(mode,half,q,k,v,g,qc,kc,table):
    return attn(bwd_kernel,mode,half,"qkk"+("t" if table is not None else ""),q,k,v,[g],qc,kc,table)


class Place:
    def __init__(self):
        row = lax.axis_index("rows")
        self.z, self.x, self.c, self.y = row // 4, (row // 2) % 2, row % 2, lax.axis_index("seq")

    def device(self, axis):
        z, x, c, y = self.z, self.x, self.c, self.y
        if axis == "up":
            z = z + 1
        if axis == "down":
            z = z - 1
        if axis == "x":
            x = 1 - x
        if axis == "c":
            c = 1 - c
        if axis == "y":
            y = 1 - y
        return {"rows": z * 4 + x * 2 + c, "seq": y}


def greet(place):
    barrier = pltpu.get_barrier_semaphore()

    def signal(axis):
        pl.semaphore_signal(
            barrier, inc=1, device_id=place.device(axis), device_id_type=pl.DeviceIdType.MESH
        )

    for axis in "xcy":
        signal(axis)
    pl.when(place.z < CHAIN - 1)(lambda: signal("up"))
    pl.when(place.z > 0)(lambda: signal("down"))
    ends = (place.z == 0) | (place.z == CHAIN - 1)
    pl.when(ends)(lambda: pl.semaphore_wait(barrier, 4))
    pl.when(jnp.logical_not(ends))(lambda: pl.semaphore_wait(barrier, 5))


def third_of(width, third):
    if third is None:
        return slice(None)
    return slice(width // 3 * third, width // 3 * (third + 1))


class GatherStream:
    def __init__(self, place, own, out, third, kind, u, v, send, recv):
        self.place, self.own, self.out, self.third = place, own, out, third
        self.kind, self.u, self.v, self.send, self.recv = kind, u, v, send, recv
        self.cols = third_of(own.shape[-1], third)

    def block(self, z, pair):
        p = self.place
        x = slice(None) if pair and self.u == "x" else p.x
        y = slice(None) if pair and self.u == "y" else p.y
        return self.out.at[:, z, x, p.c, y, :, self.cols]

    def other(self, z, axis, pair):
        p = self.place
        x, y = p.x, p.y
        if pair and self.u == "x":
            x = slice(None)
        elif axis == "x":
            x = 1 - x
        if pair and self.u == "y":
            y = slice(None)
        elif axis == "y":
            y = 1 - y
        return self.out.at[:, z, x, p.c, y, :, self.cols]

    def copy(self, slot, src, dst, axis):
        return pltpu.make_async_remote_copy(
            src_ref=src,
            dst_ref=dst,
            send_sem=self.send.at[slot],
            recv_sem=self.recv.at[slot],
            device_id=self.place.device(axis),
            device_id_type=pl.DeviceIdType.MESH,
        )

    def first(self, z):
        return self.own.at[:, :, self.cols]

    def chain_copy(self, up, step):
        pair = self.kind == "B"
        z = self.place.z - (step - 1) if up else self.place.z + (step - 1)
        src = self.first(z) if step == 1 and not pair else self.block(z, pair)
        return self.copy(step - 1 if up else step + 2, src, self.block(z, pair), "up" if up else "down")

    def chain_arrival(self, up, step):
        pair = self.kind == "B"
        z = self.place.z - step if up else self.place.z + step
        ref = self.block(z, pair)
        return self.copy(step - 1 if up else step + 2, ref, ref, "up" if up else "down")

    def sends_at(self, up, step):
        z = self.place.z
        if up:
            return (z < CHAIN - 1) & (z >= step - 1)
        return (z > 0) & (z <= CHAIN - step)

    def arrives_at(self, up, step):
        z = self.place.z
        return z >= step if up else z <= CHAIN - 1 - step

    def side_copy(self, slot, z, axis, pair, fresh):
        src = self.first(z) if fresh else self.block(z, pair)
        return self.copy(slot, src, self.block(z, pair), axis)

    def side_arrival(self, slot, z, axis, pair):
        ref = self.other(z, axis, pair)
        return self.copy(slot, ref, ref, axis)

    def z_of(self, number):
        if number == 0:
            return self.place.z
        return self.place.z - number if number <= CHAIN - 1 else self.place.z + (number - CHAIN + 1)

    def u_copy(self, number):
        return self.side_copy(6 + number, self.z_of(number), self.u, False, number == 0)

    def u_arrival(self, number):
        return self.side_arrival(6 + number, self.z_of(number), self.u, False)

    def v_copy(self, number):
        return self.side_copy(13 + number, self.z_of(number), self.v, True, False)

    def v_arrival(self, number):
        return self.side_arrival(13 + number, self.z_of(number), self.v, True)


SLOTS = 20


def each_arrival(stream, step, act):
    for up in (True, False):
        number = step if up else step + CHAIN - 1
        pl.when(stream.arrives_at(up, step))(functools.partial(act, up, number))


def gather_kernel(plans, count, *refs):
    owns = refs[:count]
    outs = refs[count : 2 * count]
    send, recv, core_send, core_recv, local = refs[2 * count :]
    place = Place()
    streams = [
        GatherStream(place, owns[a], outs[a], third, kind, u, v, send.at[i], recv.at[i])
        for i, (a, third, kind, u, v) in enumerate(plans)
    ]
    kept = []
    for a in range(count):
        copy = pltpu.make_async_copy(
            owns[a], outs[a].at[:, place.z, place.x, place.c, place.y], local.at[a]
        )
        copy.start()
        kept.append(copy)
    greet(place)

    def when(cond, act):
        pl.when(cond)(act)

    for s in streams:
        s.u_copy(0).start()
    for s in streams:
        if s.kind == "A":
            for up in (True, False):
                when(s.sends_at(up, 1), lambda: s.chain_copy(up, 1).start())
    for copy in kept:
        copy.wait()
    for s in streams:
        s.u_arrival(0).wait_recv()
        if s.kind == "B":
            for up in (True, False):
                when(s.sends_at(up, 1), lambda: s.chain_copy(up, 1).start())
        s.v_copy(0).start()

    def core_copy(a, number):
        z = GatherStream.z_of(streams[0], number)
        slot = a * 7 + number
        mine = outs[a].at[:, z, :, place.c]
        theirs = outs[a].at[:, z, :, 1 - place.c]
        made = functools.partial(
            pltpu.make_async_remote_copy,
            send_sem=core_send.at[slot],
            recv_sem=core_recv.at[slot],
            device_id=place.device("c"),
            device_id_type=pl.DeviceIdType.MESH,
        )
        return made(src_ref=mine, dst_ref=mine), made(src_ref=theirs, dst_ref=theirs)

    def finish(number):
        for s in streams:
            s.v_arrival(number).wait_recv()
        for a in range(count):
            core_copy(a, number)[0].start()

    def arrival(s, step, up, number):
        s.chain_arrival(up, step).wait_recv()
        if step < CHAIN - 1:
            when(s.sends_at(up, step + 1), lambda: s.chain_copy(up, step + 1).start())
        if s.kind == "A":
            s.u_copy(number).start()
        else:
            s.v_copy(number).start()

    def side(s, up, number):
        s.u_arrival(number).wait_recv()
        s.v_copy(number).start()

    for step in range(1, CHAIN):
        for s in streams:
            each_arrival(s, step, functools.partial(arrival, s, step))
        if step == 1:
            finish(0)
        for s in streams:
            if s.kind == "A":
                each_arrival(s, step, functools.partial(side, s))
        if step > 1:
            each_arrival(streams[0], step - 1, lambda up, number: finish(number))
    each_arrival(streams[0], CHAIN - 1, lambda up, number: finish(number))

    def last(up, number):
        for a in range(count):
            core_copy(a, number)[1].wait_recv()
            core_copy(a, number)[0].wait_send()
        for s in streams:
            if s.kind == "A":
                s.u_copy(number).wait_send()
            s.v_copy(number).wait_send()

    last(True, 0)
    for s in streams:
        if s.kind == "B":
            s.u_copy(0).wait_send()
        for step in range(1, CHAIN):
            for up in (True, False):
                when(s.sends_at(up, step), lambda: s.chain_copy(up, step).wait_send())
    for step in range(1, CHAIN):
        each_arrival(streams[0], step, last)


def plans_for(arrays):
    plans = []
    for a, array in enumerate(arrays):
        u, v = ("x", "y") if a % 2 == 0 else ("y", "x")
        if array.shape[-1] % 768 == 0:
            plans += [(a, 0, "B", "x", "y"), (a, 1, "B", "y", "x"), (a, 2, "A", u, v)]
        else:
            plans.append((a, None, "A", u, v))
    return tuple(plans)


def gather_weights(arrays, collective_id):
    plans = plans_for(arrays)
    count = len(arrays)
    shapes = [(a.shape[0], CHAIN, 2, 2, 2) + a.shape[1:] for a in arrays]
    sems = pltpu.SemaphoreType.DMA
    outs = pl.pallas_call(
        functools.partial(gather_kernel, plans, count),
        out_shape=[jax.ShapeDtypeStruct(s, a.dtype) for s, a in zip(shapes, arrays)],
        in_specs=[pl.BlockSpec(memory_space=pltpu.VMEM)] * count,
        out_specs=[pl.BlockSpec(memory_space=pltpu.HBM)] * count,
        scratch_shapes=[
            sems((len(plans), SLOTS)),
            sems((len(plans), SLOTS)),
            sems((count * 7,)),
            sems((count * 7,)),
            sems((count,)),
        ],
        compiler_params=pltpu.CompilerParams(collective_id=collective_id, has_side_effects=True),
    )(*arrays)
    return [o.reshape(a.shape[0], -1, a.shape[2]) for o, a in zip(outs, arrays)]


def add_into(target, terms, cols):
    lead = target.shape[:-2]
    total = 1
    for size in lead:
        total *= size

    def one(flat, unused):
        index = []
        for size in reversed(lead):
            index.insert(0, flat % size)
            flat = flat // size
        value = target[(*index, slice(None), cols)].astype(jnp.float32)
        for term in terms:
            value = value + term[(*index, slice(None), cols)].astype(jnp.float32)
        target[(*index, slice(None), cols)] = value.astype(target.dtype)
        return unused

    lax.fori_loop(0, total, one, 0)


class ReduceStream:
    def __init__(self, place, bufs, third, kind, u, v, send, recv):
        self.place, self.kind, self.u, self.v, self.send, self.recv = place, kind, u, v, send, recv
        self.acc, self.side_v, self.side_u, self.chain = bufs
        self.cols = third_of(self.acc.shape[-1], third)

    def z_of(self, number):
        return GatherStream.z_of(self, number)

    def pair(self, z, v_other=False):
        p = self.place
        flip = lambda at: 1 - at if v_other else at
        if self.u == "x":
            return self.acc.at[:, z, :, flip(p.y)]
        return self.acc.at[:, z, flip(p.x), :]

    def single(self, z, u_other=False):
        p = self.place
        x = 1 - p.x if u_other and self.u == "x" else p.x
        y = 1 - p.y if u_other and self.u == "y" else p.y
        return self.acc.at[:, z, x, y]

    def copy(self, slot, src, dst, axis):
        return pltpu.make_async_remote_copy(
            src_ref=src.at[..., self.cols],
            dst_ref=dst.at[..., self.cols],
            send_sem=self.send.at[slot],
            recv_sem=self.recv.at[slot],
            device_id=self.place.device(axis),
            device_id_type=pl.DeviceIdType.MESH,
        )

    def v_copy(self, number):
        z = self.z_of(number)
        return self.copy(6 + number, self.pair(z, True), self.side_v.at[:, z], self.v)

    def v_add(self, number):
        z = self.z_of(number)
        self.v_copy(number).wait_recv()
        add_into(self.pair(z), [self.side_v.at[:, z]], self.cols)

    def u_copy(self, number):
        z = self.z_of(number)
        return self.copy(13 + number, self.single(z, True), self.side_u.at[:, z], self.u)

    def u_add(self, number):
        z = self.z_of(number)
        self.u_copy(number).wait_recv()
        add_into(self.single(z), [self.side_u.at[:, z]], self.cols)

    def chain_block(self, z):
        return self.pair(z) if self.kind == "B" else self.single(z)

    def chain_slot(self, up, step):
        at = self.chain.at[:, 0 if up else 1, step - 1]
        return at if self.kind == "B" else at.at[:, 0]

    def chain_copy(self, up, step):
        z = self.place.z + step if up else self.place.z - step
        return self.copy(
            step - 1 if up else step + 2,
            self.chain_block(z),
            self.chain_slot(up, step),
            "up" if up else "down",
        )

    def has_before(self, up):
        return self.place.z > 0 if up else self.place.z < CHAIN - 1

    def chain_arrival(self, up, step):
        ref = self.chain_slot(up, step)
        return self.copy(step - 1 if up else step + 2, ref, ref, "up" if up else "down")

    def chain_step(self, up, step):
        z = self.place.z + step if up else self.place.z - step
        if step < CHAIN - 1:

            @pl.when(self.has_before(up))
            def arrived():
                self.chain_arrival(up, step + 1).wait_recv()
                add_into(self.chain_block(z), [self.chain_slot(up, step + 1)], self.cols)

        self.chain_copy(up, step).start()

    def chain_end(self):
        for up in (True, False):

            @pl.when(self.has_before(up))
            def arrived():
                self.chain_arrival(up, 1).wait_recv()
                add_into(self.chain_block(self.place.z), [self.chain_slot(up, 1)], self.cols)


def reduce_kernel(plans, count, *refs):
    grads = refs[:count]
    outs = refs[count : 2 * count]
    bufs = refs[2 * count : 7 * count]
    send, recv, core_send, core_recv, local = refs[7 * count :]
    place = Place()
    accs, cores = bufs[:count], bufs[count : 2 * count]
    streams = [
        ReduceStream(
            place, [bufs[k * count + a] for k in (0, 2, 3, 4)], third, kind, u, v, send.at[i], recv.at[i]
        )
        for i, (a, third, kind, u, v) in enumerate(plans)
    ]

    def z_of(number):
        return GatherStream.z_of(streams[0], number)

    def valid(number):
        return place.z >= number if number < CHAIN else place.z <= 2 * (CHAIN - 1) - number

    def each(act):
        for step in range(CHAIN - 1, 0, -1):
            for number in (step, step + CHAIN - 1):
                pl.when(valid(number))(functools.partial(act, number))
        act(0)

    def load(a, number):
        z = z_of(number)
        return pltpu.make_async_copy(
            grads[a].at[:, z, :, place.c], accs[a].at[:, z], local.at[a * 7 + number]
        )

    def core_copy(a, number):
        z = z_of(number)
        return pltpu.make_async_remote_copy(
            src_ref=grads[a].at[:, z, :, 1 - place.c],
            dst_ref=cores[a].at[:, z],
            send_sem=core_send.at[a * 7 + number],
            recv_sem=core_recv.at[a * 7 + number],
            device_id=place.device("c"),
            device_id_type=pl.DeviceIdType.MESH,
        )

    def begin(number):
        for a in range(count):
            load(a, number).start()

    def begin_core(number):
        for a in range(count):
            core_copy(a, number).start()

    each(begin)
    greet(place)
    each(begin_core)

    def first(number):
        z = z_of(number)
        for a in range(count):
            load(a, number).wait()
            core_copy(a, number).wait_recv()
            add_into(accs[a].at[:, z], [cores[a].at[:, z]], slice(None))
            for s, plan in zip(streams, plans):
                if plan[0] == a:
                    s.v_copy(number).start()

    each(first)

    def second(number):
        for s in streams:
            s.v_add(number)
            if s.kind == "A":
                s.u_copy(number).start()
            elif number > 0:
                up = number >= CHAIN
                s.chain_step(up, number - (CHAIN - 1) if up else number)

    each(second)

    def third(number):
        for s in streams:
            if s.kind == "A":
                s.u_add(number)
                if number > 0:
                    up = number >= CHAIN
                    s.chain_step(up, number - (CHAIN - 1) if up else number)

    each(third)
    for s in streams:
        if s.kind == "B":
            s.chain_end()
            s.u_copy(0).start()
    for s in streams:
        if s.kind == "A":
            s.chain_end()
    for s, plan in zip(streams, plans):
        if s.kind == "B":
            s.u_add(0)
    for a in range(count):
        for item in range(outs[a].shape[0]):
            outs[a][item] = accs[a][item, place.z, place.x, place.y].astype(jnp.float32)

    def last(number):
        for a in range(count):
            core_copy(a, number).wait_send()
        for s in streams:
            s.v_copy(number).wait_send()
            if s.kind == "A" or number == 0:
                s.u_copy(number).wait_send()
            if number > 0:
                up = number >= CHAIN
                s.chain_copy(up, number - (CHAIN - 1) if up else number).wait_send()

    each(last)


def reduce_gradients(grads, collective_id):
    parts = 8 * CHAIN
    arrays = [g.reshape(g.shape[0], CHAIN, 2, 2, 2, g.shape[1] // parts, g.shape[2]) for g in grads]
    plans = plans_for(arrays)
    count = len(arrays)
    sems = pltpu.SemaphoreType.DMA
    scratch = []
    for lead in ((CHAIN, 2, 2), (CHAIN, 2, 2), (CHAIN, 2), (CHAIN,), (2, CHAIN - 1, 2)):
        for a in arrays:
            scratch.append(pltpu.VMEM((a.shape[0],) + lead + a.shape[-2:], a.dtype))
    return pl.pallas_call(
        functools.partial(reduce_kernel, plans, count),
        out_shape=[jax.ShapeDtypeStruct((a.shape[0],) + a.shape[-2:], jnp.float32) for a in arrays],
        in_specs=[pl.BlockSpec(memory_space=pltpu.HBM)] * count,
        out_specs=[pl.BlockSpec(memory_space=pltpu.VMEM)] * count,
        scratch_shapes=scratch
        + [
            sems((len(plans), SLOTS)),
            sems((len(plans), SLOTS)),
            sems((count * 7,)),
            sems((count * 7,)),
            sems((count * 7,)),
        ],
        compiler_params=pltpu.CompilerParams(
            collective_id=collective_id, has_side_effects=True, vmem_limit_bytes=60 * 2**20
        ),
    )(*arrays)


def hop(value, bit):
    size = 4 * CHAIN * 2
    return lax.ppermute(value, BOTH, [(i, i ^ bit) for i in range(size)])


def sum_everywhere(value):
    for bit in (1, 2, 4, 8, 16):
        value = value + hop(value, bit)
    return value


def whole_row(halves):
    mine = lax.axis_index("seq")
    keep = lax.dynamic_index_in_dim(halves, mine, 0, keepdims=False)
    other = lax.ppermute(
        lax.dynamic_index_in_dim(halves, 1 - mine, 0, keepdims=False), "seq", [(0, 1), (1, 0)]
    )
    first = jnp.where(mine == 0, keep, other)
    second = jnp.where(mine == 0, other, keep)
    return jnp.concatenate([first, second], axis=0)


def own_slots(row):
    mine = lax.axis_index("seq")
    half = row.shape[0] // 2
    keep = lax.dynamic_slice_in_dim(row, mine * half, half, 0)
    sent = lax.dynamic_slice_in_dim(row, (1 - mine) * half, half, 0).astype(jnp.bfloat16)
    other = lax.ppermute(sent, "seq", [(0, 1), (1, 0)]).astype(row.dtype)
    return jnp.stack([jnp.where(mine == 0, keep, other), jnp.where(mine == 0, other, keep)])


def matmul(left, right):
    return jnp.dot(left, right, preferred_element_type=jnp.float32)


def matmul_back(grads, weight):
    return dotf(grads, weight, CONTRACT_LAST)


def weight_grad(inputs, grads):
    return dotf(inputs, grads, CONTRACT_FIRST).astype(jnp.bfloat16)


def rms_scale(values, gain_vec):
    return (
        values * lax.rsqrt(jnp.mean(values * values, axis=-1, keepdims=True) + EPSILON) * gain_vec
    )


def gelu_float(values):
    return jax.nn.gelu(values, approximate=True)


def norm_back(values, gain_vec, upstream):
    unused_value, pullback = jax.vjp(rms_scale, values, gain_vec)
    return pullback(upstream)


def low(values):
    return values.astype(jnp.bfloat16)


def feedforward_back(normed, pre_values, active, widen, narrow, upstream):
    branch_low = low(upstream)
    narrow_grad = weight_grad(active, branch_low)
    active_grad = matmul_back(branch_low, narrow)
    unused_value, gelu_pull = jax.vjp(gelu_float, pre_values)
    pre_low = low(gelu_pull(active_grad)[0])
    return (matmul_back(pre_low, widen), weight_grad(normed, pre_low), narrow_grad)


def distance_table(table_in, buckets):
    ids = jnp.arange(BUCKETS, dtype=jnp.int32)
    selector = (buckets[:, None] == ids[None, :]).astype(jnp.float32)
    by_distance = jnp.einsum("db,bh->hd", selector, table_in, precision=HIGHEST_PRECISION)
    padded = jnp.pad(by_distance, ((0, 0), (0, SPAN - by_distance.shape[1])))
    return padded.reshape(HEADS // 2, 2, SPAN), selector


def table_grad(selector, by_distance):
    flat = by_distance.reshape(HEADS, SPAN)[:, : selector.shape[0]]
    return jnp.einsum("db,hd->bh", selector, flat, precision=HIGHEST_PRECISION)


def layers(encoder_row, decoder_row, lengths_row, target_length, buckets, gains, weights, encoder_cotangent, decoder_cotangent, encoder_table_in, decoder_table_in):
    encoder_length, feature_count = encoder_row.shape
    decoder_length = decoder_row.shape[0]
    half = encoder_length - 1
    positions = jnp.arange(encoder_length, dtype=jnp.int32)
    target_positions = jnp.arange(decoder_length, dtype=jnp.int32)
    count = lengths_row.shape[0]
    order = jnp.arange(count, dtype=jnp.int32)
    ends = jnp.sum(jnp.where(order[None, :] <= order[:, None], lengths_row[None, :], 0), axis=1)
    segment = jnp.sum((ends[None, :] <= positions[:, None]).astype(jnp.int32), axis=1)
    valid = positions < jnp.sum(lengths_row)
    target_valid = target_positions < target_length
    column = lambda code: code.astype(jnp.int32)[:, None]
    line = lambda code: code.astype(jnp.int32)[None, :]
    encoder_codes = (column(segment), line(segment))
    self_codes = (column(target_valid), line(target_valid))
    cross_codes = (column(target_valid), line(valid))
    encoder_table, selector = distance_table(encoder_table_in, buckets)
    decoder_table, unused_selector = distance_table(decoder_table_in, buckets)
    (
        first_gain,
        second_gain,
        final_gain,
        self_gain,
        cross_gain,
        third_gain,
    ) = [gains[i] for i in range(6)]
    w = weights

    residual = encoder_row.astype(jnp.float32)
    first_normed = low(rms_scale(residual, first_gain))
    queries = low(matmul(first_normed, w["eq"]))
    keys = low(matmul(first_normed, w["ek"]))
    values = low(matmul(first_normed, w["ev"]))
    attended = attn_fwd("segment", half, queries, keys, values, *encoder_codes, encoder_table)
    middle = residual + matmul(attended, w["eo"])
    second_normed = low(rms_scale(middle, second_gain))
    pre = matmul(second_normed, w["ew"])
    active = low(gelu_float(pre))
    branch = matmul(active, w["en"])
    output = middle + branch
    memory = low(rms_scale(output, final_gain))

    target = decoder_row.astype(jnp.float32)
    self_normed = low(rms_scale(target, self_gain))
    self_queries = low(matmul(self_normed, w["dq"]))
    self_keys = low(matmul(self_normed, w["dk"]))
    self_values = low(matmul(self_normed, w["dv"]))
    self_attended = attn_fwd(
        "causal", half, self_queries, self_keys, self_values, *self_codes, decoder_table
    )
    target_middle = target + matmul(self_attended, w["do"])
    cross_normed = low(rms_scale(target_middle, cross_gain))
    cross_queries = low(matmul(cross_normed, w["cq"]))
    cross_keys = low(matmul(memory, w["ck"]))
    cross_values = low(matmul(memory, w["cv"]))
    cross_attended = attn_fwd(
        "cross", half, cross_queries, cross_keys, cross_values, *cross_codes, None
    )
    crossed = target_middle + matmul(cross_attended, w["co"])
    third_normed = low(rms_scale(crossed, third_gain))
    decoder_pre = matmul(third_normed, w["dw"])
    decoder_active = low(gelu_float(decoder_pre))
    decoder_branch = matmul(decoder_active, w["dn"])
    decoder_output = crossed + decoder_branch

    grads = {}
    upstream = decoder_cotangent.astype(jnp.float32)
    normed_grad, grads["dw"], grads["dn"] = feedforward_back(
        third_normed, decoder_pre, decoder_active, w["dw"], w["dn"], upstream
    )
    part, third_gain_grad = norm_back(crossed, third_gain, normed_grad)
    crossed_grad = upstream + part

    crossed_low = low(crossed_grad)
    grads["co"] = weight_grad(cross_attended, crossed_low)
    mixed_grad = low(matmul_back(crossed_low, w["co"]))
    query_low, key_low, value_low = attn_bwd(
        "cross", half, cross_queries, cross_keys, cross_values, mixed_grad, *cross_codes, None
    )
    grads["cq"] = weight_grad(cross_normed, query_low)
    grads["ck"] = weight_grad(memory, key_low)
    grads["cv"] = weight_grad(memory, value_low)
    memory_grad = matmul_back(key_low, w["ck"]) + matmul_back(value_low, w["cv"])
    part, cross_gain_grad = norm_back(target_middle, cross_gain, matmul_back(query_low, w["cq"]))
    middle_grad = crossed_grad + part

    middle_low = low(middle_grad)
    grads["do"] = weight_grad(self_attended, middle_low)
    mixed_grad = low(matmul_back(middle_low, w["do"]))
    query_low, key_low, value_low, decoder_distance = attn_bwd(
        "causal", half, self_queries, self_keys, self_values, mixed_grad, *self_codes, decoder_table
    )
    grads["dq"] = weight_grad(self_normed, query_low)
    grads["dk"] = weight_grad(self_normed, key_low)
    grads["dv"] = weight_grad(self_normed, value_low)
    normed_grad = (
        matmul_back(query_low, w["dq"])
        + matmul_back(key_low, w["dk"])
        + matmul_back(value_low, w["dv"])
    )
    part, self_gain_grad = norm_back(target, self_gain, normed_grad)
    decoder_input_grad = middle_grad + part

    part, final_gain_grad = norm_back(output, final_gain, memory_grad)
    output_grad = encoder_cotangent.astype(jnp.float32) + part
    normed_grad, grads["ew"], grads["en"] = feedforward_back(
        second_normed, pre, active, w["ew"], w["en"], output_grad
    )
    part, second_gain_grad = norm_back(middle, second_gain, normed_grad)
    encoder_middle_grad = output_grad + part

    middle_low = low(encoder_middle_grad)
    grads["eo"] = weight_grad(attended, middle_low)
    mixed_grad = low(matmul_back(middle_low, w["eo"]))
    query_low, key_low, value_low, encoder_distance = attn_bwd(
        "segment", half, queries, keys, values, mixed_grad, *encoder_codes, encoder_table
    )
    grads["eq"] = weight_grad(first_normed, query_low)
    grads["ek"] = weight_grad(first_normed, key_low)
    grads["ev"] = weight_grad(first_normed, value_low)
    normed_grad = (
        matmul_back(query_low, w["eq"])
        + matmul_back(key_low, w["ek"])
        + matmul_back(value_low, w["ev"])
    )
    part, first_gain_grad = norm_back(residual, first_gain, normed_grad)
    encoder_input_grad = encoder_middle_grad + part

    keep = valid[:, None]
    target_keep = target_valid[:, None]
    sums = jnp.stack(
        [
            jnp.sum(jnp.where(keep, output * output, 0.0)),
            jnp.sum(jnp.where(keep, branch * branch, 0.0)),
            jnp.sum(jnp.where(target_keep, decoder_output * decoder_output, 0.0)),
            jnp.sum(jnp.where(target_keep, decoder_branch * decoder_branch, 0.0)),
            jnp.sum(valid.astype(jnp.float32)),
            jnp.sum(target_valid.astype(jnp.float32)),
        ]
    )
    small = jnp.concatenate(
        [
            first_gain_grad,
            second_gain_grad,
            final_gain_grad,
            self_gain_grad,
            cross_gain_grad,
            third_gain_grad,
            table_grad(selector, encoder_distance).reshape(-1),
            table_grad(selector, decoder_distance).reshape(-1),
            sums,
        ]
    )
    return (output, decoder_output, encoder_input_grad, decoder_input_grad, grads, small)


GROUPS = (
    ("eq", "ek", "ev", "eo"),
    ("ew",),
    ("en",),
    ("dq", "dk", "dv", "do", "cq", "ck", "cv", "co"),
    ("dw",),
    ("dn",),
)
WEIGHT_ARGS = {
    "eq": 6, "ek": 7, "ev": 8, "eo": 9, "ew": 12, "en": 13, "dq": 16, "dk": 17, "dv": 18, "do": 19,
    "cq": 22, "ck": 23, "cv": 24, "co": 25, "dw": 27, "dn": 28,
}
GAIN_ARGS = (5, 11, 14, 15, 21, 26)
WEIGHT_OUTS = {
    "eq": 5, "ek": 6, "ev": 7, "eo": 8, "ew": 11, "en": 12, "dq": 15, "dk": 16, "dv": 17, "do": 18,
    "cq": 21, "ck": 22, "cv": 23, "co": 24, "dw": 26, "dn": 27,
}
GAIN_OUTS = (4, 10, 13, 14, 20, 25)


def body(near, *args):
    row_count = lax.axis_size("rows") * lax.axis_size("seq")
    me = lax.axis_index("rows") * lax.axis_size("seq") + lax.axis_index("seq")
    seq_index = lax.axis_index("seq")
    shards = {name: args[i] for name, i in WEIGHT_ARGS.items()}
    own_gains = jnp.stack([args[i] for i in GAIN_ARGS])
    weights = {}
    if near:
        tile = jnp.pad(own_gains, ((0, 2), (0, 128 - own_gains.shape[1])))[None]
        stacks = [jnp.stack([shards[n] for n in names]) for names in GROUPS]
        gathered = gather_weights(stacks + [tile], 0)
        for names, stack in zip(GROUPS, gathered):
            weights.update((n, stack[i]) for i, n in enumerate(names))
        tiles = gathered[-1].reshape(row_count, 8, 128)[:, :6, : own_gains.shape[1]]
        gains = jnp.transpose(tiles, (1, 0, 2)).reshape(6, -1)
    else:
        gains = lax.all_gather(own_gains, BOTH, axis=1, tiled=True)
        for name, shard in shards.items():
            weights[name] = lax.all_gather(shard, BOTH, axis=0, tiled=True)
    encoder_row = whole_row(args[0])
    decoder_row = whole_row(args[1])
    lengths_row = lax.dynamic_index_in_dim(args[2], seq_index, 0, keepdims=False)
    target_length = lax.dynamic_index_in_dim(args[3], seq_index, 0, keepdims=False)
    output, decoder_output, encoder_input_grad, decoder_input_grad, grads, small = layers(
        encoder_row,
        decoder_row,
        lengths_row,
        target_length,
        args[4],
        gains.astype(jnp.float32),
        weights,
        whole_row(args[29]),
        whole_row(args[30]),
        args[10],
        args[20],
    )
    outs = [None] * 29
    for i, value in enumerate((output, decoder_output, encoder_input_grad, decoder_input_grad)):
        outs[i] = own_slots(value)
    reduced = {}
    if near:
        for number, groups in ((1, GROUPS[3:]), (2, GROUPS[:3])):
            stacks = [jnp.stack([grads[n] for n in names]) for names in groups]
            for names, total in zip(groups, reduce_gradients(stacks, number)):
                reduced.update((n, total[i]) for i, n in enumerate(names))
        small = sum_everywhere(small)
    else:
        for name, grad in grads.items():
            reduced[name] = lax.psum_scatter(
                grad.astype(jnp.float32), BOTH, scatter_dimension=0, tiled=True
            )
        small = lax.psum(small, BOTH)
    for name, i in WEIGHT_OUTS.items():
        outs[i] = reduced[name]
    feature_count = args[0].shape[2]
    share = feature_count // row_count
    for number, i in enumerate(GAIN_OUTS):
        outs[i] = lax.dynamic_slice_in_dim(small, number * feature_count + me * share, share)
    offset = 6 * feature_count
    size = BUCKETS * HEADS
    outs[9] = small[offset : offset + size].reshape(BUCKETS, HEADS)
    outs[19] = small[offset + size : offset + 2 * size].reshape(BUCKETS, HEADS)
    sums = small[offset + 2 * size :]
    divisors = jnp.stack([sums[4], sums[4], sums[5], sums[5]]) * feature_count
    outs[28] = jnp.sqrt(sums[:4] / divisors)
    return tuple(outs)


def solution(mesh):
    row_spec = P("rows", "seq", None)
    matrix = P(BOTH, None)
    vector = P(BOTH)
    in_specs = [row_spec, row_spec, P("rows", None), P("rows"), P()] + [None] * 26
    in_specs[10] = in_specs[20] = P()
    in_specs[29] = in_specs[30] = row_spec
    for i in GAIN_ARGS:
        in_specs[i] = vector
    for i in WEIGHT_ARGS.values():
        in_specs[i] = matrix
    out_specs = [row_spec] * 4 + [None] * 25
    out_specs[9] = out_specs[19] = out_specs[28] = P()
    for i in GAIN_OUTS:
        out_specs[i] = vector
    for i in WEIGHT_OUTS.values():
        out_specs[i] = matrix
    near = mesh.shape["rows"] == 4 * CHAIN and mesh.shape["seq"] == 2
    return jax.shard_map(
        functools.partial(body, near),
        mesh=mesh,
        in_specs=tuple(in_specs),
        out_specs=tuple(out_specs),
        check_vma=False,
    )
```

```python
import functools
from types import SimpleNamespace
from typing import NamedTuple

import jax
import jax.numpy as jnp
from jax import lax
from jax.experimental import pallas as pl
from jax.experimental.pallas import tpu as pltpu
from jax.sharding import PartitionSpec as P

HEADS = 12
BUCKETS = 32
EPSILON = 1e-06
NEGATIVE = -1e30
HIGHEST_PRECISION = lax.Precision.HIGHEST
BOTH = ("rows", "seq")
CHAIN = 4
PAIRS = HEADS // 2

SPAN=1024
CONTRACT_LAST=(((1,),(1,)),((),()))
CONTRACT_FIRST=(((0,),(0,)),((),()))

def dotf(a,b,dims):
    return lax.dot_general(a,b,dims,preferred_element_type=jnp.float32)

def allowed_of(mode,qcode,kcode,shape):
    if mode=="segment":
        return qcode==kcode
    if mode=="causal":
        qi=lax.broadcasted_iota(jnp.int32,shape,0); ki=lax.broadcasted_iota(jnp.int32,shape,1)
        return (ki<=qi)&(qcode==kcode)
    return (qcode==0)|(kcode==1)

def probs_of(q,k,row,allowed,half):
    s=dotf(q,k,CONTRACT_LAST)
    if row is not None:
        wide=jnp.broadcast_to(row,(s.shape[0],SPAN))
        s=s+pltpu.roll(wide,SPAN-half,1,stride=1,stride_axis=0)[:,:s.shape[1]]
    s=jnp.where(allowed,s,NEGATIVE)
    e=jnp.exp(s-jnp.max(s,axis=-1,keepdims=True))
    return e*(1.0/jnp.sum(e,axis=-1,keepdims=True))

def fwd_kernel(mode,half,*refs):
    if mode=="cross":
        q_ref,k_ref,v_ref,qc,kc,o_ref=refs; t_ref=None
    else:
        q_ref,k_ref,v_ref,qc,kc,t_ref,o_ref=refs
    allowed=allowed_of(mode,qc[...],kc[...],(q_ref.shape[0],k_ref.shape[0]))
    for h in range(2):
        sl=slice(64*h,64*h+64)
        p=probs_of(q_ref[:,sl],k_ref[:,sl],None if t_ref is None else t_ref[0,h:h+1,:],allowed,half)
        o_ref[:,sl]=jnp.dot(p.astype(jnp.bfloat16),v_ref[:,sl],preferred_element_type=jnp.float32).astype(jnp.bfloat16)

def bwd_kernel(mode,half,*refs):
    if mode=="cross":
        q_ref,k_ref,v_ref,g_ref,qc,kc,dq_ref,dk_ref,dv_ref=refs; t_ref=None
    else:
        q_ref,k_ref,v_ref,g_ref,qc,kc,t_ref,dq_ref,dk_ref,dv_ref,dt_ref=refs
    allowed=allowed_of(mode,qc[...],kc[...],(q_ref.shape[0],k_ref.shape[0]))
    for h in range(2):
        sl=slice(64*h,64*h+64)
        q=q_ref[:,sl];k=k_ref[:,sl];v=v_ref[:,sl];g=g_ref[:,sl]
        p=probs_of(q,k,None if t_ref is None else t_ref[0,h:h+1,:],allowed,half)
        dv_ref[:,sl]=dotf(p.astype(jnp.bfloat16),g,CONTRACT_FIRST).astype(jnp.bfloat16)
        dp=dotf(g,v,CONTRACT_LAST)
        ds=p*(dp-jnp.sum(dp*p,axis=-1,keepdims=True))
        dsb=ds.astype(jnp.bfloat16)
        dq_ref[:,sl]=jnp.dot(dsb,k,preferred_element_type=jnp.float32).astype(jnp.bfloat16)
        dk_ref[:,sl]=dotf(dsb,q,CONTRACT_FIRST).astype(jnp.bfloat16)
        if t_ref is not None:
            sq=ds.shape[0]
            flip=(lax.broadcasted_iota(jnp.int32,(sq,sq),0)+lax.broadcasted_iota(jnp.int32,(sq,sq),1)==sq-1).astype(jnp.bfloat16)
            flipped=jnp.dot(flip,dsb,preferred_element_type=jnp.float32)
            wide=jnp.concatenate([flipped,jnp.zeros((sq,SPAN-ds.shape[1]),jnp.float32)],axis=1)
            rolled=pltpu.roll(wide,half-(sq-1),1,stride=1,stride_axis=0)
            dt_ref[0,h:h+1,:]=jnp.sum(rolled,axis=0,keepdims=True)

def attn(kernel,mode,half,outs,q,k,v,extra,qc,kc,table):
    sq,width=q.shape; sk=k.shape[0]
    qs=pl.BlockSpec((sq,128),lambda i:(0,i)); ks=pl.BlockSpec((sk,128),lambda i:(0,i))
    ts=pl.BlockSpec((1,2,SPAN),lambda i:(i,0,0))
    ins=[q,k,v]+extra+[qc,kc]; specs=[qs,ks,ks]+[qs]*len(extra)+[pl.BlockSpec((sq,1),lambda i:(0,0)),pl.BlockSpec((1,sk),lambda i:(0,0))]
    if table is not None: ins.append(table); specs.append(ts)
    shapes={"q":(jax.ShapeDtypeStruct((sq,width),jnp.bfloat16),qs),"k":(jax.ShapeDtypeStruct((sk,width),jnp.bfloat16),ks),"t":(jax.ShapeDtypeStruct((width//128,2,SPAN),jnp.float32),ts)}
    return pl.pallas_call(functools.partial(kernel,mode,half),grid=(width//128,),in_specs=specs,
        out_shape=[shapes[o][0] for o in outs],out_specs=[shapes[o][1] for o in outs],
        compiler_params=pltpu.CompilerParams(vmem_limit_bytes=48*2**20))(*ins)

def attn_fwd(mode,half,q,k,v,qc,kc,table):
    return attn(fwd_kernel,mode,half,"q",q,k,v,[],qc,kc,table)[0]
def attn_bwd(mode,half,q,k,v,g,qc,kc,table):
    return attn(bwd_kernel,mode,half,"qkk"+("t" if table is not None else ""),q,k,v,[g],qc,kc,table)


class Place:
    def __init__(self):
        row = lax.axis_index("rows")
        self.z, self.x, self.c, self.y = row // 4, (row // 2) % 2, row % 2, lax.axis_index("seq")

    def device(self, axis):
        z, x, c, y = self.z, self.x, self.c, self.y
        if axis == "up":
            z = z + 1
        if axis == "down":
            z = z - 1
        if axis == "n":
            z = z + 1 - 2 * (z % 2)
        if axis == "f":
            z = (z + 2) % 4
        if axis == "x":
            x = 1 - x
        if axis == "c":
            c = 1 - c
        if axis == "y":
            y = 1 - y
        return {"rows": z * 4 + x * 2 + c, "seq": y}


def greet(place, far=False):
    barrier = pltpu.get_barrier_semaphore()

    def signal(axis):
        pl.semaphore_signal(
            barrier, inc=1, device_id=place.device(axis), device_id_type=pl.DeviceIdType.MESH
        )

    for axis in "xcyf" if far else "xcy":
        signal(axis)
    pl.when(place.z < CHAIN - 1)(lambda: signal("up"))
    pl.when(place.z > 0)(lambda: signal("down"))
    ends = (place.z == 0) | (place.z == CHAIN - 1)
    pl.when(ends)(lambda: pl.semaphore_wait(barrier, 5 if far else 4))
    pl.when(jnp.logical_not(ends))(lambda: pl.semaphore_wait(barrier, 6 if far else 5))


def third_of(width, third):
    if third is None:
        return slice(None)
    return slice(width // 3 * third, width // 3 * (third + 1))


class GatherStream:
    def __init__(self, place, own, out, third, kind, u, v, send, recv):
        self.place, self.own, self.out, self.third = place, own, out, third
        self.kind, self.u, self.v, self.send, self.recv = kind, u, v, send, recv
        self.span = third_of(own.shape[-1], third)

    def block(self, z, pair):
        p = self.place
        x = slice(None) if pair and self.u == "x" else p.x
        y = slice(None) if pair and self.u == "y" else p.y
        return self.out.at[:, z, x, p.c, y, :, self.span]

    def other(self, z, axis, pair):
        p = self.place
        x, y = p.x, p.y
        if pair and self.u == "x":
            x = slice(None)
        elif axis == "x":
            x = 1 - x
        if pair and self.u == "y":
            y = slice(None)
        elif axis == "y":
            y = 1 - y
        return self.out.at[:, z, x, p.c, y, :, self.span]

    def copy(self, slot, src, dst, axis):
        return pltpu.make_async_remote_copy(
            src_ref=src,
            dst_ref=dst,
            send_sem=self.send.at[slot],
            recv_sem=self.recv.at[slot],
            device_id=self.place.device(axis),
            device_id_type=pl.DeviceIdType.MESH,
        )

    def first(self, z):
        return self.own.at[:, :, self.span]

    def chain_copy(self, up, step):
        pair = self.kind == "B"
        z = self.place.z - (step - 1) if up else self.place.z + (step - 1)
        src = self.first(z) if step == 1 and not pair else self.block(z, pair)
        return self.copy(step - 1 if up else step + 2, src, self.block(z, pair), "up" if up else "down")

    def chain_arrival(self, up, step):
        pair = self.kind == "B"
        z = self.place.z - step if up else self.place.z + step
        ref = self.block(z, pair)
        return self.copy(step - 1 if up else step + 2, ref, ref, "up" if up else "down")

    def sends_at(self, up, step):
        z = self.place.z
        if up:
            return (z < CHAIN - 1) & (z >= step - 1)
        return (z > 0) & (z <= CHAIN - step)

    def arrives_at(self, up, step):
        z = self.place.z
        return z >= step if up else z <= CHAIN - 1 - step

    def side_copy(self, slot, z, axis, pair, fresh):
        src = self.first(z) if fresh else self.block(z, pair)
        return self.copy(slot, src, self.block(z, pair), axis)

    def side_arrival(self, slot, z, axis, pair):
        ref = self.other(z, axis, pair)
        return self.copy(slot, ref, ref, axis)

    def z_of(self, number):
        if number == 0:
            return self.place.z
        return self.place.z - number if number <= CHAIN - 1 else self.place.z + (number - CHAIN + 1)

    def u_copy(self, number):
        return self.side_copy(6 + number, self.z_of(number), self.u, False, number == 0)

    def u_arrival(self, number):
        return self.side_arrival(6 + number, self.z_of(number), self.u, False)

    def v_copy(self, number):
        return self.side_copy(13 + number, self.z_of(number), self.v, True, False)

    def v_arrival(self, number):
        return self.side_arrival(13 + number, self.z_of(number), self.v, True)


SLOTS = 20


def each_arrival(stream, step, act):
    for up in (True, False):
        number = step if up else step + CHAIN - 1
        pl.when(stream.arrives_at(up, step))(functools.partial(act, up, number))


def plans_for(arrays):
    plans = []
    for a, array in enumerate(arrays):
        u, v = ("x", "y") if a % 2 == 0 else ("y", "x")
        if array.shape[-1] % 768 == 0:
            plans += [(a, 0, "B", "x", "y"), (a, 1, "B", "y", "x"), (a, 2, "A", u, v)]
        else:
            plans.append((a, None, "A", u, v))
    return tuple(plans)


def add_into(target, terms, span):
    lead = target.shape[:-2]
    total = 1
    for size in lead:
        total *= size

    def one(flat, unused):
        index = []
        for size in reversed(lead):
            index.insert(0, flat % size)
            flat = flat // size
        value = target[(*index, slice(None), span)].astype(jnp.float32)
        for term in terms:
            value = value + term[(*index, slice(None), span)].astype(jnp.float32)
        target[(*index, slice(None), span)] = value.astype(target.dtype)
        return unused

    lax.fori_loop(0, total, one, 0)


class ReduceStream:
    def __init__(self, place, bufs, third, kind, u, v, send, recv):
        self.place, self.kind, self.u, self.v, self.send, self.recv = place, kind, u, v, send, recv
        self.acc, self.side_v, self.side_u, self.chain = bufs
        self.span = third_of(self.acc.shape[-1], third)

    def z_of(self, number):
        return GatherStream.z_of(self, number)

    def pair(self, z, v_other=False):
        p = self.place
        flip = lambda at: 1 - at if v_other else at
        if self.u == "x":
            return self.acc.at[:, z, :, flip(p.y)]
        return self.acc.at[:, z, flip(p.x), :]

    def single(self, z, u_other=False):
        p = self.place
        x = 1 - p.x if u_other and self.u == "x" else p.x
        y = 1 - p.y if u_other and self.u == "y" else p.y
        return self.acc.at[:, z, x, y]

    def copy(self, slot, src, dst, axis):
        return pltpu.make_async_remote_copy(
            src_ref=src.at[..., self.span],
            dst_ref=dst.at[..., self.span],
            send_sem=self.send.at[slot],
            recv_sem=self.recv.at[slot],
            device_id=self.place.device(axis),
            device_id_type=pl.DeviceIdType.MESH,
        )

    def v_copy(self, number):
        z = self.z_of(number)
        return self.copy(6 + number, self.pair(z, True), self.side_v.at[:, z], self.v)

    def v_add(self, number):
        z = self.z_of(number)
        self.v_copy(number).wait_recv()
        add_into(self.pair(z), [self.side_v.at[:, z]], self.span)

    def u_copy(self, number):
        z = self.z_of(number)
        return self.copy(13 + number, self.single(z, True), self.side_u.at[:, z], self.u)

    def u_add(self, number):
        z = self.z_of(number)
        self.u_copy(number).wait_recv()
        add_into(self.single(z), [self.side_u.at[:, z]], self.span)

    def chain_block(self, z):
        return self.pair(z) if self.kind == "B" else self.single(z)

    def chain_slot(self, up, step):
        at = self.chain.at[:, 0 if up else 1, step - 1]
        return at if self.kind == "B" else at.at[:, 0]

    def chain_copy(self, up, step):
        z = self.place.z + step if up else self.place.z - step
        return self.copy(
            step - 1 if up else step + 2,
            self.chain_block(z),
            self.chain_slot(up, step),
            "up" if up else "down",
        )

    def has_before(self, up):
        return self.place.z > 0 if up else self.place.z < CHAIN - 1

    def chain_arrival(self, up, step):
        ref = self.chain_slot(up, step)
        return self.copy(step - 1 if up else step + 2, ref, ref, "up" if up else "down")

    def chain_step(self, up, step):
        z = self.place.z + step if up else self.place.z - step
        if step < CHAIN - 1:

            @pl.when(self.has_before(up))
            def arrived():
                self.chain_arrival(up, step + 1).wait_recv()
                add_into(self.chain_block(z), [self.chain_slot(up, step + 1)], self.span)

        self.chain_copy(up, step).start()

    def chain_end(self):
        for up in (True, False):

            @pl.when(self.has_before(up))
            def arrived():
                self.chain_arrival(up, 1).wait_recv()
                add_into(self.chain_block(self.place.z), [self.chain_slot(up, 1)], self.span)


class Reduction:
    def __init__(self, place, plans, items, outs, bufs, sems):
        count = len(items)
        self.place, self.plans, self.items, self.outs = place, plans, items, outs
        send, recv, self.core_send, self.core_recv, self.local = sems
        self.accs, self.cores = bufs[:count], bufs[count : 2 * count]
        self.streams = [
            ReduceStream(
                place, [bufs[k * count + a] for k in (0, 2, 3, 4)], third, kind, u, v,
                send.at[i], recv.at[i],
            )
            for i, (a, third, kind, u, v) in enumerate(plans)
        ]

    def z_of(self, number):
        return GatherStream.z_of(self, number)

    def valid(self, number):
        z = self.place.z
        return z >= number if number < CHAIN else z <= 2 * (CHAIN - 1) - number

    def at(self, number, act):
        if number == 0:
            act(0)
        else:
            pl.when(self.valid(number))(functools.partial(act, number))

    def each(self, act):
        for number in NUMBERS:
            self.at(number, act)

    def begin(self):
        def loads(number):
            z = self.z_of(number)
            for a, refs in enumerate(self.items):
                for i, ref in enumerate(refs):
                    pltpu.make_async_copy(
                        ref.at[z, :, self.place.c],
                        self.accs[a].at[i, z],
                        self.local.at[a * 7 + number],
                    ).start()

        self.each(loads)

    def core_copy(self, a, number, src, dst):
        return pltpu.make_async_remote_copy(
            src_ref=src,
            dst_ref=dst,
            send_sem=self.core_send.at[a * 7 + number],
            recv_sem=self.core_recv.at[a * 7 + number],
            device_id=self.place.device("c"),
            device_id_type=pl.DeviceIdType.MESH,
        )

    def begin_core(self):
        def sends(number):
            z = self.z_of(number)
            for a, refs in enumerate(self.items):
                for i, ref in enumerate(refs):
                    self.core_copy(
                        a, number, ref.at[z, :, 1 - self.place.c], self.cores[a].at[i, z]
                    ).start()

        self.each(sends)

    def core_whole(self, a, number):
        whole = self.cores[a].at[:, self.z_of(number)]
        return self.core_copy(a, number, whole, whole)

    def first(self, number):
        z = self.z_of(number)
        for a in range(len(self.items)):
            whole = self.accs[a].at[:, z]
            pltpu.make_async_copy(whole, whole, self.local.at[a * 7 + number]).wait()
            self.core_whole(a, number).wait_recv()
            add_into(whole, [self.cores[a].at[:, z]], slice(None))
            for s, plan in zip(self.streams, self.plans):
                if plan[0] == a:
                    s.v_copy(number).start()

    def onward(self, s, number):
        up = number >= CHAIN
        s.chain_step(up, number - (CHAIN - 1) if up else number)

    def second(self, number):
        for s in self.streams:
            s.v_add(number)
            if s.kind == "A":
                s.u_copy(number).start()
            elif number > 0:
                self.onward(s, number)

    def third(self, number):
        for s in self.streams:
            if s.kind == "A":
                s.u_add(number)
                if number > 0:
                    self.onward(s, number)

    def events(self):
        return [
            functools.partial(self.at, number, act)
            for act in (self.first, self.second, self.third)
            for number in NUMBERS
        ]

    def end(self):
        for s in self.streams:
            if s.kind == "B":
                s.chain_end()
                s.u_copy(0).start()
        for s in self.streams:
            if s.kind == "A":
                s.chain_end()
        for s in self.streams:
            if s.kind == "B":
                s.u_add(0)
        p = self.place
        for acc, out in zip(self.accs, self.outs):
            for item in range(out.shape[0]):
                out[item] = acc[item, p.z, p.x, p.y].astype(jnp.float32)

        def last(number):
            for a in range(len(self.items)):
                self.core_whole(a, number).wait_send()
            for s in self.streams:
                s.v_copy(number).wait_send()
                if s.kind == "A" or number == 0:
                    s.u_copy(number).wait_send()
                if number > 0:
                    up = number >= CHAIN
                    s.chain_copy(up, number - (CHAIN - 1) if up else number).wait_send()

        self.each(last)


NUMBERS = (3, 6, 2, 5, 1, 4, 0)


def reduction_parts(groups):
    parts = 8 * CHAIN
    items = [
        [g.reshape(CHAIN, 2, 2, 2, g.shape[0] // parts, g.shape[1]) for g in group] for group in groups
    ]
    shapes = [jax.ShapeDtypeStruct((len(i),) + i[0].shape[-2:], i[0].dtype) for i in items]
    plans = plans_for(shapes)
    count = len(items)
    scratch = [
        pltpu.VMEM((a.shape[0],) + lead + a.shape[-2:], a.dtype)
        for lead in ((CHAIN, 2, 2), (CHAIN, 2, 2), (CHAIN, 2), (CHAIN,), (2, CHAIN - 1, 2))
        for a in shapes
    ]
    sems = pltpu.SemaphoreType.DMA
    scratch += [sems((len(plans), SLOTS))] * 2 + [sems((count * 7,))] * 3
    outs = [jax.ShapeDtypeStruct(a.shape, jnp.float32) for a in shapes]
    return items, plans, scratch, outs


def heads_backward(half, pair, q_ref, k_ref, v_ref, g_ref, qc, kc, t_ref, dq_ref, dk_ref, dv_ref, dt_ref):
    lanes = pl.ds(pl.multiple_of(pair * 128, 128), 128)
    q2, k2, v2, g2 = q_ref[:, lanes], k_ref[:, lanes], v_ref[:, lanes], g_ref[:, lanes]
    size = q2.shape[0]
    allowed = qc == kc
    turn = lax.broadcasted_iota(jnp.int32, (size, size), 0) + lax.broadcasted_iota(
        jnp.int32, (size, size), 1
    )
    flip = (turn == size - 1).astype(jnp.bfloat16)
    made = []
    for h in range(2):
        sl = slice(64 * h, 64 * h + 64)
        q, k, v, g = q2[:, sl], k2[:, sl], v2[:, sl], g2[:, sl]
        p = probs_of(q, k, t_ref[pl.ds(2 * pair + h, 1), :], allowed, half)
        dv = dotf(p.astype(jnp.bfloat16), g, CONTRACT_FIRST)
        dp = dotf(g, v, CONTRACT_LAST)
        ds = (p * (dp - jnp.sum(dp * p, axis=-1, keepdims=True))).astype(jnp.bfloat16)
        dq = jnp.dot(ds, k, preferred_element_type=jnp.float32)
        dk = dotf(ds, q, CONTRACT_FIRST)
        made.append((dq, dk, dv))
        flipped = jnp.dot(flip, ds, preferred_element_type=jnp.float32)
        wide = jnp.concatenate([flipped, jnp.zeros((size, SPAN - size), jnp.float32)], axis=1)
        rolled = pltpu.roll(wide, half - (size - 1), 1, stride=1, stride_axis=0)
        dt_ref[pl.ds(2 * pair + h, 1), :] = jnp.sum(rolled, axis=0, keepdims=True)
    for ref, pieces in zip((dq_ref, dk_ref, dv_ref), zip(*made)):
        ref[:, lanes] = jnp.concatenate(pieces, axis=1).astype(jnp.bfloat16)


def choose(t, starts, acts):
    if len(acts) == 1:
        acts[0]()
        return
    middle = len(acts) // 2

    @pl.when(t < starts[middle])
    def before():
        choose(t, starts[:middle], acts[:middle])

    @pl.when(t >= starts[middle])
    def after():
        choose(t, starts[middle:], acts[middle:])


BACK_TICKS = (
    (0, 1), (2, 3), (4, 5), (6, 7, 8), (9, 10), (11, 12, 13), (14, 15), (16, 17), (18, 19, 20),
)


def backward_kernel(plans, counts, half, *refs):
    refs = list(refs)
    take = lambda n: [refs.pop(0) for unused in range(n)]
    items = [take(n) for n in counts]
    q, k, v, g, first, etable, lengths = take(7)
    weights = take(3)
    outs = take(len(counts))
    dist, normed = take(2)
    grads = take(3)
    bufs = take(5 * len(counts))
    sems = take(5)
    derived = take(3)
    place = Place()
    run = Reduction(place, plans, items, outs, bufs, sems)
    run.begin()
    greet(place)
    run.begin_core()
    size = q.shape[0]

    def segment(axis):
        shape = (size, 1) if axis == 0 else (1, size)
        at = lax.broadcasted_iota(jnp.int32, shape, axis)
        code, end = jnp.zeros(shape, jnp.int32), 0
        for j in range(lengths.shape[1]):
            end = end + lengths[place.y, j]
            code = code + (end <= at).astype(jnp.int32)
        return code

    events = run.events()

    def tick(t, unused):
        def some(numbers):
            for number in numbers:
                events[number]()

        choose(t, list(range(len(BACK_TICKS))), [functools.partial(some, n) for n in BACK_TICKS])

        @pl.when(t < PAIRS)
        def attention():
            heads_backward(half, t, q, k, v, g, segment(0), segment(1), etable, *derived, dist)

        for i in range(3):

            @pl.when(t == PAIRS + i)
            def project():
                grads[i][...] = dotf(first[...], derived[i][...], CONTRACT_FIRST).astype(jnp.bfloat16)
                part = dotf(derived[i][...], weights[i][...], CONTRACT_LAST)
                normed[...] = part if i == 0 else normed[...] + part

        return unused

    lax.fori_loop(0, len(BACK_TICKS), tick, 0)
    run.end()


def reduce_with_attention(groups, q, k, v, g, first, etable, lengths, weights):
    items, plans, scratch, out_shapes = reduction_parts(groups)
    flat = [i for group in items for i in group]
    vmem, hbm = pl.BlockSpec(memory_space=pltpu.VMEM), pl.BlockSpec(memory_space=pltpu.HBM)
    length, width = q.shape
    outs = pl.pallas_call(
        functools.partial(backward_kernel, plans, tuple(len(i) for i in items), length - 1),
        out_shape=out_shapes
        + [
            jax.ShapeDtypeStruct((16, SPAN), jnp.float32),
            jax.ShapeDtypeStruct((length, width), jnp.float32),
        ]
        + [jax.ShapeDtypeStruct((width, width), jnp.bfloat16)] * 3,
        in_specs=[hbm] * len(flat)
        + [vmem] * 6
        + [pl.BlockSpec(memory_space=pltpu.SMEM)]
        + [vmem] * 3,
        out_specs=[vmem] * (len(out_shapes) + 5),
        scratch_shapes=scratch + [pltpu.VMEM((length, width), jnp.bfloat16)] * 3,
        compiler_params=pltpu.CompilerParams(
            collective_id=1, has_side_effects=True, vmem_limit_bytes=62 * 2**20
        ),
    )(*flat, q, k, v, g, first, etable, lengths, *weights)
    count = len(out_shapes)
    return outs[:count], outs[count], outs[count + 1], outs[count + 2 :]


def finish_kernel(plans, counts, *refs):
    refs = list(refs)
    take = lambda n: [refs.pop(0) for unused in range(n)]
    items = [take(n) for n in counts]
    small, halves = take(2)
    outs = take(len(counts))
    total, theirs = take(2)
    bufs = take(5 * len(counts))
    sems = take(5)
    arrived, hop_send, hop_recv, half_send, half_recv = take(5)
    place = Place()
    run = Reduction(place, plans, items, outs, bufs, sems)
    run.begin()
    greet(place, True)
    run.begin_core()
    half = pltpu.make_async_remote_copy(
        src_ref=halves.at[1 - place.y],
        dst_ref=theirs,
        send_sem=half_send.at[0],
        recv_sem=half_recv.at[0],
        device_id=place.device("y"),
        device_id_type=pl.DeviceIdType.MESH,
    )
    half.start()
    total[0] = small[...]

    def hop(number):
        return pltpu.make_async_remote_copy(
            src_ref=total.at[number],
            dst_ref=arrived.at[number],
            send_sem=hop_send.at[number],
            recv_sem=hop_recv.at[number],
            device_id=place.device("cxynf"[number]),
            device_id_type=pl.DeviceIdType.MESH,
        )

    def hopped(number):
        hop(number).wait_recv()
        total[number + 1] = total[number] + arrived[number]

    hop(0).start()
    for number, event in enumerate(run.events()):
        event()
        if number % 4 == 3:
            hopped(number // 4)
            if number // 4 < 4:
                hop(number // 4 + 1).start()
    run.end()
    half.wait_recv()
    half.wait_send()
    for number in range(5):
        hop(number).wait_send()


def reduce_and_finish(groups, small, halves):
    items, plans, scratch, out_shapes = reduction_parts(groups)
    flat = [i for group in items for i in group]
    vmem, hbm = pl.BlockSpec(memory_space=pltpu.VMEM), pl.BlockSpec(memory_space=pltpu.HBM)
    lines = -(-small.shape[0] // 1024) * 8
    padded = jnp.pad(small, (0, lines * 128 - small.shape[0])).reshape(lines, 128)
    sems = pltpu.SemaphoreType.DMA
    outs = pl.pallas_call(
        functools.partial(finish_kernel, plans, tuple(len(i) for i in items)),
        out_shape=out_shapes
        + [
            jax.ShapeDtypeStruct((6, lines, 128), jnp.float32),
            jax.ShapeDtypeStruct(halves.shape[1:], halves.dtype),
        ],
        in_specs=[hbm] * len(flat) + [vmem] * 2,
        out_specs=[vmem] * (len(out_shapes) + 2),
        scratch_shapes=scratch
        + [pltpu.VMEM((5, lines, 128), jnp.float32), sems((5,)), sems((5,)), sems((1,)), sems((1,))],
        compiler_params=pltpu.CompilerParams(
            collective_id=2, has_side_effects=True, vmem_limit_bytes=62 * 2**20
        ),
    )(*flat, padded, halves)
    return outs[:-2], outs[-2][5].reshape(-1)[: small.shape[0]], outs[-1]


class GatherStage:
    def __init__(self, place, streams, items, sems):
        self.place, self.streams, self.items = place, streams, items
        self.core_send, self.core_recv, self.local = sems

    def own_copy(self, k):
        a, own, out = self.items[k]
        p = self.place
        return pltpu.make_async_copy(own, out.at[:, p.z, p.x, p.c, p.y], self.local.at[a])

    def core_copy(self, k, number, arriving):
        a, own, out = self.items[k]
        z = GatherStream.z_of(self.streams[0], number)
        ref = out.at[:, z, :, 1 - self.place.c if arriving else self.place.c]
        return pltpu.make_async_remote_copy(
            src_ref=ref,
            dst_ref=ref,
            send_sem=self.core_send.at[a * 7 + number],
            recv_sem=self.core_recv.at[a * 7 + number],
            device_id=self.place.device("c"),
            device_id_type=pl.DeviceIdType.MESH,
        )

    def start(self):
        for k in range(len(self.items)):
            self.own_copy(k).start()
        for s in self.streams:
            s.u_copy(0).start()
            if s.kind == "A":
                self.chain_start(s)

    def chain_start(self, s):
        for up in (True, False):
            pl.when(s.sends_at(up, 1))(lambda: s.chain_copy(up, 1).start())

    def after_u(self):
        for k in range(len(self.items)):
            self.own_copy(k).wait()
        for s in self.streams:
            s.u_arrival(0).wait_recv()
            if s.kind == "B":
                self.chain_start(s)
            s.v_copy(0).start()

    def arrivals(self, step):
        def arrival(s, up, number):
            s.chain_arrival(up, step).wait_recv()
            if step < CHAIN - 1:
                pl.when(s.sends_at(up, step + 1))(lambda: s.chain_copy(up, step + 1).start())
            if s.kind == "A":
                s.u_copy(number).start()
            else:
                s.v_copy(number).start()

        for s in self.streams:
            each_arrival(s, step, functools.partial(arrival, s))

    def sides(self, step):
        def side(s, up, number):
            s.u_arrival(number).wait_recv()
            s.v_copy(number).start()

        for s in self.streams:
            if s.kind == "A":
                each_arrival(s, step, functools.partial(side, s))

    def finish(self, number):
        for s in self.streams:
            s.v_arrival(number).wait_recv()
        for k in range(len(self.items)):
            self.core_copy(k, number, False).start()

    def finishes(self, step):
        each_arrival(self.streams[0], step, lambda up, number: self.finish(number))

    def last(self):
        def one(up, number):
            for k in range(len(self.items)):
                self.core_copy(k, number, True).wait_recv()

        one(True, 0)
        for step in range(1, CHAIN):
            each_arrival(self.streams[0], step, one)

    def events(self):
        steps = range(1, CHAIN)
        moves = [
            act
            for step in steps
            for act in (functools.partial(self.arrivals, step), functools.partial(self.sides, step))
        ]
        ends = [functools.partial(self.finishes, step) for step in steps]
        return [self.start, self.after_u] + moves + [lambda: self.finish(0)] + ends + [self.last]

    def sent(self):
        def one(up, number):
            for k in range(len(self.items)):
                self.core_copy(k, number, False).wait_send()
            for s in self.streams:
                if s.kind == "A":
                    s.u_copy(number).wait_send()
                s.v_copy(number).wait_send()

        one(True, 0)
        for s in self.streams:
            if s.kind == "B":
                s.u_copy(0).wait_send()
            for step in range(1, CHAIN):
                for up in (True, False):
                    pl.when(s.sends_at(up, step))(lambda: s.chain_copy(up, step).wait_send())
        for step in range(1, CHAIN):
            each_arrival(self.streams[0], step, one)


class Weights(NamedTuple):
    eq: jax.Array
    ek: jax.Array
    ev: jax.Array
    eo: jax.Array
    ew: jax.Array
    en: jax.Array
    dq: jax.Array
    dk: jax.Array
    dv: jax.Array
    do: jax.Array
    cq: jax.Array
    ck: jax.Array
    cv: jax.Array
    co: jax.Array
    dw: jax.Array
    dn: jax.Array


class Rows(NamedTuple):
    x: jax.Array
    first: jax.Array
    q: jax.Array
    k: jax.Array
    v: jax.Array
    attended: jax.Array
    middle: jax.Array
    second: jax.Array
    output: jax.Array
    memory: jax.Array
    ck: jax.Array
    cv: jax.Array
    cotangent: jax.Array
    target: jax.Array
    own: jax.Array
    sq: jax.Array
    sk: jax.Array
    sv: jax.Array
    sattended: jax.Array
    tmiddle: jax.Array
    cross: jax.Array
    cq: jax.Array
    cattended: jax.Array
    crossed: jax.Array
    third: jax.Array
    doutput: jax.Array
    tcotangent: jax.Array


ROW_KINDS = (
    (True, False),
    (True, False),
    (True, False),
    (True, False),
    (True, False),
    (True, False),
    (True, True),
    (True, False),
    (True, True),
    (True, False),
    (True, False),
    (True, False),
    (True, False),
    (False, False),
    (False, False),
    (False, False),
    (False, False),
    (False, False),
    (False, False),
    (False, True),
    (False, False),
    (False, False),
    (False, False),
    (False, True),
    (False, False),
    (False, True),
    (False, False),
)
GROUP_ARRAYS = ((0, 1), (2, 3), (4,), (5, 6))
(
    TABLES, BEGIN, QKV, ATTEND, JOIN, FFN, CLOSE, SELF, SELF_ATTEND, CROSS, CROSS_ATTEND, CROSSED,
    DFFN, DCLOSE,
) = range(14)
TICKS = (
    (TABLES, ((0, 0),)),
    (BEGIN, (
        (0, 1), (0, 2), (0, 3), (0, 4), (1, 0), (1, 1), (0, 5), (0, 6), (0, 7), (0, 8), (0, 9),
        (1, 2), (0, 10), (0, 11), (1, 3), (0, 12),
    )),
    (QKV, ()),
    (ATTEND, ((1, 4),)),
    (ATTEND, ((2, 0), (2, 1), (1, 5))),
    (ATTEND, ((1, 6),)),
    (ATTEND, ((1, 7),)),
    (ATTEND, ((2, 2), (1, 8), (1, 9))),
    (ATTEND, ((2, 3), (1, 10))),
    (JOIN, ((1, 11), (2, 4), (3, 0), (3, 1), (1, 12))),
    (FFN, ((2, 5),)),
    (FFN, ((2, 6),)),
    (FFN, ((2, 7),)),
    (FFN, ((3, 2), (2, 8), (2, 9))),
    (CLOSE, ((3, 3), (2, 10))),
    (SELF, ((3, 4), (2, 11), (2, 12))),
    (SELF_ATTEND, ((3, 5),)),
    (CROSS, ((3, 6),)),
    (CROSS_ATTEND, ((3, 7), (3, 8))),
    (CROSS_ATTEND, ((3, 9),)),
    (CROSSED, ((3, 10),)),
    (DFFN, ((3, 11), (3, 12))),
    (DFFN, ()), (DFFN, ()), (DFFN, ()),
    (DCLOSE, ()),
)


def first_of(kind):
    return [k for k, unused in TICKS].index(kind)


def load_blocks(src, items, landing, sem, dst):
    height, width = landing.shape[-2:]
    copy = pltpu.make_async_copy(src.at[items], landing, sem)
    copy.start()
    copy.wait()

    def one(flat, unused):
        z, x, c = flat // 4, (flat // 2) % 2, flat % 2
        rows = pl.ds(pl.multiple_of(flat * 2 * height, 2 * height), 2 * height)
        for item in range(landing.shape[0]):
            pair = [landing[item, z, x, c, y].astype(jnp.float32) for y in range(2)]
            dst[item, rows] = jnp.concatenate(pair, axis=0).astype(dst.dtype)
        return unused

    lax.fori_loop(0, 4 * CHAIN, one, 0)


def matmul(left, right):
    return jnp.dot(left, right, preferred_element_type=jnp.float32)


def low(values):
    return values.astype(jnp.bfloat16)


def rms_of(values, gain):
    return (
        values * lax.rsqrt(jnp.mean(values * values, axis=-1, keepdims=True) + EPSILON) * gain
    )


def heads_forward(mode, half, pair, q_ref, k_ref, v_ref, o_ref, qc, kc, t_ref):
    lanes = pl.ds(pl.multiple_of(pair * 128, 128), 128)
    q2, k2, v2 = q_ref[:, lanes], k_ref[:, lanes], v_ref[:, lanes]
    allowed = allowed_of(mode, qc, kc, (q2.shape[0], k2.shape[0]))
    mixed = []
    for h in range(2):
        sl = slice(64 * h, 64 * h + 64)
        row = None if t_ref is None else t_ref[pl.ds(2 * pair + h, 1), :]
        p = probs_of(q2[:, sl], k2[:, sl], row, allowed, half)
        mixed.append(matmul(low(p), v2[:, sl]))
    o_ref[:, lanes] = low(jnp.concatenate(mixed, axis=1))


def forward_kernel(plans, *refs):
    refs = list(refs)
    take = lambda n: [refs.pop(0) for unused in range(n)]
    shards = Weights(*take(16))
    tile, halves_x, halves_t, halves_c, halves_tc = take(5)
    lengths, target_lengths, buckets, etable_in, dtable_in = take(5)
    w_sq, w_wide, w_narrow, w_dsq, w_dwide, w_dnarrow = take(6)
    row = Rows(*take(len(ROW_KINDS)))
    gains, etable, dtable, sums, pre_hbm, act_hbm, dpre, dact = take(8)
    stack_e, stack_d, stack_w, stack_dw, gbuf, branch, dbranch = take(7)
    send, recv, core_send, core_recv, local, load_sem, store_sem, swap_send, swap_recv = take(9)
    sq, wide, narrow, dwide, landing, pre, act = take(7)
    place = Place()
    mine = place.y
    half = row.x.shape[0] - 1

    for i in range(4):
        stack_e[i] = shards[i][...]
    for i in range(8):
        stack_d[i] = shards[6 + i][...]
    for j in range(4):
        columns = slice(j * stack_w.shape[2], (j + 1) * stack_w.shape[2])
        stack_w[j] = shards.ew[:, columns]
        stack_dw[j] = shards.dw[:, columns]
    owns = [stack_e, tile, stack_w, shards.en, stack_d, stack_dw, shards.dn]
    hbm = [w_sq, None, w_wide, w_narrow, w_dsq, w_dwide, w_dnarrow]
    full = [gbuf if out is None else out for out in hbm]
    stages = []
    for group in GROUP_ARRAYS:
        streams = [
            GatherStream(place, owns[a], full[a], third, kind, u, v, send.at[i], recv.at[i])
            for i, (a, third, kind, u, v) in enumerate(plans)
            if a in group
        ]
        items = [(a, owns[a], full[a]) for a in group]
        stages.append(GatherStage(place, streams, items, (core_send, core_recv, local)))

    def half_copy(number, halves, whole):
        size = halves.shape[1]
        return pltpu.make_async_remote_copy(
            src_ref=halves.at[1 - mine],
            dst_ref=whole.at[pl.ds(pl.multiple_of(mine * size, 64), size)],
            send_sem=swap_send.at[number],
            recv_sem=swap_recv.at[number],
            device_id=place.device("y"),
            device_id_type=pl.DeviceIdType.MESH,
        )

    swaps = [
        half_copy(0, halves_x, row.x),
        half_copy(1, halves_t, row.target),
        half_copy(2, halves_c, row.cotangent),
        half_copy(3, halves_tc, row.tcotangent),
    ]
    for halves, whole in (
        (halves_x, row.x),
        (halves_t, row.target),
        (halves_c, row.cotangent),
        (halves_tc, row.tcotangent),
    ):
        size = halves.shape[1]
        whole[pl.ds(pl.multiple_of(mine * size, 64), size)] = halves[mine]
    greet(place)

    count = lengths.shape[1]
    ends, total = [], 0
    for j in range(count):
        total = total + lengths[mine, j]
        ends.append(total)
    target_length = target_lengths[mine, 0]

    def codes(size, axis):
        shape = (size, 1) if axis == 0 else (1, size)
        at = lax.broadcasted_iota(jnp.int32, shape, axis)
        segment = jnp.zeros(shape, jnp.int32)
        for end in ends:
            segment = segment + (end <= at).astype(jnp.int32)
        return at, segment

    length, target_count = row.x.shape[0], row.target.shape[0]

    def mean_parts(kept, first, second, rows):
        keep = lax.broadcasted_iota(jnp.int32, (first.shape[0], 1), 0) < kept
        for i, value in enumerate((first, second)):
            total_square = jnp.sum(jnp.where(keep, value * value, 0.0))
            sums[rows + i : rows + i + 1, :] = jnp.full((1, 128), total_square, jnp.float32)
        sums[rows // 2 + 4 : rows // 2 + 5, :] = jnp.full((1, 128), kept.astype(jnp.float32))

    def load_narrow(src):
        return [
            pltpu.make_async_copy(
                src.at[0, z, x, c, y],
                narrow.at[pl.ds((((z * 2 + x) * 2 + c) * 2 + y) * src.shape[5], src.shape[5])],
                load_sem.at[0],
            )
            for z in range(CHAIN)
            for x in range(2)
            for c in range(2)
            for y in range(2)
        ]

    def narrow_loaded():
        pltpu.make_async_copy(narrow, narrow, load_sem.at[0]).wait()

    chunk = row.x.shape[1]
    chunks = wide.shape[0]

    def store(j, slot):
        columns = pl.ds(pl.multiple_of(j * chunk, 128), chunk)
        return (
            pltpu.make_async_copy(pre.at[slot], pre_hbm.at[:, columns], store_sem.at[0, slot]),
            pltpu.make_async_copy(act.at[slot], act_hbm.at[:, columns], store_sem.at[1, slot]),
        )

    def tick(t, unused):
        pieces = {}

        def at_tick(kind):
            def keep(act):
                pieces[kind] = act
                return act

            return keep

        def comm(events):
            for stage, number in events:
                stages[stage].events()[number]()

        choose(
            t, list(range(len(TICKS))), [functools.partial(comm, events) for unused, events in TICKS]
        )

        @at_tick(TABLES)
        def tables():
            swaps[0].start()
            swaps[1].start()
            for table_in, table in ((etable_in, etable), (dtable_in, dtable)):
                value = jnp.zeros(table.shape, jnp.float32)
                for b in range(BUCKETS):
                    value = value + jnp.where(buckets[...] == b, table_in[:, b : b + 1], 0.0)
                table[...] = value

        @at_tick(BEGIN)
        def begin():
            load_blocks(w_sq, slice(0, 4), landing, load_sem.at[1], sq)
            tiles = gbuf.at[0]
            value = jnp.zeros(gains.shape, jnp.float32)
            share = gains.shape[1] // (8 * CHAIN)
            for d in range(8 * CHAIN):
                z, x, c, y = d // 8, (d // 4) % 2, (d // 2) % 2, d % 2
                part = tiles[z, x, c, y].astype(jnp.float32)
                spread = jnp.concatenate(
                    [part, jnp.zeros((8, gains.shape[1] - 128), jnp.float32)], axis=1
                )
                value = value + (pltpu.roll(spread, share * d, 1) if d else spread)
            gains[...] = value
            swaps[0].wait_recv()
            swaps[1].wait_recv()
            row.first[...] = low(rms_of(row.x[...].astype(jnp.float32), value[0:1, :]))

        @at_tick(QKV)
        def project():
            for i, ref in enumerate((row.q, row.k, row.v)):
                ref[...] = low(matmul(row.first[...], sq[i]))

        @at_tick(ATTEND)
        def attention():
            heads_forward(
                "segment", half, t - first_of(ATTEND), row.q, row.k, row.v, row.attended,
                codes(length, 0)[1], codes(length, 1)[1], etable,
            )

        @at_tick(JOIN)
        def join():
            for copy in load_narrow(w_narrow):
                copy.start()
            value = row.x[...].astype(jnp.float32) + matmul(row.attended[...], sq[3])
            row.middle[...] = value
            row.second[...] = low(rms_of(value, gains[1:2, :]))
            load_blocks(w_wide, slice(0, 4), landing, load_sem.at[1], wide)
            narrow_loaded()

        @at_tick(FFN)
        def feedforward():
            j = t - first_of(FFN)
            slot = lax.rem(j, 2)

            @pl.when(j >= 2)
            def stored():
                for copy in store(j - 2, slot):
                    copy.wait()

            columns = pl.ds(pl.multiple_of(j * chunk, 128), chunk)
            value = matmul(row.second[...], wide[j])
            active = low(jax.nn.gelu(value, approximate=True))
            pre[slot] = value
            act[slot] = active
            for copy in store(j, slot):
                copy.start()
            part = matmul(active, narrow[columns, :])

            @pl.when(j == 0)
            def first_part():
                branch[...] = part

            @pl.when(j > 0)
            def more():
                branch[...] = branch[...] + part

        @at_tick(CLOSE)
        def close():
            value = row.middle[...] + branch[...]
            row.output[...] = value
            row.memory[...] = low(rms_of(value, gains[2:3, :]))
            mean_parts(total, value, branch[...], 0)
            swaps[2].start()
            swaps[3].start()
            for j in (chunks - 2, chunks - 1):
                for copy in store(j, j % 2):
                    copy.wait()

        @at_tick(SELF)
        def self_project():
            load_blocks(w_dsq, slice(0, 4), landing, load_sem.at[1], sq)
            load_blocks(w_dsq, slice(4, 8), landing, load_sem.at[1], wide)
            normed = low(rms_of(row.target[...].astype(jnp.float32), gains[3:4, :]))
            row.own[...] = normed
            for i, ref in enumerate((row.sq, row.sk, row.sv)):
                ref[...] = low(matmul(normed, sq[i]))
            row.ck[...] = low(matmul(row.memory[...], wide[1]))
            row.cv[...] = low(matmul(row.memory[...], wide[2]))

        def valid_code(size, axis, limit):
            return (codes(size, axis)[0] < limit).astype(jnp.int32)

        @at_tick(SELF_ATTEND)
        def self_attention():
            def one(pair, unused):
                heads_forward(
                    "causal", half, pair, row.sq, row.sk, row.sv, row.sattended,
                    valid_code(target_count, 0, target_length),
                    valid_code(target_count, 1, target_length), dtable,
                )
                return unused

            lax.fori_loop(0, PAIRS, one, 0)

        @at_tick(CROSS)
        def self_join():
            value = row.target[...].astype(jnp.float32) + matmul(row.sattended[...], sq[3])
            row.tmiddle[...] = value
            normed = low(rms_of(value, gains[4:5, :]))
            row.cross[...] = normed
            row.cq[...] = low(matmul(normed, wide[0]))

        @at_tick(CROSS_ATTEND)
        def cross_attention():
            def one(pair, unused):
                heads_forward(
                    "cross", half, pair, row.cq, row.ck, row.cv, row.cattended,
                    valid_code(target_count, 0, target_length), valid_code(length, 1, total), None,
                )
                return unused

            begin_pair = (t - first_of(CROSS_ATTEND)) * (PAIRS // 2)
            lax.fori_loop(begin_pair, begin_pair + PAIRS // 2, one, 0)

        @at_tick(CROSSED)
        def cross_join():
            value = row.tmiddle[...] + matmul(row.cattended[...], wide[3])
            row.crossed[...] = value
            row.third[...] = low(rms_of(value, gains[5:6, :]))

        @at_tick(DFFN)
        def decoder_feedforward():
            j = t - first_of(DFFN)

            @pl.when(j == 0)
            def decoder_load():
                for copy in load_narrow(w_dnarrow):
                    copy.start()
                load_blocks(w_dwide, slice(0, 4), landing, load_sem.at[1], dwide)
                narrow_loaded()

            columns = pl.ds(pl.multiple_of(j * chunk, 128), chunk)
            value = matmul(row.third[...], dwide[j])
            active = low(jax.nn.gelu(value, approximate=True))
            dpre[:, columns] = value
            dact[:, columns] = active
            part = matmul(active, narrow[columns, :])

            @pl.when(j == 0)
            def first_part():
                dbranch[...] = part

            @pl.when(j > 0)
            def more():
                dbranch[...] = dbranch[...] + part

        @at_tick(DCLOSE)
        def decoder_close():
            value = row.crossed[...] + dbranch[...]
            row.doutput[...] = value
            mean_parts(target_length, value, dbranch[...], 2)

        kinds = range(DCLOSE + 1)
        choose(t, [first_of(kind) for kind in kinds], [pieces[kind] for kind in kinds])
        return unused

    lax.fori_loop(0, len(TICKS), tick, 0)
    swaps[2].wait_recv()
    swaps[3].wait_recv()
    for copy in swaps:
        copy.wait_send()
    for stage in stages:
        stage.sent()


def forward(shards, tile, x, t, c, tc, lengths, target_lengths, buckets, etable, dtable):
    bf, f32 = jnp.bfloat16, jnp.float32
    sems = pltpu.SemaphoreType.DMA
    length, target_count, width = 2 * x.shape[1], 2 * t.shape[1], x.shape[2]
    height, hidden = shards.ew.shape
    fake = lambda *s: jax.ShapeDtypeStruct(s, bf)
    arrays = [
        fake(4, height, width), tile, fake(4, height, width), fake(1, hidden // (8 * CHAIN), width),
        fake(8, height, width), fake(4, height, width), fake(1, hidden // (8 * CHAIN), width),
    ]
    plans = plans_for(arrays)
    shape = lambda s, kind: jax.ShapeDtypeStruct(s, kind)
    rows = [
        shape((length if encoder else target_count, width), f32 if exact else bf)
        for encoder, exact in ROW_KINDS
    ]
    gathered = [
        shape((a.shape[0], CHAIN, 2, 2, 2) + a.shape[1:], bf)
        for i, a in enumerate(arrays)
        if i != 1
    ]
    more = [
        shape((8, width), f32), shape((16, SPAN), f32), shape((16, SPAN), f32), shape((8, 128), f32),
        shape((length, hidden), f32), shape((length, hidden), bf),
        shape((target_count, hidden), f32), shape((target_count, hidden), bf),
    ]
    vmem, hbm = pl.BlockSpec(memory_space=pltpu.VMEM), pl.BlockSpec(memory_space=pltpu.HBM)
    smem = pl.BlockSpec(memory_space=pltpu.SMEM)
    count = len(arrays)
    ordered = shards._replace(en=shards.en[None], dn=shards.dn[None])
    outs = pl.pallas_call(
        functools.partial(forward_kernel, plans),
        out_shape=gathered + rows + more,
        in_specs=[vmem] * 21 + [smem] * 2 + [vmem] * 3,
        out_specs=[hbm] * 6 + [vmem] * len(rows) + [vmem] * 4 + [hbm] * 2 + [vmem] * 2,
        scratch_shapes=[
            pltpu.VMEM((4, height, width), bf),
            pltpu.VMEM((8, height, width), bf),
            pltpu.VMEM((4, height, width), bf),
            pltpu.VMEM((4, height, width), bf),
            pltpu.VMEM((1, CHAIN, 2, 2, 2, 8, 128), bf),
            pltpu.VMEM((length, width), f32),
            pltpu.VMEM((target_count, width), f32),
            sems((len(plans), SLOTS)),
            sems((len(plans), SLOTS)),
            sems((count * 7,)),
            sems((count * 7,)),
            sems((count,)),
            sems((6,)),
            sems((2, 2)),
            sems((4,)),
            sems((4,)),
            pltpu.VMEM((4, width, width), bf),
            pltpu.VMEM((4, width, width), bf),
            pltpu.VMEM((hidden, width), bf),
            pltpu.VMEM((4, width, width), bf),
            pltpu.VMEM((4, CHAIN, 2, 2, 2, height, width), bf),
            pltpu.VMEM((2, length, width), f32),
            pltpu.VMEM((2, length, width), bf),
        ],
        compiler_params=pltpu.CompilerParams(
            collective_id=0, has_side_effects=True, vmem_limit_bytes=62 * 2**20
        ),
    )(*ordered, tile, x, t, c, tc, lengths, target_lengths, buckets, etable, dtable)
    whole = [o.reshape(o.shape[0], -1, o.shape[-1]) for o in outs[:6]]
    joined = [jnp.concatenate([whole[at][j] for j in range(4)], axis=1) for at in (1, 4)]
    weights = Weights(
        *[whole[0][i] for i in range(4)], joined[0], whole[2][0],
        *[whole[3][i] for i in range(8)], joined[1], whole[5][0],
    )
    rows_out = Rows(*outs[6 : 6 + len(rows)])
    gains, etable, dtable, sums, pre, act, dpre, dact = outs[6 + len(rows) :]
    kept = SimpleNamespace(
        **rows_out._asdict(), gains=gains, etable=etable, dtable=dtable, sums=sums, pre=pre, act=act,
        dpre=dpre, dact=dact,
    )
    return weights, kept


def whole_row(halves):
    mine = lax.axis_index("seq")
    keep = lax.dynamic_index_in_dim(halves, mine, 0, keepdims=False)
    other = lax.ppermute(
        lax.dynamic_index_in_dim(halves, 1 - mine, 0, keepdims=False), "seq", [(0, 1), (1, 0)]
    )
    first = jnp.where(mine == 0, keep, other)
    second = jnp.where(mine == 0, other, keep)
    return jnp.concatenate([first, second], axis=0)


def own_slots(row):
    mine = lax.axis_index("seq")
    half = row.shape[0] // 2
    sent = lax.dynamic_slice_in_dim(row, (1 - mine) * half, half, 0).astype(jnp.bfloat16)
    return placed_slots(row, lax.ppermute(sent, "seq", [(0, 1), (1, 0)]))


def placed_slots(row, other):
    mine = lax.axis_index("seq")
    half = row.shape[0] // 2
    keep = lax.dynamic_slice_in_dim(row, mine * half, half, 0)
    other = other.astype(row.dtype)
    return jnp.stack([jnp.where(mine == 0, keep, other), jnp.where(mine == 0, other, keep)])


def matmul_back(grads, weight):
    return dotf(grads, weight, CONTRACT_LAST)


def weight_grad(inputs, grads):
    return dotf(inputs, grads, CONTRACT_FIRST).astype(jnp.bfloat16)


def rms_scale(values, gain_vec):
    return (
        values * lax.rsqrt(jnp.mean(values * values, axis=-1, keepdims=True) + EPSILON) * gain_vec
    )


def gelu_float(values):
    return jax.nn.gelu(values, approximate=True)


def norm_back(values, gain_vec, upstream):
    unused_value, pullback = jax.vjp(rms_scale, values, gain_vec)
    return pullback(upstream)


def feedforward_back(near, normed, pre_values, active, widen, narrow, upstream):
    branch_low = low(upstream)
    narrow_grad = weight_grad(active, branch_low)
    active_grad = matmul_back(branch_low, narrow)
    unused_value, gelu_pull = jax.vjp(gelu_float, pre_values)
    pre_low = low(gelu_pull(active_grad)[0])
    if near:
        chunk = widen.shape[1] // 4
        widen_grad = [weight_grad(normed, pre_low[:, j * chunk : (j + 1) * chunk]) for j in range(4)]
    else:
        widen_grad = weight_grad(normed, pre_low)
    return (matmul_back(pre_low, widen), widen_grad, narrow_grad)


def selector_of(buckets):
    ids = jnp.arange(BUCKETS, dtype=jnp.int32)
    return (buckets[:, None] == ids[None, :]).astype(jnp.float32)


def distance_table(table_in, buckets):
    by_distance = jnp.einsum(
        "db,bh->hd", selector_of(buckets), table_in, precision=HIGHEST_PRECISION
    )
    return jnp.pad(by_distance, ((0, 4), (0, SPAN - by_distance.shape[1])))


def by_pair(table):
    return table[:HEADS].reshape(PAIRS, 2, SPAN)


def table_grad(selector, by_distance):
    flat = by_distance.reshape(-1, SPAN)[:HEADS, : selector.shape[0]]
    return jnp.einsum("db,hd->bh", selector, flat, precision=HIGHEST_PRECISION)


def forward_plain(w, gains, x, t, c, tc, lengths_row, target_length, buckets, encoder_table_in, decoder_table_in):
    kept = SimpleNamespace(x=x, target=t, cotangent=c, tcotangent=tc)
    half = x.shape[0] - 1
    encoder_codes, self_codes, cross_codes, valid, target_valid = row_codes(
        lengths_row, target_length, x.shape[0], t.shape[0]
    )
    etable = distance_table(encoder_table_in, buckets)
    dtable = distance_table(decoder_table_in, buckets)
    gain = [gains[i] for i in range(6)]
    residual = x.astype(jnp.float32)
    kept.first = low(rms_scale(residual, gain[0]))
    kept.q, kept.k, kept.v = [low(matmul(kept.first, weight)) for weight in (w.eq, w.ek, w.ev)]
    kept.attended = attn_fwd(
        "segment", half, kept.q, kept.k, kept.v, *encoder_codes, by_pair(etable)
    )
    kept.middle = residual + matmul(kept.attended, w.eo)
    kept.second = low(rms_scale(kept.middle, gain[1]))
    kept.pre = matmul(kept.second, w.ew)
    kept.act = low(gelu_float(kept.pre))
    branch = matmul(kept.act, w.en)
    kept.output = kept.middle + branch
    kept.memory = low(rms_scale(kept.output, gain[2]))
    target = t.astype(jnp.float32)
    kept.own = low(rms_scale(target, gain[3]))
    kept.sq, kept.sk, kept.sv = [low(matmul(kept.own, weight)) for weight in (w.dq, w.dk, w.dv)]
    kept.sattended = attn_fwd(
        "causal", half, kept.sq, kept.sk, kept.sv, *self_codes, by_pair(dtable)
    )
    kept.tmiddle = target + matmul(kept.sattended, w.do)
    kept.cross = low(rms_scale(kept.tmiddle, gain[4]))
    kept.cq = low(matmul(kept.cross, w.cq))
    kept.ck = low(matmul(kept.memory, w.ck))
    kept.cv = low(matmul(kept.memory, w.cv))
    kept.cattended = attn_fwd(
        "cross", half, kept.cq, kept.ck, kept.cv, *cross_codes, None
    )
    kept.crossed = kept.tmiddle + matmul(kept.cattended, w.co)
    kept.third = low(rms_scale(kept.crossed, gain[5]))
    kept.dpre = matmul(kept.third, w.dw)
    kept.dact = low(gelu_float(kept.dpre))
    decoder_branch = matmul(kept.dact, w.dn)
    kept.doutput = kept.crossed + decoder_branch
    kept.gains, kept.etable, kept.dtable = gains, etable, dtable
    keep, target_keep = valid[:, None], target_valid[:, None]
    sums = jnp.stack(
        [
            jnp.sum(jnp.where(keep, kept.output * kept.output, 0.0)),
            jnp.sum(jnp.where(keep, branch * branch, 0.0)),
            jnp.sum(jnp.where(target_keep, kept.doutput * kept.doutput, 0.0)),
            jnp.sum(jnp.where(target_keep, decoder_branch * decoder_branch, 0.0)),
            jnp.sum(valid.astype(jnp.float32)),
            jnp.sum(target_valid.astype(jnp.float32)),
        ]
    )
    kept.sums = sums[:, None]
    return kept


def row_codes(lengths_row, target_length, encoder_length, decoder_length):
    positions = jnp.arange(encoder_length, dtype=jnp.int32)
    target_positions = jnp.arange(decoder_length, dtype=jnp.int32)
    order = jnp.arange(lengths_row.shape[0], dtype=jnp.int32)
    ends = jnp.sum(jnp.where(order[None, :] <= order[:, None], lengths_row[None, :], 0), axis=1)
    segment = jnp.sum((ends[None, :] <= positions[:, None]).astype(jnp.int32), axis=1)
    valid = positions < jnp.sum(lengths_row)
    target_valid = target_positions < target_length
    column = lambda code: code.astype(jnp.int32)[:, None]
    line = lambda code: code.astype(jnp.int32)[None, :]
    return (
        (column(segment), line(segment)),
        (column(target_valid), line(target_valid)),
        (column(target_valid), line(valid)),
        valid,
        target_valid,
    )


def backward(near, w, kept, lengths_row, target_length, buckets, all_lengths):
    half = kept.x.shape[0] - 1
    encoder_codes, self_codes, cross_codes, unused_valid, unused_target = row_codes(
        lengths_row, target_length, kept.x.shape[0], kept.target.shape[0]
    )
    selector = selector_of(buckets)
    encoder_table, decoder_table = by_pair(kept.etable), by_pair(kept.dtable)
    first_gain, second_gain, final_gain, self_gain, cross_gain, third_gain = [
        kept.gains[i] for i in range(6)
    ]
    residual, target = kept.x.astype(jnp.float32), kept.target.astype(jnp.float32)
    first_normed, second_normed = kept.first, kept.second
    queries, keys, values, attended = kept.q, kept.k, kept.v, kept.attended
    middle, output, memory, pre, active = (
        kept.middle, kept.output, kept.memory, kept.pre, kept.act
    )
    self_normed, cross_normed, third_normed = kept.own, kept.cross, kept.third
    self_queries, self_keys, self_values = kept.sq, kept.sk, kept.sv
    cross_queries, cross_keys, cross_values = kept.cq, kept.ck, kept.cv
    self_attended, cross_attended = kept.sattended, kept.cattended
    target_middle, crossed = kept.tmiddle, kept.crossed
    decoder_pre, decoder_active = kept.dpre, kept.dact
    encoder_cotangent, decoder_cotangent = kept.cotangent, kept.tcotangent
    grads = SimpleNamespace()
    upstream = decoder_cotangent.astype(jnp.float32)
    normed_grad, grads.dw, grads.dn = feedforward_back(
        near, third_normed, decoder_pre, decoder_active, w.dw, w.dn, upstream
    )
    part, third_gain_grad = norm_back(crossed, third_gain, normed_grad)
    crossed_grad = upstream + part

    crossed_low = low(crossed_grad)
    grads.co = weight_grad(cross_attended, crossed_low)
    mixed_grad = low(matmul_back(crossed_low, w.co))
    query_low, key_low, value_low = attn_bwd(
        "cross", half, cross_queries, cross_keys, cross_values, mixed_grad, *cross_codes, None
    )
    grads.cq = weight_grad(cross_normed, query_low)
    grads.ck = weight_grad(memory, key_low)
    grads.cv = weight_grad(memory, value_low)
    memory_grad = matmul_back(key_low, w.ck) + matmul_back(value_low, w.cv)
    part, cross_gain_grad = norm_back(target_middle, cross_gain, matmul_back(query_low, w.cq))
    middle_grad = crossed_grad + part

    middle_low = low(middle_grad)
    grads.do = weight_grad(self_attended, middle_low)
    mixed_grad = low(matmul_back(middle_low, w.do))
    query_low, key_low, value_low, decoder_distance = attn_bwd(
        "causal", half, self_queries, self_keys, self_values, mixed_grad, *self_codes, decoder_table
    )
    grads.dq = weight_grad(self_normed, query_low)
    grads.dk = weight_grad(self_normed, key_low)
    grads.dv = weight_grad(self_normed, value_low)
    normed_grad = (
        matmul_back(query_low, w.dq)
        + matmul_back(key_low, w.dk)
        + matmul_back(value_low, w.dv)
    )
    part, self_gain_grad = norm_back(target, self_gain, normed_grad)
    decoder_input_grad = middle_grad + part

    part, final_gain_grad = norm_back(output, final_gain, memory_grad)
    output_grad = encoder_cotangent.astype(jnp.float32) + part
    normed_grad, grads.ew, grads.en = feedforward_back(
        near, second_normed, pre, active, w.ew, w.en, output_grad
    )
    part, second_gain_grad = norm_back(middle, second_gain, normed_grad)
    encoder_middle_grad = output_grad + part

    middle_low = low(encoder_middle_grad)
    grads.eo = weight_grad(attended, middle_low)
    mixed_grad = low(matmul_back(middle_low, w.eo))
    reduced = None
    if near:
        made, encoder_distance, normed_grad, weight_grads = reduce_with_attention(
            decoder_groups(grads), queries, keys, values, mixed_grad, first_normed, kept.etable,
            all_lengths, (w.eq, w.ek, w.ev),
        )
        reduced = unpack(made)
        grads.eq, grads.ek, grads.ev = weight_grads
    else:
        query_low, key_low, value_low, encoder_distance = attn_bwd(
            "segment", half, queries, keys, values, mixed_grad, *encoder_codes, encoder_table
        )
        grads.eq = weight_grad(first_normed, query_low)
        grads.ek = weight_grad(first_normed, key_low)
        grads.ev = weight_grad(first_normed, value_low)
        normed_grad = (
            matmul_back(query_low, w.eq)
            + matmul_back(key_low, w.ek)
            + matmul_back(value_low, w.ev)
        )
    part, first_gain_grad = norm_back(residual, first_gain, normed_grad)
    encoder_input_grad = encoder_middle_grad + part

    small = jnp.concatenate(
        [
            first_gain_grad,
            second_gain_grad,
            final_gain_grad,
            self_gain_grad,
            cross_gain_grad,
            third_gain_grad,
            table_grad(selector, encoder_distance).reshape(-1),
            table_grad(selector, decoder_distance).reshape(-1),
            kept.sums[:6, 0],
        ]
    )
    return (output, kept.doutput, encoder_input_grad, decoder_input_grad, grads, small, reduced)


def decoder_groups(g):
    squares = [g.dq, g.dk, g.dv, g.do, g.cq, g.ck, g.cv, g.co]
    return [squares, list(g.dw), [g.dn]]


def unpack(made):
    squares, wide, narrow = made
    return list(squares) + [jnp.concatenate([wide[j] for j in range(4)], axis=1), narrow[0]]


WEIGHT_ARGS = (6, 7, 8, 9, 12, 13, 16, 17, 18, 19, 22, 23, 24, 25, 27, 28)
GAIN_ARGS = (5, 11, 14, 15, 21, 26)
WEIGHT_OUTS = (5, 6, 7, 8, 11, 12, 15, 16, 17, 18, 21, 22, 23, 24, 26, 27)
GAIN_OUTS = (4, 10, 13, 14, 20, 25)


def body(near, *args):
    row_count = lax.axis_size("rows") * lax.axis_size("seq")
    me = lax.axis_index("rows") * lax.axis_size("seq") + lax.axis_index("seq")
    seq_index = lax.axis_index("seq")
    shards = Weights(*[args[i] for i in WEIGHT_ARGS])
    own_gains = jnp.stack([args[i] for i in GAIN_ARGS])
    lengths_row = lax.dynamic_index_in_dim(args[2], seq_index, 0, keepdims=False)
    target_length = lax.dynamic_index_in_dim(args[3], seq_index, 0, keepdims=False)
    if near:
        tile = jnp.pad(own_gains, ((0, 2), (0, 128 - own_gains.shape[1])))[None]
        tables = [jnp.pad(args[i].T, ((0, 4), (0, 0))) for i in (10, 20)]
        line = jnp.pad(args[4], (0, SPAN - args[4].shape[0]), constant_values=-1)[None]
        weights, kept = forward(
            shards, tile, args[0], args[1], args[29], args[30], args[2], args[3][:, None], line, *tables
        )
    else:
        gains = lax.all_gather(own_gains, BOTH, axis=1, tiled=True).astype(jnp.float32)
        weights = Weights(*[lax.all_gather(shard, BOTH, axis=0, tiled=True) for shard in shards])
        rows = [whole_row(args[i]) for i in (0, 1, 29, 30)]
        kept = forward_plain(
            weights, gains, *rows, lengths_row, target_length, args[4], args[10], args[20]
        )
    output, decoder_output, encoder_input_grad, decoder_input_grad, grads, small, decoder_reduced = backward(
        near, weights, kept, lengths_row, target_length, args[4], args[2]
    )
    outs = [None] * 29
    for i, value in ((0, output), (1, decoder_output), (3, decoder_input_grad)):
        outs[i] = own_slots(value)
    if near:
        g = grads
        halves = low(encoder_input_grad).reshape((2, -1) + encoder_input_grad.shape[1:])
        made, small, other = reduce_and_finish(
            [[g.eq, g.ek, g.ev, g.eo], list(g.ew), [g.en]], small, halves
        )
        reduced = unpack(made) + decoder_reduced
        outs[2] = placed_slots(encoder_input_grad, other)
    else:
        g = grads
        every = Weights(
            g.eq, g.ek, g.ev, g.eo, g.ew, g.en, g.dq, g.dk, g.dv, g.do, g.cq, g.ck, g.cv, g.co, g.dw, g.dn
        )
        reduced = [
            lax.psum_scatter(grad.astype(jnp.float32), BOTH, scatter_dimension=0, tiled=True)
            for grad in every
        ]
        small = lax.psum(small, BOTH)
        outs[2] = own_slots(encoder_input_grad)
    for i, value in zip(WEIGHT_OUTS, reduced):
        outs[i] = value
    feature_count = args[0].shape[2]
    share = feature_count // row_count
    for number, i in enumerate(GAIN_OUTS):
        outs[i] = lax.dynamic_slice_in_dim(small, number * feature_count + me * share, share)
    offset = 6 * feature_count
    size = BUCKETS * HEADS
    outs[9] = small[offset : offset + size].reshape(BUCKETS, HEADS)
    outs[19] = small[offset + size : offset + 2 * size].reshape(BUCKETS, HEADS)
    sums = small[offset + 2 * size :]
    divisors = jnp.stack([sums[4], sums[4], sums[5], sums[5]]) * feature_count
    outs[28] = jnp.sqrt(sums[:4] / divisors)
    return tuple(outs)


def solution(mesh):
    row_spec = P("rows", "seq", None)
    matrix = P(BOTH, None)
    vector = P(BOTH)
    in_specs = [row_spec, row_spec, P("rows", None), P("rows"), P()] + [None] * 26
    in_specs[10] = in_specs[20] = P()
    in_specs[29] = in_specs[30] = row_spec
    for i in GAIN_ARGS:
        in_specs[i] = vector
    for i in WEIGHT_ARGS:
        in_specs[i] = matrix
    out_specs = [row_spec] * 4 + [None] * 25
    out_specs[9] = out_specs[19] = out_specs[28] = P()
    for i in GAIN_OUTS:
        out_specs[i] = vector
    for i in WEIGHT_OUTS:
        out_specs[i] = matrix
    near = mesh.shape["rows"] == 4 * CHAIN and mesh.shape["seq"] == 2
    return jax.shard_map(
        functools.partial(body, near),
        mesh=mesh,
        in_specs=tuple(in_specs),
        out_specs=tuple(out_specs),
        check_vma=False,
    )
```

```python
import functools
from types import SimpleNamespace
from typing import NamedTuple

import jax
import jax.numpy as jnp
from jax import lax
from jax.experimental import pallas as pl
from jax.experimental.pallas import tpu as pltpu
from jax.sharding import PartitionSpec as P

HEADS = 12
BUCKETS = 32
EPSILON = 1e-06
NEGATIVE = -1e30
HIGHEST_PRECISION = lax.Precision.HIGHEST
BOTH = ("rows", "seq")
CHAIN = 4
PAIRS = HEADS // 2

SPAN=1024
CONTRACT_LAST=(((1,),(1,)),((),()))
CONTRACT_FIRST=(((0,),(0,)),((),()))

def dotf(a,b,dims):
    return lax.dot_general(a,b,dims,preferred_element_type=jnp.float32)

def allowed_of(mode,qcode,kcode,shape):
    if mode=="segment":
        return qcode==kcode
    if mode=="causal":
        qi=lax.broadcasted_iota(jnp.int32,shape,0); ki=lax.broadcasted_iota(jnp.int32,shape,1)
        return (ki<=qi)&(qcode==kcode)
    return (qcode==0)|(kcode==1)

def probs_of(q,k,row,allowed,half):
    s=dotf(q,k,CONTRACT_LAST)
    if row is not None:
        wide=jnp.broadcast_to(row,(s.shape[0],SPAN))
        s=s+pltpu.roll(wide,SPAN-half,1,stride=1,stride_axis=0)[:,:s.shape[1]]
    s=jnp.where(allowed,s,NEGATIVE)
    e=jnp.exp(s-jnp.max(s,axis=-1,keepdims=True))
    return e*(1.0/jnp.sum(e,axis=-1,keepdims=True))

def fwd_kernel(mode,half,*refs):
    if mode=="cross":
        q_ref,k_ref,v_ref,qc,kc,o_ref=refs; t_ref=None
    else:
        q_ref,k_ref,v_ref,qc,kc,t_ref,o_ref=refs
    allowed=allowed_of(mode,qc[...],kc[...],(q_ref.shape[0],k_ref.shape[0]))
    for h in range(2):
        sl=slice(64*h,64*h+64)
        p=probs_of(q_ref[:,sl],k_ref[:,sl],None if t_ref is None else t_ref[0,h:h+1,:],allowed,half)
        o_ref[:,sl]=jnp.dot(p.astype(jnp.bfloat16),v_ref[:,sl],preferred_element_type=jnp.float32).astype(jnp.bfloat16)

def bwd_kernel(mode,half,*refs):
    if mode=="cross":
        q_ref,k_ref,v_ref,g_ref,qc,kc,dq_ref,dk_ref,dv_ref=refs; t_ref=None
    else:
        q_ref,k_ref,v_ref,g_ref,qc,kc,t_ref,dq_ref,dk_ref,dv_ref,dt_ref=refs
    allowed=allowed_of(mode,qc[...],kc[...],(q_ref.shape[0],k_ref.shape[0]))
    for h in range(2):
        sl=slice(64*h,64*h+64)
        q=q_ref[:,sl];k=k_ref[:,sl];v=v_ref[:,sl];g=g_ref[:,sl]
        p=probs_of(q,k,None if t_ref is None else t_ref[0,h:h+1,:],allowed,half)
        dv_ref[:,sl]=dotf(p.astype(jnp.bfloat16),g,CONTRACT_FIRST).astype(jnp.bfloat16)
        dp=dotf(g,v,CONTRACT_LAST)
        ds=p*(dp-jnp.sum(dp*p,axis=-1,keepdims=True))
        dsb=ds.astype(jnp.bfloat16)
        dq_ref[:,sl]=jnp.dot(dsb,k,preferred_element_type=jnp.float32).astype(jnp.bfloat16)
        dk_ref[:,sl]=dotf(dsb,q,CONTRACT_FIRST).astype(jnp.bfloat16)
        if t_ref is not None:
            sq=ds.shape[0]
            flip=(lax.broadcasted_iota(jnp.int32,(sq,sq),0)+lax.broadcasted_iota(jnp.int32,(sq,sq),1)==sq-1).astype(jnp.bfloat16)
            flipped=jnp.dot(flip,dsb,preferred_element_type=jnp.float32)
            wide=jnp.concatenate([flipped,jnp.zeros((sq,SPAN-ds.shape[1]),jnp.float32)],axis=1)
            rolled=pltpu.roll(wide,half-(sq-1),1,stride=1,stride_axis=0)
            dt_ref[0,h:h+1,:]=jnp.sum(rolled,axis=0,keepdims=True)

def attn(kernel,mode,half,outs,q,k,v,extra,qc,kc,table):
    sq,width=q.shape; sk=k.shape[0]
    qs=pl.BlockSpec((sq,128),lambda i:(0,i)); ks=pl.BlockSpec((sk,128),lambda i:(0,i))
    ts=pl.BlockSpec((1,2,SPAN),lambda i:(i,0,0))
    ins=[q,k,v]+extra+[qc,kc]; specs=[qs,ks,ks]+[qs]*len(extra)+[pl.BlockSpec((sq,1),lambda i:(0,0)),pl.BlockSpec((1,sk),lambda i:(0,0))]
    if table is not None: ins.append(table); specs.append(ts)
    shapes={"q":(jax.ShapeDtypeStruct((sq,width),jnp.bfloat16),qs),"k":(jax.ShapeDtypeStruct((sk,width),jnp.bfloat16),ks),"t":(jax.ShapeDtypeStruct((width//128,2,SPAN),jnp.float32),ts)}
    return pl.pallas_call(functools.partial(kernel,mode,half),grid=(width//128,),in_specs=specs,
        out_shape=[shapes[o][0] for o in outs],out_specs=[shapes[o][1] for o in outs],
        compiler_params=pltpu.CompilerParams(vmem_limit_bytes=48*2**20))(*ins)

def attn_fwd(mode,half,q,k,v,qc,kc,table):
    return attn(fwd_kernel,mode,half,"q",q,k,v,[],qc,kc,table)[0]
def attn_bwd(mode,half,q,k,v,g,qc,kc,table):
    return attn(bwd_kernel,mode,half,"qkk"+("t" if table is not None else ""),q,k,v,[g],qc,kc,table)


class Place:
    def __init__(self):
        row = lax.axis_index("rows")
        self.z, self.x, self.c, self.y = row // 4, (row // 2) % 2, row % 2, lax.axis_index("seq")

    def device(self, axis):
        z, x, c, y = self.z, self.x, self.c, self.y
        if axis == "up":
            z = z + 1
        if axis == "down":
            z = z - 1
        if axis == "x":
            x = 1 - x
        if axis == "c":
            c = 1 - c
        if axis == "y":
            y = 1 - y
        return {"rows": z * 4 + x * 2 + c, "seq": y}


    def flipped(self, number):
        x, c, y = [
            1 - at if number & bit else at for at, bit in ((self.x, 4), (self.c, 2), (self.y, 1))
        ]
        return {"rows": self.z * 4 + x * 2 + c, "seq": y}

    def along(self, number):
        return {"rows": (self.z + number) % CHAIN * 4 + self.x * 2 + self.c, "seq": self.y}


def greet_all(place):
    barrier = pltpu.get_barrier_semaphore()
    others = [place.flipped(n) for n in range(1, 8)] + [place.along(n) for n in range(1, CHAIN)]
    for device in others:
        pl.semaphore_signal(
            barrier, inc=1, device_id=device, device_id_type=pl.DeviceIdType.MESH
        )
    pl.semaphore_wait(barrier, len(others))


def greet(place):
    barrier = pltpu.get_barrier_semaphore()

    def signal(axis):
        pl.semaphore_signal(
            barrier, inc=1, device_id=place.device(axis), device_id_type=pl.DeviceIdType.MESH
        )

    for axis in "xcy":
        signal(axis)
    pl.when(place.z < CHAIN - 1)(lambda: signal("up"))
    pl.when(place.z > 0)(lambda: signal("down"))
    ends = (place.z == 0) | (place.z == CHAIN - 1)
    pl.when(ends)(lambda: pl.semaphore_wait(barrier, 4))
    pl.when(jnp.logical_not(ends))(lambda: pl.semaphore_wait(barrier, 5))


def third_of(width, third):
    if third is None:
        return slice(None)
    return slice(width // 3 * third, width // 3 * (third + 1))


class GatherStream:
    def __init__(self, place, own, out, third, kind, u, v, send, recv):
        self.place, self.own, self.out, self.third = place, own, out, third
        self.kind, self.u, self.v, self.send, self.recv = kind, u, v, send, recv
        self.span = third_of(own.shape[-1], third)

    def block(self, z, pair):
        p = self.place
        x = slice(None) if pair and self.u == "x" else p.x
        y = slice(None) if pair and self.u == "y" else p.y
        return self.out.at[:, z, x, p.c, y, :, self.span]

    def other(self, z, axis, pair):
        p = self.place
        x, y = p.x, p.y
        if pair and self.u == "x":
            x = slice(None)
        elif axis == "x":
            x = 1 - x
        if pair and self.u == "y":
            y = slice(None)
        elif axis == "y":
            y = 1 - y
        return self.out.at[:, z, x, p.c, y, :, self.span]

    def copy(self, slot, src, dst, axis):
        return pltpu.make_async_remote_copy(
            src_ref=src,
            dst_ref=dst,
            send_sem=self.send.at[slot],
            recv_sem=self.recv.at[slot],
            device_id=self.place.device(axis),
            device_id_type=pl.DeviceIdType.MESH,
        )

    def first(self, z):
        return self.own.at[:, :, self.span]

    def chain_copy(self, up, step):
        pair = self.kind == "B"
        z = self.place.z - (step - 1) if up else self.place.z + (step - 1)
        src = self.first(z) if step == 1 and not pair else self.block(z, pair)
        return self.copy(step - 1 if up else step + 2, src, self.block(z, pair), "up" if up else "down")

    def chain_arrival(self, up, step):
        pair = self.kind == "B"
        z = self.place.z - step if up else self.place.z + step
        ref = self.block(z, pair)
        return self.copy(step - 1 if up else step + 2, ref, ref, "up" if up else "down")

    def sends_at(self, up, step):
        z = self.place.z
        if up:
            return (z < CHAIN - 1) & (z >= step - 1)
        return (z > 0) & (z <= CHAIN - step)

    def arrives_at(self, up, step):
        z = self.place.z
        return z >= step if up else z <= CHAIN - 1 - step

    def side_copy(self, slot, z, axis, pair, fresh):
        src = self.first(z) if fresh else self.block(z, pair)
        return self.copy(slot, src, self.block(z, pair), axis)

    def side_arrival(self, slot, z, axis, pair):
        ref = self.other(z, axis, pair)
        return self.copy(slot, ref, ref, axis)

    def z_of(self, number):
        if number == 0:
            return self.place.z
        return self.place.z - number if number <= CHAIN - 1 else self.place.z + (number - CHAIN + 1)

    def u_copy(self, number):
        return self.side_copy(6 + number, self.z_of(number), self.u, False, number == 0)

    def u_arrival(self, number):
        return self.side_arrival(6 + number, self.z_of(number), self.u, False)

    def v_copy(self, number):
        return self.side_copy(13 + number, self.z_of(number), self.v, True, False)

    def v_arrival(self, number):
        return self.side_arrival(13 + number, self.z_of(number), self.v, True)


SLOTS = 20


def each_arrival(stream, step, act):
    for up in (True, False):
        number = step if up else step + CHAIN - 1
        pl.when(stream.arrives_at(up, step))(functools.partial(act, up, number))


def plans_for(arrays):
    plans = []
    for a, array in enumerate(arrays):
        u, v = ("x", "y") if a % 2 == 0 else ("y", "x")
        if array.shape[-1] % 768 == 0:
            plans += [(a, 0, "B", "x", "y"), (a, 1, "B", "y", "x"), (a, 2, "A", u, v)]
        else:
            plans.append((a, None, "A", u, v))
    return tuple(plans)


def add_into(target, terms, span):
    lead = target.shape[:-2]
    total = 1
    for size in lead:
        total *= size

    def one(flat, unused):
        index = []
        for size in reversed(lead):
            index.insert(0, flat % size)
            flat = flat // size
        value = target[(*index, slice(None), span)].astype(jnp.float32)
        for term in terms:
            value = value + term[(*index, slice(None), span)].astype(jnp.float32)
        target[(*index, slice(None), span)] = value.astype(target.dtype)
        return unused

    lax.fori_loop(0, total, one, 0)


class ReduceStream:
    def __init__(self, place, bufs, third, kind, u, v, send, recv):
        self.place, self.kind, self.u, self.v, self.send, self.recv = place, kind, u, v, send, recv
        self.acc, self.side_v, self.side_u, self.chain = bufs
        self.span = third_of(self.acc.shape[-1], third)

    def z_of(self, number):
        return GatherStream.z_of(self, number)

    def pair(self, z, v_other=False):
        p = self.place
        flip = lambda at: 1 - at if v_other else at
        if self.u == "x":
            return self.acc.at[:, z, :, flip(p.y)]
        return self.acc.at[:, z, flip(p.x), :]

    def single(self, z, u_other=False):
        p = self.place
        x = 1 - p.x if u_other and self.u == "x" else p.x
        y = 1 - p.y if u_other and self.u == "y" else p.y
        return self.acc.at[:, z, x, y]

    def copy(self, slot, src, dst, axis):
        return pltpu.make_async_remote_copy(
            src_ref=src.at[..., self.span],
            dst_ref=dst.at[..., self.span],
            send_sem=self.send.at[slot],
            recv_sem=self.recv.at[slot],
            device_id=self.place.device(axis),
            device_id_type=pl.DeviceIdType.MESH,
        )

    def v_copy(self, number):
        z = self.z_of(number)
        return self.copy(6 + number, self.pair(z, True), self.side_v.at[:, z], self.v)

    def v_add(self, number):
        z = self.z_of(number)
        self.v_copy(number).wait_recv()
        add_into(self.pair(z), [self.side_v.at[:, z]], self.span)

    def u_copy(self, number):
        z = self.z_of(number)
        return self.copy(13 + number, self.single(z, True), self.side_u.at[:, z], self.u)

    def u_add(self, number):
        z = self.z_of(number)
        self.u_copy(number).wait_recv()
        add_into(self.single(z), [self.side_u.at[:, z]], self.span)

    def chain_block(self, z):
        return self.pair(z) if self.kind == "B" else self.single(z)

    def chain_slot(self, up, step):
        at = self.chain.at[:, 0 if up else 1, step - 1]
        return at if self.kind == "B" else at.at[:, 0]

    def chain_copy(self, up, step):
        z = self.place.z + step if up else self.place.z - step
        return self.copy(
            step - 1 if up else step + 2,
            self.chain_block(z),
            self.chain_slot(up, step),
            "up" if up else "down",
        )

    def has_before(self, up):
        return self.place.z > 0 if up else self.place.z < CHAIN - 1

    def chain_arrival(self, up, step):
        ref = self.chain_slot(up, step)
        return self.copy(step - 1 if up else step + 2, ref, ref, "up" if up else "down")

    def chain_step(self, up, step):
        z = self.place.z + step if up else self.place.z - step
        if step < CHAIN - 1:

            @pl.when(self.has_before(up))
            def arrived():
                self.chain_arrival(up, step + 1).wait_recv()
                add_into(self.chain_block(z), [self.chain_slot(up, step + 1)], self.span)

        self.chain_copy(up, step).start()

    def chain_end(self):
        for up in (True, False):

            @pl.when(self.has_before(up))
            def arrived():
                self.chain_arrival(up, 1).wait_recv()
                add_into(self.chain_block(self.place.z), [self.chain_slot(up, 1)], self.span)


class Reduction:
    def __init__(self, place, plans, items, outs, bufs, sems):
        count = len(items)
        self.place, self.plans, self.items, self.outs = place, plans, items, outs
        send, recv, self.core_send, self.core_recv, self.local = sems
        self.accs, self.cores = bufs[:count], bufs[count : 2 * count]
        self.streams = [
            ReduceStream(
                place, [bufs[k * count + a] for k in (0, 2, 3, 4)], third, kind, u, v,
                send.at[i], recv.at[i],
            )
            for i, (a, third, kind, u, v) in enumerate(plans)
        ]

    def z_of(self, number):
        return GatherStream.z_of(self, number)

    def valid(self, number):
        z = self.place.z
        return z >= number if number < CHAIN else z <= 2 * (CHAIN - 1) - number

    def at(self, number, act):
        if number == 0:
            act(0)
        else:
            pl.when(self.valid(number))(functools.partial(act, number))

    def each(self, act):
        for number in NUMBERS:
            self.at(number, act)

    def begin(self):
        def loads(number):
            z = self.z_of(number)
            for a, refs in enumerate(self.items):
                for i, ref in enumerate(refs):
                    pltpu.make_async_copy(
                        ref.at[z, :, self.place.c],
                        self.accs[a].at[i, z],
                        self.local.at[a * 7 + number],
                    ).start()

        self.each(loads)

    def core_copy(self, a, number, src, dst):
        return pltpu.make_async_remote_copy(
            src_ref=src,
            dst_ref=dst,
            send_sem=self.core_send.at[a * 7 + number],
            recv_sem=self.core_recv.at[a * 7 + number],
            device_id=self.place.device("c"),
            device_id_type=pl.DeviceIdType.MESH,
        )

    def begin_core(self):
        def sends(number):
            z = self.z_of(number)
            for a, refs in enumerate(self.items):
                for i, ref in enumerate(refs):
                    self.core_copy(
                        a, number, ref.at[z, :, 1 - self.place.c], self.cores[a].at[i, z]
                    ).start()

        self.each(sends)

    def core_whole(self, a, number):
        whole = self.cores[a].at[:, self.z_of(number)]
        return self.core_copy(a, number, whole, whole)

    def first(self, number):
        z = self.z_of(number)
        for a in range(len(self.items)):
            whole = self.accs[a].at[:, z]
            pltpu.make_async_copy(whole, whole, self.local.at[a * 7 + number]).wait()
            self.core_whole(a, number).wait_recv()
            add_into(whole, [self.cores[a].at[:, z]], slice(None))
            for s, plan in zip(self.streams, self.plans):
                if plan[0] == a:
                    s.v_copy(number).start()

    def onward(self, s, number):
        up = number >= CHAIN
        s.chain_step(up, number - (CHAIN - 1) if up else number)

    def second(self, number):
        for s in self.streams:
            s.v_add(number)
            if s.kind == "A":
                s.u_copy(number).start()
            elif number > 0:
                self.onward(s, number)

    def third(self, number):
        for s in self.streams:
            if s.kind == "A":
                s.u_add(number)
                if number > 0:
                    self.onward(s, number)

    def events(self):
        return [
            functools.partial(self.at, number, act)
            for act in (self.first, self.second, self.third)
            for number in NUMBERS
        ]

    def end(self):
        for s in self.streams:
            if s.kind == "B":
                s.chain_end()
                s.u_copy(0).start()
        for s in self.streams:
            if s.kind == "A":
                s.chain_end()
        for s in self.streams:
            if s.kind == "B":
                s.u_add(0)
        p = self.place
        for acc, refs in zip(self.accs, self.outs):
            width = acc.shape[-1]
            for item in range(acc.shape[0]):
                value = acc[item, p.z, p.x, p.y].astype(jnp.float32)
                if len(refs[0].shape) == 3:
                    refs[0][item] = value
                else:
                    refs[0][:, item * width : (item + 1) * width] = value

        def last(number):
            for a in range(len(self.items)):
                self.core_whole(a, number).wait_send()
            for s in self.streams:
                s.v_copy(number).wait_send()
                if s.kind == "A" or number == 0:
                    s.u_copy(number).wait_send()
                if number > 0:
                    up = number >= CHAIN
                    s.chain_copy(up, number - (CHAIN - 1) if up else number).wait_send()

        self.each(last)


NUMBERS = (3, 6, 2, 5, 1, 4, 0)


def reduction_parts(groups, joined):
    parts = 8 * CHAIN
    items = [
        [g.reshape(CHAIN, 2, 2, 2, g.shape[0] // parts, g.shape[1]) for g in group] for group in groups
    ]
    shapes = [jax.ShapeDtypeStruct((len(i),) + i[0].shape[-2:], i[0].dtype) for i in items]
    plans = plans_for(shapes)
    count = len(items)
    scratch = [
        pltpu.VMEM((a.shape[0],) + lead + a.shape[-2:], a.dtype)
        for lead in ((CHAIN, 2, 2), (CHAIN, 2, 2), (CHAIN, 2), (CHAIN,), (2, CHAIN - 1, 2))
        for a in shapes
    ]
    sems = pltpu.SemaphoreType.DMA
    scratch += [sems((len(plans), SLOTS))] * 2 + [sems((count * 7,))] * 3
    outs = []
    for a, whole in zip(shapes, joined):
        shape = (a.shape[1], a.shape[0] * a.shape[2]) if whole else a.shape
        outs.append([jax.ShapeDtypeStruct(shape, jnp.float32)])
    return items, plans, scratch, outs


def heads_backward(half, pair, q_ref, k_ref, v_ref, g_ref, qc, kc, t_ref, dq_ref, dk_ref, dv_ref, dt_ref):
    lanes = pl.ds(pl.multiple_of(pair * 128, 128), 128)
    q2, k2, v2, g2 = q_ref[:, lanes], k_ref[:, lanes], v_ref[:, lanes], g_ref[:, lanes]
    size = q2.shape[0]
    allowed = qc == kc
    turn = lax.broadcasted_iota(jnp.int32, (size, size), 0) + lax.broadcasted_iota(
        jnp.int32, (size, size), 1
    )
    flip = (turn == size - 1).astype(jnp.bfloat16)
    made = []
    for h in range(2):
        sl = slice(64 * h, 64 * h + 64)
        q, k, v, g = q2[:, sl], k2[:, sl], v2[:, sl], g2[:, sl]
        p = probs_of(q, k, t_ref[pl.ds(2 * pair + h, 1), :], allowed, half)
        dv = dotf(p.astype(jnp.bfloat16), g, CONTRACT_FIRST)
        dp = dotf(g, v, CONTRACT_LAST)
        ds = (p * (dp - jnp.sum(dp * p, axis=-1, keepdims=True))).astype(jnp.bfloat16)
        dq = jnp.dot(ds, k, preferred_element_type=jnp.float32)
        dk = dotf(ds, q, CONTRACT_FIRST)
        made.append((dq, dk, dv))
        flipped = jnp.dot(flip, ds, preferred_element_type=jnp.float32)
        wide = jnp.concatenate([flipped, jnp.zeros((size, SPAN - size), jnp.float32)], axis=1)
        rolled = pltpu.roll(wide, half - (size - 1), 1, stride=1, stride_axis=0)
        dt_ref[pl.ds(2 * pair + h, 1), :] = jnp.sum(rolled, axis=0, keepdims=True)
    for ref, pieces in zip((dq_ref, dk_ref, dv_ref), zip(*made)):
        ref[:, lanes] = jnp.concatenate(pieces, axis=1).astype(jnp.bfloat16)


def choose(t, starts, acts):
    if len(acts) == 1:
        acts[0]()
        return
    middle = len(acts) // 2

    @pl.when(t < starts[middle])
    def before():
        choose(t, starts[:middle], acts[:middle])

    @pl.when(t >= starts[middle])
    def after():
        choose(t, starts[middle:], acts[middle:])


BACK_TICKS = (
    (0, 1), (), (2, 3), (), (4, 5), (), (6, 7, 8), (), (9, 10), (), (11, 12, 13), (), (14, 15), (),
    (16, 17), (), (18, 19, 20), (),
)


def backward_kernel(plans, counts, out_counts, half, *refs):
    refs = list(refs)
    take = lambda n: [refs.pop(0) for unused in range(n)]
    items = [take(n) for n in counts]
    q, k, v, g, first, etable, lengths = take(7)
    weights = take(3)
    act, pre_low, second, branch_low, attended, middle_low = take(6)
    outs = [take(n) for n in out_counts]
    dist, normed = take(2)
    grads = take(3)
    outward, narrow = take(2)
    wide = take(4)
    bufs = take(5 * len(counts))
    sems = take(5)
    derived = take(3)
    place = Place()
    run = Reduction(place, plans, items, outs, bufs, sems)
    run.begin()
    greet(place)
    run.begin_core()
    size = q.shape[0]

    def segment(axis):
        shape = (size, 1) if axis == 0 else (1, size)
        at = lax.broadcasted_iota(jnp.int32, shape, axis)
        code, end = jnp.zeros(shape, jnp.int32), 0
        for j in range(lengths.shape[1]):
            end = end + lengths[place.y, j]
            code = code + (end <= at).astype(jnp.int32)
        return code

    events = run.events()

    def tick(t, unused):
        def some(numbers):
            for number in numbers:
                events[number]()

        choose(t, list(range(len(BACK_TICKS))), [functools.partial(some, n) for n in BACK_TICKS])

        @pl.when(t < PAIRS)
        def attention():
            heads_backward(half, t, q, k, v, g, segment(0), segment(1), etable, *derived, dist)

        for i in range(3):

            @pl.when(t == PAIRS + i)
            def project():
                grads[i][...] = dotf(first[...], derived[i][...], CONTRACT_FIRST).astype(jnp.bfloat16)
                part = dotf(derived[i][...], weights[i][...], CONTRACT_LAST)
                normed[...] = part if i == 0 else normed[...] + part

        rest = PAIRS + 3

        @pl.when(t == rest)
        def outward_grad():
            outward[...] = dotf(attended[...], middle_low[...], CONTRACT_FIRST).astype(jnp.bfloat16)

        width = second.shape[1]

        @pl.when((t > rest) & (t <= rest + 4))
        def narrow_grad():
            at = pl.ds(pl.multiple_of((t - rest - 1) * width, 128), width)
            narrow[at] = dotf(act[:, at], branch_low[...], CONTRACT_FIRST).astype(jnp.bfloat16)

        for j in range(4):

            @pl.when(t == rest + 5 + j)
            def wide_grad():
                at = slice(j * width, (j + 1) * width)
                wide[j][...] = dotf(second[...], pre_low[:, at], CONTRACT_FIRST).astype(jnp.bfloat16)

        return unused

    lax.fori_loop(0, len(BACK_TICKS), tick, 0)
    run.end()


def reduce_with_attention(groups, joined, q, k, v, g, first, etable, lengths, weights, others):
    items, plans, scratch, out_groups = reduction_parts(groups, joined)
    flat = [i for group in items for i in group]
    out_shapes = [o for group in out_groups for o in group]
    counts = tuple(len(i) for i in items), tuple(len(o) for o in out_groups)
    vmem, hbm = pl.BlockSpec(memory_space=pltpu.VMEM), pl.BlockSpec(memory_space=pltpu.HBM)
    length, width = q.shape
    outs = pl.pallas_call(
        functools.partial(backward_kernel, plans, *counts, length - 1),
        out_shape=out_shapes
        + [
            jax.ShapeDtypeStruct((16, SPAN), jnp.float32),
            jax.ShapeDtypeStruct((length, width), jnp.float32),
        ]
        + [jax.ShapeDtypeStruct((width, width), jnp.bfloat16)] * 4
        + [jax.ShapeDtypeStruct((others[0].shape[1], width), jnp.bfloat16)]
        + [jax.ShapeDtypeStruct((width, width), jnp.bfloat16)] * 4,
        in_specs=[hbm] * len(flat)
        + [vmem] * 6
        + [pl.BlockSpec(memory_space=pltpu.SMEM)]
        + [vmem] * 9,
        out_specs=[vmem] * (len(out_shapes) + 11),
        scratch_shapes=scratch + [pltpu.VMEM((length, width), jnp.bfloat16)] * 3,
        compiler_params=pltpu.CompilerParams(
            collective_id=1, has_side_effects=True, vmem_limit_bytes=62 * 2**20
        ),
    )(*flat, q, k, v, g, first, etable, lengths, *weights, *others)
    count = len(out_shapes)
    return outs[:count], outs[count], outs[count + 1], outs[count + 2 :]


def finish_kernel(plans, counts, out_counts, *refs):
    refs = list(refs)
    take = lambda n: [refs.pop(0) for unused in range(n)]
    items = [take(n) for n in counts]
    small, halves = take(2)
    outs = [take(n) for n in out_counts]
    total, theirs = take(2)
    bufs = take(5 * len(counts))
    sems = take(5)
    near_in, far_in, subtotal, near_send, near_recv, far_send, far_recv = take(7)
    half_send, half_recv = take(2)
    place = Place()
    run = Reduction(place, plans, items, outs, bufs, sems)
    run.begin()
    greet_all(place)
    run.begin_core()
    half = pltpu.make_async_remote_copy(
        src_ref=halves.at[1 - place.y],
        dst_ref=theirs,
        send_sem=half_send.at[0],
        recv_sem=half_recv.at[0],
        device_id=place.device("y"),
        device_id_type=pl.DeviceIdType.MESH,
    )
    half.start()
    def near(number):
        return pltpu.make_async_remote_copy(
            src_ref=small,
            dst_ref=near_in.at[number - 1],
            send_sem=near_send.at[number - 1],
            recv_sem=near_recv.at[number - 1],
            device_id=place.flipped(number),
            device_id_type=pl.DeviceIdType.MESH,
        )

    def far(number):
        return pltpu.make_async_remote_copy(
            src_ref=subtotal,
            dst_ref=far_in.at[number - 1],
            send_sem=far_send.at[number - 1],
            recv_sem=far_recv.at[number - 1],
            device_id=place.along(number),
            device_id_type=pl.DeviceIdType.MESH,
        )

    for number in range(1, 8):
        near(number).start()
    for number, event in enumerate(run.events()):
        event()
        if number == 9:
            value = small[...]
            for other in range(1, 8):
                near(other).wait_recv()
                value = value + near_in[other - 1]
            subtotal[...] = value
            for other in range(1, CHAIN):
                far(other).start()
    value = subtotal[...]
    for other in range(1, CHAIN):
        far(other).wait_recv()
        value = value + far_in[other - 1]
    total[...] = value
    run.end()
    half.wait_recv()
    half.wait_send()
    for number in range(1, 8):
        near(number).wait_send()
    for number in range(1, CHAIN):
        far(number).wait_send()


def reduce_and_finish(groups, joined, small, halves):
    items, plans, scratch, out_groups = reduction_parts(groups, joined)
    flat = [i for group in items for i in group]
    out_shapes = [o for group in out_groups for o in group]
    counts = tuple(len(i) for i in items), tuple(len(o) for o in out_groups)
    vmem, hbm = pl.BlockSpec(memory_space=pltpu.VMEM), pl.BlockSpec(memory_space=pltpu.HBM)
    sems = pltpu.SemaphoreType.DMA
    lines = -(-small.shape[0] // 1024) * 8
    padded = jnp.pad(small, (0, lines * 128 - small.shape[0])).reshape(lines, 128)
    block = jax.ShapeDtypeStruct((lines, 128), jnp.float32)
    outs = pl.pallas_call(
        functools.partial(finish_kernel, plans, *counts),
        out_shape=out_shapes + [block, jax.ShapeDtypeStruct(halves.shape[1:], halves.dtype)],
        in_specs=[hbm] * len(flat) + [vmem] * 2,
        out_specs=[vmem] * (len(out_shapes) + 2),
        scratch_shapes=scratch
        + [pltpu.VMEM((n, lines, 128), jnp.float32) for n in (7, CHAIN - 1)]
        + [pltpu.VMEM((lines, 128), jnp.float32)]
        + [sems((n,)) for n in (7, 7, CHAIN - 1, CHAIN - 1, 1, 1)],
        compiler_params=pltpu.CompilerParams(
            collective_id=2, has_side_effects=True, vmem_limit_bytes=62 * 2**20
        ),
    )(*flat, padded, halves)
    return outs[:-2], outs[-2].reshape(-1)[: small.shape[0]], outs[-1]


class GatherStage:
    def __init__(self, place, streams, items, sems):
        self.place, self.streams, self.items = place, streams, items
        self.core_send, self.core_recv, self.local = sems

    def own_copy(self, k):
        a, own, out = self.items[k]
        p = self.place
        return pltpu.make_async_copy(own, out.at[:, p.z, p.x, p.c, p.y], self.local.at[a])

    def core_copy(self, k, number, arriving):
        a, own, out = self.items[k]
        z = GatherStream.z_of(self.streams[0], number)
        ref = out.at[:, z, :, 1 - self.place.c if arriving else self.place.c]
        return pltpu.make_async_remote_copy(
            src_ref=ref,
            dst_ref=ref,
            send_sem=self.core_send.at[a * 7 + number],
            recv_sem=self.core_recv.at[a * 7 + number],
            device_id=self.place.device("c"),
            device_id_type=pl.DeviceIdType.MESH,
        )

    def start(self):
        for k in range(len(self.items)):
            self.own_copy(k).start()
        for s in self.streams:
            s.u_copy(0).start()
            if s.kind == "A":
                self.chain_start(s)

    def chain_start(self, s):
        for up in (True, False):
            pl.when(s.sends_at(up, 1))(lambda: s.chain_copy(up, 1).start())

    def after_u(self):
        for k in range(len(self.items)):
            self.own_copy(k).wait()
        for s in self.streams:
            s.u_arrival(0).wait_recv()
            if s.kind == "B":
                self.chain_start(s)
            s.v_copy(0).start()

    def arrivals(self, step):
        def arrival(s, up, number):
            s.chain_arrival(up, step).wait_recv()
            if step < CHAIN - 1:
                pl.when(s.sends_at(up, step + 1))(lambda: s.chain_copy(up, step + 1).start())
            if s.kind == "A":
                s.u_copy(number).start()
            else:
                s.v_copy(number).start()

        for s in self.streams:
            each_arrival(s, step, functools.partial(arrival, s))

    def sides(self, step):
        def side(s, up, number):
            s.u_arrival(number).wait_recv()
            s.v_copy(number).start()

        for s in self.streams:
            if s.kind == "A":
                each_arrival(s, step, functools.partial(side, s))

    def finish(self, number):
        for s in self.streams:
            s.v_arrival(number).wait_recv()
        for k in range(len(self.items)):
            self.core_copy(k, number, False).start()

    def finishes(self, step):
        each_arrival(self.streams[0], step, lambda up, number: self.finish(number))

    def last(self):
        def one(up, number):
            for k in range(len(self.items)):
                self.core_copy(k, number, True).wait_recv()

        one(True, 0)
        for step in range(1, CHAIN):
            each_arrival(self.streams[0], step, one)

    def events(self):
        steps = range(1, CHAIN)
        moves = [
            act
            for step in steps
            for act in (functools.partial(self.arrivals, step), functools.partial(self.sides, step))
        ]
        ends = [functools.partial(self.finishes, step) for step in steps]
        return [self.start, self.after_u] + moves + [lambda: self.finish(0)] + ends + [self.last]

    def sent(self):
        def one(up, number):
            for k in range(len(self.items)):
                self.core_copy(k, number, False).wait_send()
            for s in self.streams:
                if s.kind == "A":
                    s.u_copy(number).wait_send()
                s.v_copy(number).wait_send()

        one(True, 0)
        for s in self.streams:
            if s.kind == "B":
                s.u_copy(0).wait_send()
            for step in range(1, CHAIN):
                for up in (True, False):
                    pl.when(s.sends_at(up, step))(lambda: s.chain_copy(up, step).wait_send())
        for step in range(1, CHAIN):
            each_arrival(self.streams[0], step, one)


class Weights(NamedTuple):
    eq: jax.Array
    ek: jax.Array
    ev: jax.Array
    eo: jax.Array
    ew: jax.Array
    en: jax.Array
    dq: jax.Array
    dk: jax.Array
    dv: jax.Array
    do: jax.Array
    cq: jax.Array
    ck: jax.Array
    cv: jax.Array
    co: jax.Array
    dw: jax.Array
    dn: jax.Array


class Rows(NamedTuple):
    x: jax.Array
    first: jax.Array
    q: jax.Array
    k: jax.Array
    v: jax.Array
    attended: jax.Array
    middle: jax.Array
    second: jax.Array
    output: jax.Array
    memory: jax.Array
    ck: jax.Array
    cv: jax.Array
    cotangent: jax.Array
    target: jax.Array
    own: jax.Array
    sq: jax.Array
    sk: jax.Array
    sv: jax.Array
    sattended: jax.Array
    tmiddle: jax.Array
    cross: jax.Array
    cq: jax.Array
    cattended: jax.Array
    crossed: jax.Array
    third: jax.Array
    doutput: jax.Array
    tcotangent: jax.Array


ROW_KINDS = (
    (True, False),
    (True, False),
    (True, False),
    (True, False),
    (True, False),
    (True, False),
    (True, True),
    (True, False),
    (True, True),
    (True, False),
    (True, False),
    (True, False),
    (True, False),
    (False, False),
    (False, False),
    (False, False),
    (False, False),
    (False, False),
    (False, False),
    (False, True),
    (False, False),
    (False, False),
    (False, False),
    (False, True),
    (False, False),
    (False, True),
    (False, False),
)
GROUP_ARRAYS = ((0, 1), (2, 3), (4,), (5, 6))
(
    TABLES, BEGIN, QKV, ATTEND, JOIN, FFN, CLOSE, SELF, SELF_ATTEND, CROSS, CROSS_ATTEND, CROSSED,
    DFFN, DCLOSE,
) = range(14)
TICKS = (
    (TABLES, ((0, 0),)),
    (BEGIN, (
        (0, 1), (0, 2), (0, 3), (0, 4), (1, 0), (1, 1), (0, 5), (0, 6), (0, 7), (0, 8), (0, 9),
        (1, 2), (0, 10), (0, 11), (1, 3), (0, 12),
    )),
    (QKV, ()),
    (ATTEND, ((1, 4),)),
    (ATTEND, ((2, 0), (2, 1), (1, 5))),
    (ATTEND, ((1, 6),)),
    (ATTEND, ((1, 7),)),
    (ATTEND, ((2, 2), (1, 8), (1, 9))),
    (ATTEND, ((2, 3), (1, 10))),
    (JOIN, ((1, 11), (2, 4), (3, 0), (3, 1), (1, 12))),
    (FFN, ((2, 5),)),
    (FFN, ((2, 6),)),
    (FFN, ((2, 7),)),
    (FFN, ((3, 2), (2, 8), (2, 9))),
    (CLOSE, ((3, 3), (2, 10))),
    (SELF, ((3, 4), (2, 11), (2, 12))),
    (SELF_ATTEND, ((3, 5),)),
    (CROSS, ((3, 6),)),
    (CROSS_ATTEND, ((3, 7), (3, 8))),
    (CROSS_ATTEND, ((3, 9),)),
    (CROSSED, ((3, 10),)),
    (DFFN, ((3, 11), (3, 12))),
    (DFFN, ()), (DFFN, ()), (DFFN, ()),
    (DCLOSE, ()),
)


def first_of(kind):
    return [k for k, unused in TICKS].index(kind)


def load_blocks(src, items, landing, sem, dst):
    height, width = landing.shape[-2:]
    copy = pltpu.make_async_copy(src.at[items], landing, sem)
    copy.start()
    copy.wait()

    def one(flat, unused):
        z, x, c = flat // 4, (flat // 2) % 2, flat % 2
        rows = pl.ds(pl.multiple_of(flat * 2 * height, 2 * height), 2 * height)
        for item in range(landing.shape[0]):
            pair = [landing[item, z, x, c, y].astype(jnp.float32) for y in range(2)]
            dst[item, rows] = jnp.concatenate(pair, axis=0).astype(dst.dtype)
        return unused

    lax.fori_loop(0, 4 * CHAIN, one, 0)


def matmul(left, right):
    return jnp.dot(left, right, preferred_element_type=jnp.float32)


def low(values):
    return values.astype(jnp.bfloat16)


def rms_of(values, gain):
    return (
        values * lax.rsqrt(jnp.mean(values * values, axis=-1, keepdims=True) + EPSILON) * gain
    )


def heads_forward(mode, half, pair, q_ref, k_ref, v_ref, o_ref, qc, kc, t_ref):
    lanes = pl.ds(pl.multiple_of(pair * 128, 128), 128)
    q2, k2, v2 = q_ref[:, lanes], k_ref[:, lanes], v_ref[:, lanes]
    allowed = allowed_of(mode, qc, kc, (q2.shape[0], k2.shape[0]))
    mixed = []
    for h in range(2):
        sl = slice(64 * h, 64 * h + 64)
        row = None if t_ref is None else t_ref[pl.ds(2 * pair + h, 1), :]
        p = probs_of(q2[:, sl], k2[:, sl], row, allowed, half)
        mixed.append(matmul(low(p), v2[:, sl]))
    o_ref[:, lanes] = low(jnp.concatenate(mixed, axis=1))


def forward_kernel(plans, *refs):
    refs = list(refs)
    take = lambda n: [refs.pop(0) for unused in range(n)]
    shards = Weights(*take(16))
    tile, halves_x, halves_t, halves_c, halves_tc = take(5)
    lengths, target_lengths, buckets, etable_in, dtable_in = take(5)
    w_sq, w_wide, w_narrow, w_dsq, w_dwide, w_dnarrow = take(6)
    row = Rows(*take(len(ROW_KINDS)))
    gains, etable, dtable, sums, pre_hbm, act_hbm, dpre, dact = take(8)
    stack_e, stack_d, stack_w, stack_dw, gbuf, branch, dbranch = take(7)
    send, recv, core_send, core_recv, local, load_sem, store_sem, swap_send, swap_recv = take(9)
    sq, wide, narrow, dwide, landing, pre, act = take(7)
    place = Place()
    mine = place.y
    half = row.x.shape[0] - 1

    for i in range(4):
        stack_e[i] = shards[i][...]
    for i in range(8):
        stack_d[i] = shards[6 + i][...]
    for j in range(4):
        columns = slice(j * stack_w.shape[2], (j + 1) * stack_w.shape[2])
        stack_w[j] = shards.ew[:, columns]
        stack_dw[j] = shards.dw[:, columns]
    owns = [stack_e, tile, stack_w, shards.en, stack_d, stack_dw, shards.dn]
    hbm = [w_sq, None, w_wide, w_narrow, w_dsq, w_dwide, w_dnarrow]
    full = [gbuf if out is None else out for out in hbm]
    stages = []
    for group in GROUP_ARRAYS:
        streams = [
            GatherStream(place, owns[a], full[a], third, kind, u, v, send.at[i], recv.at[i])
            for i, (a, third, kind, u, v) in enumerate(plans)
            if a in group
        ]
        items = [(a, owns[a], full[a]) for a in group]
        stages.append(GatherStage(place, streams, items, (core_send, core_recv, local)))

    def half_copy(number, halves, whole):
        size = halves.shape[1]
        return pltpu.make_async_remote_copy(
            src_ref=halves.at[1 - mine],
            dst_ref=whole.at[pl.ds(pl.multiple_of(mine * size, 64), size)],
            send_sem=swap_send.at[number],
            recv_sem=swap_recv.at[number],
            device_id=place.device("y"),
            device_id_type=pl.DeviceIdType.MESH,
        )

    swaps = [
        half_copy(0, halves_x, row.x),
        half_copy(1, halves_t, row.target),
        half_copy(2, halves_c, row.cotangent),
        half_copy(3, halves_tc, row.tcotangent),
    ]
    for halves, whole in (
        (halves_x, row.x),
        (halves_t, row.target),
        (halves_c, row.cotangent),
        (halves_tc, row.tcotangent),
    ):
        size = halves.shape[1]
        whole[pl.ds(pl.multiple_of(mine * size, 64), size)] = halves[mine]
    greet(place)

    count = lengths.shape[1]
    ends, total = [], 0
    for j in range(count):
        total = total + lengths[mine, j]
        ends.append(total)
    target_length = target_lengths[mine, 0]

    def codes(size, axis):
        shape = (size, 1) if axis == 0 else (1, size)
        at = lax.broadcasted_iota(jnp.int32, shape, axis)
        segment = jnp.zeros(shape, jnp.int32)
        for end in ends:
            segment = segment + (end <= at).astype(jnp.int32)
        return at, segment

    length, target_count = row.x.shape[0], row.target.shape[0]

    def mean_parts(kept, first, second, rows):
        keep = lax.broadcasted_iota(jnp.int32, (first.shape[0], 1), 0) < kept
        for i, value in enumerate((first, second)):
            total_square = jnp.sum(jnp.where(keep, value * value, 0.0))
            sums[rows + i : rows + i + 1, :] = jnp.full((1, 128), total_square, jnp.float32)
        sums[rows // 2 + 4 : rows // 2 + 5, :] = jnp.full((1, 128), kept.astype(jnp.float32))

    def load_narrow(src):
        return [
            pltpu.make_async_copy(
                src.at[0, z, x, c, y],
                narrow.at[pl.ds((((z * 2 + x) * 2 + c) * 2 + y) * src.shape[5], src.shape[5])],
                load_sem.at[0],
            )
            for z in range(CHAIN)
            for x in range(2)
            for c in range(2)
            for y in range(2)
        ]

    def narrow_loaded():
        pltpu.make_async_copy(narrow, narrow, load_sem.at[0]).wait()

    chunk = row.x.shape[1]
    chunks = wide.shape[0]

    def store(j, slot):
        columns = pl.ds(pl.multiple_of(j * chunk, 128), chunk)
        return (
            pltpu.make_async_copy(pre.at[slot], pre_hbm.at[:, columns], store_sem.at[0, slot]),
            pltpu.make_async_copy(act.at[slot], act_hbm.at[:, columns], store_sem.at[1, slot]),
        )

    def tick(t, unused):
        pieces = {}

        def at_tick(kind):
            def keep(act):
                pieces[kind] = act
                return act

            return keep

        def comm(events):
            for stage, number in events:
                stages[stage].events()[number]()

        choose(
            t, list(range(len(TICKS))), [functools.partial(comm, events) for unused, events in TICKS]
        )

        @at_tick(TABLES)
        def tables():
            swaps[0].start()
            swaps[1].start()
            for table_in, table in ((etable_in, etable), (dtable_in, dtable)):
                value = jnp.zeros(table.shape, jnp.float32)
                for b in range(BUCKETS):
                    value = value + jnp.where(buckets[...] == b, table_in[:, b : b + 1], 0.0)
                table[...] = value

        @at_tick(BEGIN)
        def begin():
            load_blocks(w_sq, slice(0, 4), landing, load_sem.at[1], sq)
            tiles = gbuf.at[0]
            value = jnp.zeros(gains.shape, jnp.float32)
            share = gains.shape[1] // (8 * CHAIN)
            for d in range(8 * CHAIN):
                z, x, c, y = d // 8, (d // 4) % 2, (d // 2) % 2, d % 2
                part = tiles[z, x, c, y].astype(jnp.float32)
                spread = jnp.concatenate(
                    [part, jnp.zeros((8, gains.shape[1] - 128), jnp.float32)], axis=1
                )
                value = value + (pltpu.roll(spread, share * d, 1) if d else spread)
            gains[...] = value
            swaps[0].wait_recv()
            swaps[1].wait_recv()
            row.first[...] = low(rms_of(row.x[...].astype(jnp.float32), value[0:1, :]))

        @at_tick(QKV)
        def project():
            for i, ref in enumerate((row.q, row.k, row.v)):
                ref[...] = low(matmul(row.first[...], sq[i]))

        @at_tick(ATTEND)
        def attention():
            heads_forward(
                "segment", half, t - first_of(ATTEND), row.q, row.k, row.v, row.attended,
                codes(length, 0)[1], codes(length, 1)[1], etable,
            )

        @at_tick(JOIN)
        def join():
            for copy in load_narrow(w_narrow):
                copy.start()
            value = row.x[...].astype(jnp.float32) + matmul(row.attended[...], sq[3])
            row.middle[...] = value
            row.second[...] = low(rms_of(value, gains[1:2, :]))
            load_blocks(w_wide, slice(0, 4), landing, load_sem.at[1], wide)
            narrow_loaded()

        @at_tick(FFN)
        def feedforward():
            j = t - first_of(FFN)
            slot = lax.rem(j, 2)

            @pl.when(j >= 2)
            def stored():
                for copy in store(j - 2, slot):
                    copy.wait()

            columns = pl.ds(pl.multiple_of(j * chunk, 128), chunk)
            value = matmul(row.second[...], wide[j])
            active = low(jax.nn.gelu(value, approximate=True))
            pre[slot] = value
            act[slot] = active
            for copy in store(j, slot):
                copy.start()
            part = matmul(active, narrow[columns, :])

            @pl.when(j == 0)
            def first_part():
                branch[...] = part

            @pl.when(j > 0)
            def more():
                branch[...] = branch[...] + part

        @at_tick(CLOSE)
        def close():
            value = row.middle[...] + branch[...]
            row.output[...] = value
            row.memory[...] = low(rms_of(value, gains[2:3, :]))
            mean_parts(total, value, branch[...], 0)
            swaps[2].start()
            swaps[3].start()
            for j in (chunks - 2, chunks - 1):
                for copy in store(j, j % 2):
                    copy.wait()

        @at_tick(SELF)
        def self_project():
            load_blocks(w_dsq, slice(0, 4), landing, load_sem.at[1], sq)
            load_blocks(w_dsq, slice(4, 8), landing, load_sem.at[1], wide)
            normed = low(rms_of(row.target[...].astype(jnp.float32), gains[3:4, :]))
            row.own[...] = normed
            for i, ref in enumerate((row.sq, row.sk, row.sv)):
                ref[...] = low(matmul(normed, sq[i]))
            row.ck[...] = low(matmul(row.memory[...], wide[1]))
            row.cv[...] = low(matmul(row.memory[...], wide[2]))

        def valid_code(size, axis, limit):
            return (codes(size, axis)[0] < limit).astype(jnp.int32)

        @at_tick(SELF_ATTEND)
        def self_attention():
            def one(pair, unused):
                heads_forward(
                    "causal", half, pair, row.sq, row.sk, row.sv, row.sattended,
                    valid_code(target_count, 0, target_length),
                    valid_code(target_count, 1, target_length), dtable,
                )
                return unused

            lax.fori_loop(0, PAIRS, one, 0)

        @at_tick(CROSS)
        def self_join():
            value = row.target[...].astype(jnp.float32) + matmul(row.sattended[...], sq[3])
            row.tmiddle[...] = value
            normed = low(rms_of(value, gains[4:5, :]))
            row.cross[...] = normed
            row.cq[...] = low(matmul(normed, wide[0]))

        @at_tick(CROSS_ATTEND)
        def cross_attention():
            def one(pair, unused):
                heads_forward(
                    "cross", half, pair, row.cq, row.ck, row.cv, row.cattended,
                    valid_code(target_count, 0, target_length), valid_code(length, 1, total), None,
                )
                return unused

            begin_pair = (t - first_of(CROSS_ATTEND)) * (PAIRS // 2)
            lax.fori_loop(begin_pair, begin_pair + PAIRS // 2, one, 0)

        @at_tick(CROSSED)
        def cross_join():
            value = row.tmiddle[...] + matmul(row.cattended[...], wide[3])
            row.crossed[...] = value
            row.third[...] = low(rms_of(value, gains[5:6, :]))

        @at_tick(DFFN)
        def decoder_feedforward():
            j = t - first_of(DFFN)

            @pl.when(j == 0)
            def decoder_load():
                for copy in load_narrow(w_dnarrow):
                    copy.start()
                load_blocks(w_dwide, slice(0, 4), landing, load_sem.at[1], dwide)
                narrow_loaded()

            columns = pl.ds(pl.multiple_of(j * chunk, 128), chunk)
            value = matmul(row.third[...], dwide[j])
            active = low(jax.nn.gelu(value, approximate=True))
            dpre[:, columns] = value
            dact[:, columns] = active
            part = matmul(active, narrow[columns, :])

            @pl.when(j == 0)
            def first_part():
                dbranch[...] = part

            @pl.when(j > 0)
            def more():
                dbranch[...] = dbranch[...] + part

        @at_tick(DCLOSE)
        def decoder_close():
            value = row.crossed[...] + dbranch[...]
            row.doutput[...] = value
            mean_parts(target_length, value, dbranch[...], 2)

        kinds = range(DCLOSE + 1)
        choose(t, [first_of(kind) for kind in kinds], [pieces[kind] for kind in kinds])
        return unused

    lax.fori_loop(0, len(TICKS), tick, 0)
    swaps[2].wait_recv()
    swaps[3].wait_recv()
    for copy in swaps:
        copy.wait_send()
    for stage in stages:
        stage.sent()


def forward(shards, tile, x, t, c, tc, lengths, target_lengths, buckets, etable, dtable):
    bf, f32 = jnp.bfloat16, jnp.float32
    sems = pltpu.SemaphoreType.DMA
    length, target_count, width = 2 * x.shape[1], 2 * t.shape[1], x.shape[2]
    height, hidden = shards.ew.shape
    fake = lambda *s: jax.ShapeDtypeStruct(s, bf)
    arrays = [
        fake(4, height, width), tile, fake(4, height, width), fake(1, hidden // (8 * CHAIN), width),
        fake(8, height, width), fake(4, height, width), fake(1, hidden // (8 * CHAIN), width),
    ]
    plans = plans_for(arrays)
    shape = lambda s, kind: jax.ShapeDtypeStruct(s, kind)
    rows = [
        shape((length if encoder else target_count, width), f32 if exact else bf)
        for encoder, exact in ROW_KINDS
    ]
    gathered = [
        shape((a.shape[0], CHAIN, 2, 2, 2) + a.shape[1:], bf)
        for i, a in enumerate(arrays)
        if i != 1
    ]
    more = [
        shape((8, width), f32), shape((16, SPAN), f32), shape((16, SPAN), f32), shape((8, 128), f32),
        shape((length, hidden), f32), shape((length, hidden), bf),
        shape((target_count, hidden), f32), shape((target_count, hidden), bf),
    ]
    vmem, hbm = pl.BlockSpec(memory_space=pltpu.VMEM), pl.BlockSpec(memory_space=pltpu.HBM)
    smem = pl.BlockSpec(memory_space=pltpu.SMEM)
    count = len(arrays)
    ordered = shards._replace(en=shards.en[None], dn=shards.dn[None])
    outs = pl.pallas_call(
        functools.partial(forward_kernel, plans),
        out_shape=gathered + rows + more,
        in_specs=[vmem] * 21 + [smem] * 2 + [vmem] * 3,
        out_specs=[hbm] * 6 + [vmem] * len(rows) + [vmem] * 4 + [hbm] * 2 + [vmem] * 2,
        scratch_shapes=[
            pltpu.VMEM((4, height, width), bf),
            pltpu.VMEM((8, height, width), bf),
            pltpu.VMEM((4, height, width), bf),
            pltpu.VMEM((4, height, width), bf),
            pltpu.VMEM((1, CHAIN, 2, 2, 2, 8, 128), bf),
            pltpu.VMEM((length, width), f32),
            pltpu.VMEM((target_count, width), f32),
            sems((len(plans), SLOTS)),
            sems((len(plans), SLOTS)),
            sems((count * 7,)),
            sems((count * 7,)),
            sems((count,)),
            sems((6,)),
            sems((2, 2)),
            sems((4,)),
            sems((4,)),
            pltpu.VMEM((4, width, width), bf),
            pltpu.VMEM((4, width, width), bf),
            pltpu.VMEM((hidden, width), bf),
            pltpu.VMEM((4, width, width), bf),
            pltpu.VMEM((4, CHAIN, 2, 2, 2, height, width), bf),
            pltpu.VMEM((2, length, width), f32),
            pltpu.VMEM((2, length, width), bf),
        ],
        compiler_params=pltpu.CompilerParams(
            collective_id=0, has_side_effects=True, vmem_limit_bytes=62 * 2**20
        ),
    )(*ordered, tile, x, t, c, tc, lengths, target_lengths, buckets, etable, dtable)
    whole = [o.reshape(o.shape[0], -1, o.shape[-1]) for o in outs[:6]]
    joined = [jnp.concatenate([whole[at][j] for j in range(4)], axis=1) for at in (1, 4)]
    weights = Weights(
        *[whole[0][i] for i in range(4)], joined[0], whole[2][0],
        *[whole[3][i] for i in range(8)], joined[1], whole[5][0],
    )
    rows_out = Rows(*outs[6 : 6 + len(rows)])
    gains, etable, dtable, sums, pre, act, dpre, dact = outs[6 + len(rows) :]
    kept = SimpleNamespace(
        **rows_out._asdict(), gains=gains, etable=etable, dtable=dtable, sums=sums, pre=pre, act=act,
        dpre=dpre, dact=dact,
    )
    return weights, kept


def whole_row(halves):
    mine = lax.axis_index("seq")
    keep = lax.dynamic_index_in_dim(halves, mine, 0, keepdims=False)
    other = lax.ppermute(
        lax.dynamic_index_in_dim(halves, 1 - mine, 0, keepdims=False), "seq", [(0, 1), (1, 0)]
    )
    first = jnp.where(mine == 0, keep, other)
    second = jnp.where(mine == 0, other, keep)
    return jnp.concatenate([first, second], axis=0)


def own_slots(row):
    mine = lax.axis_index("seq")
    half = row.shape[0] // 2
    sent = lax.dynamic_slice_in_dim(row, (1 - mine) * half, half, 0).astype(jnp.bfloat16)
    return placed_slots(row, lax.ppermute(sent, "seq", [(0, 1), (1, 0)]))


def placed_slots(row, other):
    mine = lax.axis_index("seq")
    half = row.shape[0] // 2
    keep = lax.dynamic_slice_in_dim(row, mine * half, half, 0)
    other = other.astype(row.dtype)
    return jnp.stack([jnp.where(mine == 0, keep, other), jnp.where(mine == 0, other, keep)])


def matmul_back(grads, weight):
    return dotf(grads, weight, CONTRACT_LAST)


def weight_grad(inputs, grads):
    return dotf(inputs, grads, CONTRACT_FIRST).astype(jnp.bfloat16)


def rms_scale(values, gain_vec):
    return (
        values * lax.rsqrt(jnp.mean(values * values, axis=-1, keepdims=True) + EPSILON) * gain_vec
    )


def gelu_float(values):
    return jax.nn.gelu(values, approximate=True)


def norm_back(values, gain_vec, upstream):
    unused_value, pullback = jax.vjp(rms_scale, values, gain_vec)
    return pullback(upstream)


def widen_grad_of(near, normed, pre_low):
    if not near:
        return weight_grad(normed, pre_low)
    chunk = pre_low.shape[1] // 4
    return [weight_grad(normed, pre_low[:, j * chunk : (j + 1) * chunk]) for j in range(4)]


def feedforward_back(near, normed, pre_values, active, widen, narrow, upstream):
    branch_low = low(upstream)
    narrow_grad = weight_grad(active, branch_low)
    active_grad = matmul_back(branch_low, narrow)
    unused_value, gelu_pull = jax.vjp(gelu_float, pre_values)
    pre_low = low(gelu_pull(active_grad)[0])
    return (matmul_back(pre_low, widen), widen_grad_of(near, normed, pre_low), narrow_grad, pre_low)


def selector_of(buckets):
    ids = jnp.arange(BUCKETS, dtype=jnp.int32)
    return (buckets[:, None] == ids[None, :]).astype(jnp.float32)


def distance_table(table_in, buckets):
    by_distance = jnp.einsum(
        "db,bh->hd", selector_of(buckets), table_in, precision=HIGHEST_PRECISION
    )
    return jnp.pad(by_distance, ((0, 4), (0, SPAN - by_distance.shape[1])))


def by_pair(table):
    return table[:HEADS].reshape(PAIRS, 2, SPAN)


def table_grad(selector, by_distance):
    flat = by_distance.reshape(-1, SPAN)[:HEADS, : selector.shape[0]]
    return jnp.einsum("db,hd->bh", selector, flat, precision=HIGHEST_PRECISION)


def forward_plain(w, gains, x, t, c, tc, lengths_row, target_length, buckets, encoder_table_in, decoder_table_in):
    kept = SimpleNamespace(x=x, target=t, cotangent=c, tcotangent=tc)
    half = x.shape[0] - 1
    encoder_codes, self_codes, cross_codes, valid, target_valid = row_codes(
        lengths_row, target_length, x.shape[0], t.shape[0]
    )
    etable = distance_table(encoder_table_in, buckets)
    dtable = distance_table(decoder_table_in, buckets)
    gain = [gains[i] for i in range(6)]
    residual = x.astype(jnp.float32)
    kept.first = low(rms_scale(residual, gain[0]))
    kept.q, kept.k, kept.v = [low(matmul(kept.first, weight)) for weight in (w.eq, w.ek, w.ev)]
    kept.attended = attn_fwd(
        "segment", half, kept.q, kept.k, kept.v, *encoder_codes, by_pair(etable)
    )
    kept.middle = residual + matmul(kept.attended, w.eo)
    kept.second = low(rms_scale(kept.middle, gain[1]))
    kept.pre = matmul(kept.second, w.ew)
    kept.act = low(gelu_float(kept.pre))
    branch = matmul(kept.act, w.en)
    kept.output = kept.middle + branch
    kept.memory = low(rms_scale(kept.output, gain[2]))
    target = t.astype(jnp.float32)
    kept.own = low(rms_scale(target, gain[3]))
    kept.sq, kept.sk, kept.sv = [low(matmul(kept.own, weight)) for weight in (w.dq, w.dk, w.dv)]
    kept.sattended = attn_fwd(
        "causal", half, kept.sq, kept.sk, kept.sv, *self_codes, by_pair(dtable)
    )
    kept.tmiddle = target + matmul(kept.sattended, w.do)
    kept.cross = low(rms_scale(kept.tmiddle, gain[4]))
    kept.cq = low(matmul(kept.cross, w.cq))
    kept.ck = low(matmul(kept.memory, w.ck))
    kept.cv = low(matmul(kept.memory, w.cv))
    kept.cattended = attn_fwd(
        "cross", half, kept.cq, kept.ck, kept.cv, *cross_codes, None
    )
    kept.crossed = kept.tmiddle + matmul(kept.cattended, w.co)
    kept.third = low(rms_scale(kept.crossed, gain[5]))
    kept.dpre = matmul(kept.third, w.dw)
    kept.dact = low(gelu_float(kept.dpre))
    decoder_branch = matmul(kept.dact, w.dn)
    kept.doutput = kept.crossed + decoder_branch
    kept.gains, kept.etable, kept.dtable = gains, etable, dtable
    keep, target_keep = valid[:, None], target_valid[:, None]
    sums = jnp.stack(
        [
            jnp.sum(jnp.where(keep, kept.output * kept.output, 0.0)),
            jnp.sum(jnp.where(keep, branch * branch, 0.0)),
            jnp.sum(jnp.where(target_keep, kept.doutput * kept.doutput, 0.0)),
            jnp.sum(jnp.where(target_keep, decoder_branch * decoder_branch, 0.0)),
            jnp.sum(valid.astype(jnp.float32)),
            jnp.sum(target_valid.astype(jnp.float32)),
        ]
    )
    kept.sums = sums[:, None]
    return kept


def row_codes(lengths_row, target_length, encoder_length, decoder_length):
    positions = jnp.arange(encoder_length, dtype=jnp.int32)
    target_positions = jnp.arange(decoder_length, dtype=jnp.int32)
    order = jnp.arange(lengths_row.shape[0], dtype=jnp.int32)
    ends = jnp.sum(jnp.where(order[None, :] <= order[:, None], lengths_row[None, :], 0), axis=1)
    segment = jnp.sum((ends[None, :] <= positions[:, None]).astype(jnp.int32), axis=1)
    valid = positions < jnp.sum(lengths_row)
    target_valid = target_positions < target_length
    column = lambda code: code.astype(jnp.int32)[:, None]
    line = lambda code: code.astype(jnp.int32)[None, :]
    return (
        (column(segment), line(segment)),
        (column(target_valid), line(target_valid)),
        (column(target_valid), line(valid)),
        valid,
        target_valid,
    )


def backward(near, w, kept, lengths_row, target_length, buckets, all_lengths):
    half = kept.x.shape[0] - 1
    encoder_codes, self_codes, cross_codes, unused_valid, unused_target = row_codes(
        lengths_row, target_length, kept.x.shape[0], kept.target.shape[0]
    )
    selector = selector_of(buckets)
    encoder_table, decoder_table = by_pair(kept.etable), by_pair(kept.dtable)
    first_gain, second_gain, final_gain, self_gain, cross_gain, third_gain = [
        kept.gains[i] for i in range(6)
    ]
    residual, target = kept.x.astype(jnp.float32), kept.target.astype(jnp.float32)
    first_normed, second_normed = kept.first, kept.second
    queries, keys, values, attended = kept.q, kept.k, kept.v, kept.attended
    middle, output, memory, pre, active = (
        kept.middle, kept.output, kept.memory, kept.pre, kept.act
    )
    self_normed, cross_normed, third_normed = kept.own, kept.cross, kept.third
    self_queries, self_keys, self_values = kept.sq, kept.sk, kept.sv
    cross_queries, cross_keys, cross_values = kept.cq, kept.ck, kept.cv
    self_attended, cross_attended = kept.sattended, kept.cattended
    target_middle, crossed = kept.tmiddle, kept.crossed
    decoder_pre, decoder_active = kept.dpre, kept.dact
    encoder_cotangent, decoder_cotangent = kept.cotangent, kept.tcotangent
    grads = SimpleNamespace()
    upstream = decoder_cotangent.astype(jnp.float32)
    normed_grad, grads.dw, grads.dn, unused_low = feedforward_back(
        near, third_normed, decoder_pre, decoder_active, w.dw, w.dn, upstream
    )
    part, third_gain_grad = norm_back(crossed, third_gain, normed_grad)
    crossed_grad = upstream + part

    crossed_low = low(crossed_grad)
    grads.co = weight_grad(cross_attended, crossed_low)
    mixed_grad = low(matmul_back(crossed_low, w.co))
    query_low, key_low, value_low = attn_bwd(
        "cross", half, cross_queries, cross_keys, cross_values, mixed_grad, *cross_codes, None
    )
    grads.cq = weight_grad(cross_normed, query_low)
    grads.ck = weight_grad(memory, key_low)
    grads.cv = weight_grad(memory, value_low)
    memory_grad = matmul_back(key_low, w.ck) + matmul_back(value_low, w.cv)
    part, cross_gain_grad = norm_back(target_middle, cross_gain, matmul_back(query_low, w.cq))
    middle_grad = crossed_grad + part

    middle_low = low(middle_grad)
    grads.do = weight_grad(self_attended, middle_low)
    mixed_grad = low(matmul_back(middle_low, w.do))
    query_low, key_low, value_low, decoder_distance = attn_bwd(
        "causal", half, self_queries, self_keys, self_values, mixed_grad, *self_codes, decoder_table
    )
    grads.dq = weight_grad(self_normed, query_low)
    grads.dk = weight_grad(self_normed, key_low)
    grads.dv = weight_grad(self_normed, value_low)
    normed_grad = (
        matmul_back(query_low, w.dq)
        + matmul_back(key_low, w.dk)
        + matmul_back(value_low, w.dv)
    )
    part, self_gain_grad = norm_back(target, self_gain, normed_grad)
    decoder_input_grad = middle_grad + part

    part, final_gain_grad = norm_back(output, final_gain, memory_grad)
    output_grad = encoder_cotangent.astype(jnp.float32) + part
    normed_grad, grads.ew, grads.en, pre_low = feedforward_back(
        near, second_normed, pre, active, w.ew, w.en, output_grad
    )
    part, second_gain_grad = norm_back(middle, second_gain, normed_grad)
    encoder_middle_grad = output_grad + part

    middle_low = low(encoder_middle_grad)
    grads.eo = weight_grad(attended, middle_low)
    mixed_grad = low(matmul_back(middle_low, w.eo))
    reduced = None
    if near:
        made, encoder_distance, normed_grad, weight_grads = reduce_with_attention(
            [[grads.dq, grads.dk, grads.dv, grads.do, grads.cq, grads.ck, grads.cv, grads.co]], (False,), queries, keys, values, mixed_grad, first_normed, kept.etable,
            all_lengths, (w.eq, w.ek, w.ev),
            (active, pre_low, second_normed, low(output_grad), attended, middle_low),
        )
        reduced = [made[0][i] for i in range(8)] + scatter_feedforward(grads.dw, grads.dn)
        grads.eq, grads.ek, grads.ev, grads.eo, grads.en = weight_grads[:5]
        grads.ew = weight_grads[5:]
    else:
        query_low, key_low, value_low, encoder_distance = attn_bwd(
            "segment", half, queries, keys, values, mixed_grad, *encoder_codes, encoder_table
        )
        grads.eq = weight_grad(first_normed, query_low)
        grads.ek = weight_grad(first_normed, key_low)
        grads.ev = weight_grad(first_normed, value_low)
        normed_grad = (
            matmul_back(query_low, w.eq)
            + matmul_back(key_low, w.ek)
            + matmul_back(value_low, w.ev)
        )
    part, first_gain_grad = norm_back(residual, first_gain, normed_grad)
    encoder_input_grad = encoder_middle_grad + part

    small = jnp.concatenate(
        [
            first_gain_grad,
            second_gain_grad,
            final_gain_grad,
            self_gain_grad,
            cross_gain_grad,
            third_gain_grad,
            table_grad(selector, encoder_distance).reshape(-1),
            table_grad(selector, decoder_distance).reshape(-1),
            kept.sums[:6, 0],
        ]
    )
    return (output, kept.doutput, encoder_input_grad, decoder_input_grad, grads, small, reduced)


def scatter_feedforward(wide, narrow):
    count = lax.axis_size("rows") * lax.axis_size("seq")
    width = narrow.shape[1]
    parts = [grad.reshape(count, -1, width) for grad in [*wide, narrow]]
    whole = jnp.concatenate(parts, axis=1).reshape(-1, width)
    mine = lax.psum_scatter(whole, BOTH, scatter_dimension=0, tiled=True).astype(jnp.float32)
    share = parts[0].shape[1]
    pieces = [mine[j * share : (j + 1) * share] for j in range(4)]
    return [jnp.concatenate(pieces, axis=1), mine[4 * share :]]


WEIGHT_ARGS = (6, 7, 8, 9, 12, 13, 16, 17, 18, 19, 22, 23, 24, 25, 27, 28)
GAIN_ARGS = (5, 11, 14, 15, 21, 26)
WEIGHT_OUTS = (5, 6, 7, 8, 11, 12, 15, 16, 17, 18, 21, 22, 23, 24, 26, 27)
GAIN_OUTS = (4, 10, 13, 14, 20, 25)


def body(near, *args):
    row_count = lax.axis_size("rows") * lax.axis_size("seq")
    me = lax.axis_index("rows") * lax.axis_size("seq") + lax.axis_index("seq")
    seq_index = lax.axis_index("seq")
    shards = Weights(*[args[i] for i in WEIGHT_ARGS])
    own_gains = jnp.stack([args[i] for i in GAIN_ARGS])
    lengths_row = lax.dynamic_index_in_dim(args[2], seq_index, 0, keepdims=False)
    target_length = lax.dynamic_index_in_dim(args[3], seq_index, 0, keepdims=False)
    if near:
        tile = jnp.pad(own_gains, ((0, 2), (0, 128 - own_gains.shape[1])))[None]
        tables = [jnp.pad(args[i].T, ((0, 4), (0, 0))) for i in (10, 20)]
        line = jnp.pad(args[4], (0, SPAN - args[4].shape[0]), constant_values=-1)[None]
        weights, kept = forward(
            shards, tile, args[0], args[1], args[29], args[30], args[2], args[3][:, None], line, *tables
        )
    else:
        gains = lax.all_gather(own_gains, BOTH, axis=1, tiled=True).astype(jnp.float32)
        weights = Weights(*[lax.all_gather(shard, BOTH, axis=0, tiled=True) for shard in shards])
        rows = [whole_row(args[i]) for i in (0, 1, 29, 30)]
        kept = forward_plain(
            weights, gains, *rows, lengths_row, target_length, args[4], args[10], args[20]
        )
    output, decoder_output, encoder_input_grad, decoder_input_grad, grads, small, decoder_reduced = backward(
        near, weights, kept, lengths_row, target_length, args[4], args[2]
    )
    outs = [None] * 29
    for i, value in ((0, output), (1, decoder_output), (3, decoder_input_grad)):
        outs[i] = own_slots(value)
    if near:
        g = grads
        halves = low(encoder_input_grad).reshape((2, -1) + encoder_input_grad.shape[1:])
        made, small, other = reduce_and_finish(
            [[g.eq, g.ek, g.ev, g.eo], list(g.ew), [g.en]], (False, True, True), small, halves
        )
        reduced = [made[0][i] for i in range(4)] + list(made[1:]) + decoder_reduced
        outs[2] = placed_slots(encoder_input_grad, other)
    else:
        g = grads
        every = Weights(
            g.eq, g.ek, g.ev, g.eo, g.ew, g.en, g.dq, g.dk, g.dv, g.do, g.cq, g.ck, g.cv, g.co, g.dw, g.dn
        )
        reduced = [
            lax.psum_scatter(grad.astype(jnp.float32), BOTH, scatter_dimension=0, tiled=True)
            for grad in every
        ]
        small = lax.psum(small, BOTH)
        outs[2] = own_slots(encoder_input_grad)
    for i, value in zip(WEIGHT_OUTS, reduced):
        outs[i] = value
    feature_count = args[0].shape[2]
    share = feature_count // row_count
    for number, i in enumerate(GAIN_OUTS):
        outs[i] = lax.dynamic_slice_in_dim(small, number * feature_count + me * share, share)
    offset = 6 * feature_count
    size = BUCKETS * HEADS
    outs[9] = small[offset : offset + size].reshape(BUCKETS, HEADS)
    outs[19] = small[offset + size : offset + 2 * size].reshape(BUCKETS, HEADS)
    sums = small[offset + 2 * size :]
    divisors = jnp.stack([sums[4], sums[4], sums[5], sums[5]]) * feature_count
    outs[28] = jnp.sqrt(sums[:4] / divisors)
    return tuple(outs)


def solution(mesh):
    row_spec = P("rows", "seq", None)
    matrix = P(BOTH, None)
    vector = P(BOTH)
    in_specs = [row_spec, row_spec, P("rows", None), P("rows"), P()] + [None] * 26
    in_specs[10] = in_specs[20] = P()
    in_specs[29] = in_specs[30] = row_spec
    for i in GAIN_ARGS:
        in_specs[i] = vector
    for i in WEIGHT_ARGS:
        in_specs[i] = matrix
    out_specs = [row_spec] * 4 + [None] * 25
    out_specs[9] = out_specs[19] = out_specs[28] = P()
    for i in GAIN_OUTS:
        out_specs[i] = vector
    for i in WEIGHT_OUTS:
        out_specs[i] = matrix
    near = mesh.shape["rows"] == 4 * CHAIN and mesh.shape["seq"] == 2
    return jax.shard_map(
        functools.partial(body, near),
        mesh=mesh,
        in_specs=tuple(in_specs),
        out_specs=tuple(out_specs),
        check_vma=False,
    )
```

```python
import functools
from types import SimpleNamespace
from typing import NamedTuple

import jax
import jax.numpy as jnp
from jax import lax
from jax.experimental import pallas as pl
from jax.experimental.pallas import tpu as pltpu
from jax.sharding import PartitionSpec as P

HEADS = 12
BUCKETS = 32
EPSILON = 1e-06
NEGATIVE = -1e30
HIGHEST_PRECISION = lax.Precision.HIGHEST
BOTH = ("rows", "seq")
CHAIN = 4
PAIRS = HEADS // 2

SPAN=1024
CONTRACT_LAST=(((1,),(1,)),((),()))
CONTRACT_FIRST=(((0,),(0,)),((),()))

def dotf(a,b,dims):
    return lax.dot_general(a,b,dims,preferred_element_type=jnp.float32)

def allowed_of(mode,qcode,kcode,shape):
    if mode=="segment":
        return qcode==kcode
    if mode=="causal":
        qi=lax.broadcasted_iota(jnp.int32,shape,0); ki=lax.broadcasted_iota(jnp.int32,shape,1)
        return (ki<=qi)&(qcode==kcode)
    return (qcode==0)|(kcode==1)

def probs_of(q,k,row,allowed,half):
    s=dotf(q,k,CONTRACT_LAST)
    if row is not None:
        wide=jnp.broadcast_to(row,(s.shape[0],SPAN))
        s=s+pltpu.roll(wide,SPAN-half,1,stride=1,stride_axis=0)[:,:s.shape[1]]
    s=jnp.where(allowed,s,NEGATIVE)
    e=jnp.exp(s-jnp.max(s,axis=-1,keepdims=True))
    return e*(1.0/jnp.sum(e,axis=-1,keepdims=True))

def fwd_kernel(mode,half,*refs):
    if mode=="cross":
        q_ref,k_ref,v_ref,qc,kc,o_ref=refs; t_ref=None
    else:
        q_ref,k_ref,v_ref,qc,kc,t_ref,o_ref=refs
    allowed=allowed_of(mode,qc[...],kc[...],(q_ref.shape[0],k_ref.shape[0]))
    for h in range(2):
        sl=slice(64*h,64*h+64)
        p=probs_of(q_ref[:,sl],k_ref[:,sl],None if t_ref is None else t_ref[0,h:h+1,:],allowed,half)
        o_ref[:,sl]=jnp.dot(p.astype(jnp.bfloat16),v_ref[:,sl],preferred_element_type=jnp.float32).astype(jnp.bfloat16)

def bwd_kernel(mode,half,*refs):
    if mode=="cross":
        q_ref,k_ref,v_ref,g_ref,qc,kc,dq_ref,dk_ref,dv_ref=refs; t_ref=None
    else:
        q_ref,k_ref,v_ref,g_ref,qc,kc,t_ref,dq_ref,dk_ref,dv_ref,dt_ref=refs
    allowed=allowed_of(mode,qc[...],kc[...],(q_ref.shape[0],k_ref.shape[0]))
    for h in range(2):
        sl=slice(64*h,64*h+64)
        q=q_ref[:,sl];k=k_ref[:,sl];v=v_ref[:,sl];g=g_ref[:,sl]
        p=probs_of(q,k,None if t_ref is None else t_ref[0,h:h+1,:],allowed,half)
        dv_ref[:,sl]=dotf(p.astype(jnp.bfloat16),g,CONTRACT_FIRST).astype(jnp.bfloat16)
        dp=dotf(g,v,CONTRACT_LAST)
        ds=p*(dp-jnp.sum(dp*p,axis=-1,keepdims=True))
        dsb=ds.astype(jnp.bfloat16)
        dq_ref[:,sl]=jnp.dot(dsb,k,preferred_element_type=jnp.float32).astype(jnp.bfloat16)
        dk_ref[:,sl]=dotf(dsb,q,CONTRACT_FIRST).astype(jnp.bfloat16)
        if t_ref is not None:
            sq=ds.shape[0]
            flip=(lax.broadcasted_iota(jnp.int32,(sq,sq),0)+lax.broadcasted_iota(jnp.int32,(sq,sq),1)==sq-1).astype(jnp.bfloat16)
            flipped=jnp.dot(flip,dsb,preferred_element_type=jnp.float32)
            wide=jnp.concatenate([flipped,jnp.zeros((sq,SPAN-ds.shape[1]),jnp.float32)],axis=1)
            rolled=pltpu.roll(wide,half-(sq-1),1,stride=1,stride_axis=0)
            dt_ref[0,h:h+1,:]=jnp.sum(rolled,axis=0,keepdims=True)

def attn(kernel,mode,half,outs,q,k,v,extra,qc,kc,table):
    sq,width=q.shape; sk=k.shape[0]
    qs=pl.BlockSpec((sq,128),lambda i:(0,i)); ks=pl.BlockSpec((sk,128),lambda i:(0,i))
    ts=pl.BlockSpec((1,2,SPAN),lambda i:(i,0,0))
    ins=[q,k,v]+extra+[qc,kc]; specs=[qs,ks,ks]+[qs]*len(extra)+[pl.BlockSpec((sq,1),lambda i:(0,0)),pl.BlockSpec((1,sk),lambda i:(0,0))]
    if table is not None: ins.append(table); specs.append(ts)
    shapes={"q":(jax.ShapeDtypeStruct((sq,width),jnp.bfloat16),qs),"k":(jax.ShapeDtypeStruct((sk,width),jnp.bfloat16),ks),"t":(jax.ShapeDtypeStruct((width//128,2,SPAN),jnp.float32),ts)}
    return pl.pallas_call(functools.partial(kernel,mode,half),grid=(width//128,),in_specs=specs,
        out_shape=[shapes[o][0] for o in outs],out_specs=[shapes[o][1] for o in outs],
        compiler_params=pltpu.CompilerParams(vmem_limit_bytes=48*2**20))(*ins)

def attn_fwd(mode,half,q,k,v,qc,kc,table):
    return attn(fwd_kernel,mode,half,"q",q,k,v,[],qc,kc,table)[0]
def attn_bwd(mode,half,q,k,v,g,qc,kc,table):
    return attn(bwd_kernel,mode,half,"qkk"+("t" if table is not None else ""),q,k,v,[g],qc,kc,table)


class Place:
    def __init__(self):
        row = lax.axis_index("rows")
        self.z, self.x, self.c, self.y = row // 4, (row // 2) % 2, row % 2, lax.axis_index("seq")

    def device(self, axis):
        z, x, c, y = self.z, self.x, self.c, self.y
        if axis == "up":
            z = z + 1
        if axis == "down":
            z = z - 1
        if axis == "x":
            x = 1 - x
        if axis == "c":
            c = 1 - c
        if axis == "y":
            y = 1 - y
        return {"rows": z * 4 + x * 2 + c, "seq": y}


    def flipped(self, number):
        x, c, y = [
            1 - at if number & bit else at for at, bit in ((self.x, 4), (self.c, 2), (self.y, 1))
        ]
        return {"rows": self.z * 4 + x * 2 + c, "seq": y}

    def along(self, number):
        return {"rows": (self.z + number) % CHAIN * 4 + self.x * 2 + self.c, "seq": self.y}


def greet_all(place):
    barrier = pltpu.get_barrier_semaphore()
    others = [place.flipped(n) for n in range(1, 8)] + [place.along(n) for n in range(1, CHAIN)]
    for device in others:
        pl.semaphore_signal(
            barrier, inc=1, device_id=device, device_id_type=pl.DeviceIdType.MESH
        )
    pl.semaphore_wait(barrier, len(others))


def greet(place):
    barrier = pltpu.get_barrier_semaphore()

    def signal(axis):
        pl.semaphore_signal(
            barrier, inc=1, device_id=place.device(axis), device_id_type=pl.DeviceIdType.MESH
        )

    for axis in "xcy":
        signal(axis)
    pl.when(place.z < CHAIN - 1)(lambda: signal("up"))
    pl.when(place.z > 0)(lambda: signal("down"))
    ends = (place.z == 0) | (place.z == CHAIN - 1)
    pl.when(ends)(lambda: pl.semaphore_wait(barrier, 4))
    pl.when(jnp.logical_not(ends))(lambda: pl.semaphore_wait(barrier, 5))


def third_of(width, third):
    if third is None:
        return slice(None)
    return slice(width // 3 * third, width // 3 * (third + 1))


class GatherStream:
    def __init__(self, place, own, out, third, kind, u, v, send, recv):
        self.place, self.own, self.out, self.third = place, own, out, third
        self.kind, self.u, self.v, self.send, self.recv = kind, u, v, send, recv
        self.span = third_of(own.shape[-1], third)

    def block(self, z, pair):
        p = self.place
        x = slice(None) if pair and self.u == "x" else p.x
        y = slice(None) if pair and self.u == "y" else p.y
        return self.out.at[:, z, x, p.c, y, :, self.span]

    def other(self, z, axis, pair):
        p = self.place
        x, y = p.x, p.y
        if pair and self.u == "x":
            x = slice(None)
        elif axis == "x":
            x = 1 - x
        if pair and self.u == "y":
            y = slice(None)
        elif axis == "y":
            y = 1 - y
        return self.out.at[:, z, x, p.c, y, :, self.span]

    def copy(self, slot, src, dst, axis):
        return pltpu.make_async_remote_copy(
            src_ref=src,
            dst_ref=dst,
            send_sem=self.send.at[slot],
            recv_sem=self.recv.at[slot],
            device_id=self.place.device(axis),
            device_id_type=pl.DeviceIdType.MESH,
        )

    def first(self, z):
        return self.own.at[:, :, self.span]

    def chain_copy(self, up, step):
        pair = self.kind == "B"
        z = self.place.z - (step - 1) if up else self.place.z + (step - 1)
        src = self.first(z) if step == 1 and not pair else self.block(z, pair)
        return self.copy(step - 1 if up else step + 2, src, self.block(z, pair), "up" if up else "down")

    def chain_arrival(self, up, step):
        pair = self.kind == "B"
        z = self.place.z - step if up else self.place.z + step
        ref = self.block(z, pair)
        return self.copy(step - 1 if up else step + 2, ref, ref, "up" if up else "down")

    def sends_at(self, up, step):
        z = self.place.z
        if up:
            return (z < CHAIN - 1) & (z >= step - 1)
        return (z > 0) & (z <= CHAIN - step)

    def arrives_at(self, up, step):
        z = self.place.z
        return z >= step if up else z <= CHAIN - 1 - step

    def side_copy(self, slot, z, axis, pair, fresh):
        src = self.first(z) if fresh else self.block(z, pair)
        return self.copy(slot, src, self.block(z, pair), axis)

    def side_arrival(self, slot, z, axis, pair):
        ref = self.other(z, axis, pair)
        return self.copy(slot, ref, ref, axis)

    def z_of(self, number):
        if number == 0:
            return self.place.z
        return self.place.z - number if number <= CHAIN - 1 else self.place.z + (number - CHAIN + 1)

    def u_copy(self, number):
        return self.side_copy(6 + number, self.z_of(number), self.u, False, number == 0)

    def u_arrival(self, number):
        return self.side_arrival(6 + number, self.z_of(number), self.u, False)

    def v_copy(self, number):
        return self.side_copy(13 + number, self.z_of(number), self.v, True, False)

    def v_arrival(self, number):
        return self.side_arrival(13 + number, self.z_of(number), self.v, True)


SLOTS = 20


def each_arrival(stream, step, act):
    for up in (True, False):
        number = step if up else step + CHAIN - 1
        pl.when(stream.arrives_at(up, step))(functools.partial(act, up, number))


def plans_for(arrays):
    plans = []
    for a, array in enumerate(arrays):
        u, v = ("x", "y") if a % 2 == 0 else ("y", "x")
        if array.shape[-1] % 768 == 0:
            plans += [(a, 0, "B", "x", "y"), (a, 1, "B", "y", "x"), (a, 2, "A", u, v)]
        else:
            plans.append((a, None, "A", u, v))
    return tuple(plans)


def add_into(target, terms, span):
    lead = target.shape[:-2]
    total = 1
    for size in lead:
        total *= size

    def one(flat, unused):
        index = []
        for size in reversed(lead):
            index.insert(0, flat % size)
            flat = flat // size
        value = target[(*index, slice(None), span)].astype(jnp.float32)
        for term in terms:
            value = value + term[(*index, slice(None), span)].astype(jnp.float32)
        target[(*index, slice(None), span)] = value.astype(target.dtype)
        return unused

    lax.fori_loop(0, total, one, 0)


class ReduceStream:
    def __init__(self, place, bufs, third, kind, u, v, send, recv):
        self.place, self.kind, self.u, self.v, self.send, self.recv = place, kind, u, v, send, recv
        self.acc, self.side_v, self.side_u, self.chain = bufs
        self.span = third_of(self.acc.shape[-1], third)

    def z_of(self, number):
        return GatherStream.z_of(self, number)

    def pair(self, z, v_other=False):
        p = self.place
        flip = lambda at: 1 - at if v_other else at
        if self.u == "x":
            return self.acc.at[:, z, :, flip(p.y)]
        return self.acc.at[:, z, flip(p.x), :]

    def single(self, z, u_other=False):
        p = self.place
        x = 1 - p.x if u_other and self.u == "x" else p.x
        y = 1 - p.y if u_other and self.u == "y" else p.y
        return self.acc.at[:, z, x, y]

    def copy(self, slot, src, dst, axis):
        return pltpu.make_async_remote_copy(
            src_ref=src.at[..., self.span],
            dst_ref=dst.at[..., self.span],
            send_sem=self.send.at[slot],
            recv_sem=self.recv.at[slot],
            device_id=self.place.device(axis),
            device_id_type=pl.DeviceIdType.MESH,
        )

    def v_copy(self, number):
        z = self.z_of(number)
        return self.copy(6 + number, self.pair(z, True), self.side_v.at[:, z], self.v)

    def v_add(self, number):
        z = self.z_of(number)
        self.v_copy(number).wait_recv()
        add_into(self.pair(z), [self.side_v.at[:, z]], self.span)

    def u_copy(self, number):
        z = self.z_of(number)
        return self.copy(13 + number, self.single(z, True), self.side_u.at[:, z], self.u)

    def u_add(self, number):
        z = self.z_of(number)
        self.u_copy(number).wait_recv()
        add_into(self.single(z), [self.side_u.at[:, z]], self.span)

    def chain_block(self, z):
        return self.pair(z) if self.kind == "B" else self.single(z)

    def chain_slot(self, up, step):
        at = self.chain.at[:, 0 if up else 1, step - 1]
        return at if self.kind == "B" else at.at[:, 0]

    def chain_copy(self, up, step):
        z = self.place.z + step if up else self.place.z - step
        return self.copy(
            step - 1 if up else step + 2,
            self.chain_block(z),
            self.chain_slot(up, step),
            "up" if up else "down",
        )

    def has_before(self, up):
        return self.place.z > 0 if up else self.place.z < CHAIN - 1

    def chain_arrival(self, up, step):
        ref = self.chain_slot(up, step)
        return self.copy(step - 1 if up else step + 2, ref, ref, "up" if up else "down")

    def chain_step(self, up, step):
        z = self.place.z + step if up else self.place.z - step
        if step < CHAIN - 1:

            @pl.when(self.has_before(up))
            def arrived():
                self.chain_arrival(up, step + 1).wait_recv()
                add_into(self.chain_block(z), [self.chain_slot(up, step + 1)], self.span)

        self.chain_copy(up, step).start()

    def chain_end(self):
        for up in (True, False):

            @pl.when(self.has_before(up))
            def arrived():
                self.chain_arrival(up, 1).wait_recv()
                add_into(self.chain_block(self.place.z), [self.chain_slot(up, 1)], self.span)


class Reduction:
    def __init__(self, place, plans, items, outs, bufs, sems):
        count = len(items)
        self.place, self.plans, self.items, self.outs = place, plans, items, outs
        send, recv, self.core_send, self.core_recv, self.local = sems
        self.accs, self.cores = bufs[:count], bufs[count : 2 * count]
        self.streams = [
            ReduceStream(
                place, [bufs[k * count + a] for k in (0, 2, 3, 4)], third, kind, u, v,
                send.at[i], recv.at[i],
            )
            for i, (a, third, kind, u, v) in enumerate(plans)
        ]

    def z_of(self, number):
        return GatherStream.z_of(self, number)

    def valid(self, number):
        z = self.place.z
        return z >= number if number < CHAIN else z <= 2 * (CHAIN - 1) - number

    def at(self, number, act):
        if number == 0:
            act(0)
        else:
            pl.when(self.valid(number))(functools.partial(act, number))

    def each(self, act):
        for number in NUMBERS:
            self.at(number, act)

    def begin(self):
        def loads(number):
            z = self.z_of(number)
            for a, refs in enumerate(self.items):
                for i, ref in enumerate(refs):
                    pltpu.make_async_copy(
                        ref.at[z, :, self.place.c],
                        self.accs[a].at[i, z],
                        self.local.at[a * 7 + number],
                    ).start()

        self.each(loads)

    def core_copy(self, a, number, src, dst):
        return pltpu.make_async_remote_copy(
            src_ref=src,
            dst_ref=dst,
            send_sem=self.core_send.at[a * 7 + number],
            recv_sem=self.core_recv.at[a * 7 + number],
            device_id=self.place.device("c"),
            device_id_type=pl.DeviceIdType.MESH,
        )

    def begin_core(self):
        def sends(number):
            z = self.z_of(number)
            for a, refs in enumerate(self.items):
                for i, ref in enumerate(refs):
                    self.core_copy(
                        a, number, ref.at[z, :, 1 - self.place.c], self.cores[a].at[i, z]
                    ).start()

        self.each(sends)

    def core_whole(self, a, number):
        whole = self.cores[a].at[:, self.z_of(number)]
        return self.core_copy(a, number, whole, whole)

    def first(self, number):
        z = self.z_of(number)
        for a in range(len(self.items)):
            whole = self.accs[a].at[:, z]
            pltpu.make_async_copy(whole, whole, self.local.at[a * 7 + number]).wait()
            self.core_whole(a, number).wait_recv()
            add_into(whole, [self.cores[a].at[:, z]], slice(None))
            for s, plan in zip(self.streams, self.plans):
                if plan[0] == a:
                    s.v_copy(number).start()

    def onward(self, s, number):
        up = number >= CHAIN
        s.chain_step(up, number - (CHAIN - 1) if up else number)

    def second(self, number):
        for s in self.streams:
            s.v_add(number)
            if s.kind == "A":
                s.u_copy(number).start()
            elif number > 0:
                self.onward(s, number)

    def third(self, number):
        for s in self.streams:
            if s.kind == "A":
                s.u_add(number)
                if number > 0:
                    self.onward(s, number)

    def events(self):
        return [
            functools.partial(self.at, number, act)
            for act in (self.first, self.second, self.third)
            for number in NUMBERS
        ]

    def end(self):
        for s in self.streams:
            if s.kind == "B":
                s.chain_end()
                s.u_copy(0).start()
        for s in self.streams:
            if s.kind == "A":
                s.chain_end()
        for s in self.streams:
            if s.kind == "B":
                s.u_add(0)
        p = self.place
        for acc, refs in zip(self.accs, self.outs):
            width = acc.shape[-1]
            for item in range(acc.shape[0]):
                value = acc[item, p.z, p.x, p.y].astype(jnp.float32)
                if len(refs[0].shape) == 3:
                    refs[0][item] = value
                else:
                    refs[0][:, item * width : (item + 1) * width] = value

        def last(number):
            for a in range(len(self.items)):
                self.core_whole(a, number).wait_send()
            for s in self.streams:
                s.v_copy(number).wait_send()
                if s.kind == "A" or number == 0:
                    s.u_copy(number).wait_send()
                if number > 0:
                    up = number >= CHAIN
                    s.chain_copy(up, number - (CHAIN - 1) if up else number).wait_send()

        self.each(last)


NUMBERS = (3, 6, 2, 5, 1, 4, 0)


def reduction_parts(groups, joined):
    parts = 8 * CHAIN
    items = [
        [g.reshape(CHAIN, 2, 2, 2, g.shape[0] // parts, g.shape[1]) for g in group] for group in groups
    ]
    shapes = [jax.ShapeDtypeStruct((len(i),) + i[0].shape[-2:], i[0].dtype) for i in items]
    plans = plans_for(shapes)
    count = len(items)
    scratch = [
        pltpu.VMEM((a.shape[0],) + lead + a.shape[-2:], a.dtype)
        for lead in ((CHAIN, 2, 2), (CHAIN, 2, 2), (CHAIN, 2), (CHAIN,), (2, CHAIN - 1, 2))
        for a in shapes
    ]
    sems = pltpu.SemaphoreType.DMA
    scratch += [sems((len(plans), SLOTS))] * 2 + [sems((count * 7,))] * 3
    outs = []
    for a, whole in zip(shapes, joined):
        shape = (a.shape[1], a.shape[0] * a.shape[2]) if whole else a.shape
        outs.append([jax.ShapeDtypeStruct(shape, jnp.float32)])
    return items, plans, scratch, outs


def heads_backward(half, pair, q_ref, k_ref, v_ref, g_ref, qc, kc, t_ref, dq_ref, dk_ref, dv_ref, dt_ref):
    lanes = pl.ds(pl.multiple_of(pair * 128, 128), 128)
    q2, k2, v2, g2 = q_ref[:, lanes], k_ref[:, lanes], v_ref[:, lanes], g_ref[:, lanes]
    size = q2.shape[0]
    allowed = qc == kc
    turn = lax.broadcasted_iota(jnp.int32, (size, size), 0) + lax.broadcasted_iota(
        jnp.int32, (size, size), 1
    )
    flip = (turn == size - 1).astype(jnp.bfloat16)
    made = []
    for h in range(2):
        sl = slice(64 * h, 64 * h + 64)
        q, k, v, g = q2[:, sl], k2[:, sl], v2[:, sl], g2[:, sl]
        p = probs_of(q, k, t_ref[pl.ds(2 * pair + h, 1), :], allowed, half)
        dv = dotf(p.astype(jnp.bfloat16), g, CONTRACT_FIRST)
        dp = dotf(g, v, CONTRACT_LAST)
        ds = (p * (dp - jnp.sum(dp * p, axis=-1, keepdims=True))).astype(jnp.bfloat16)
        dq = jnp.dot(ds, k, preferred_element_type=jnp.float32)
        dk = dotf(ds, q, CONTRACT_FIRST)
        made.append((dq, dk, dv))
        flipped = jnp.dot(flip, ds, preferred_element_type=jnp.float32)
        wide = jnp.concatenate([flipped, jnp.zeros((size, SPAN - size), jnp.float32)], axis=1)
        rolled = pltpu.roll(wide, half - (size - 1), 1, stride=1, stride_axis=0)
        dt_ref[pl.ds(2 * pair + h, 1), :] = jnp.sum(rolled, axis=0, keepdims=True)
    for ref, pieces in zip((dq_ref, dk_ref, dv_ref), zip(*made)):
        ref[:, lanes] = jnp.concatenate(pieces, axis=1).astype(jnp.bfloat16)


def choose(t, starts, acts):
    if len(acts) == 1:
        acts[0]()
        return
    middle = len(acts) // 2

    @pl.when(t < starts[middle])
    def before():
        choose(t, starts[:middle], acts[:middle])

    @pl.when(t >= starts[middle])
    def after():
        choose(t, starts[middle:], acts[middle:])


BACK_TICKS = ((), (0, 1), (2, 3), (4, 5), (6,), (7, 8), (9,), (10,), (11,), (12,), (13,), (14,), (15,), (16,), (17,), (18,), (19,), (20,))


def backward_kernel(plans, counts, out_counts, half, *refs):
    refs = list(refs)
    take = lambda n: [refs.pop(0) for unused in range(n)]
    items = [take(n) for n in counts]
    q, k, v, g, first, etable, lengths = take(7)
    weights = take(3)
    act, pre_low, second, branch_low, attended, middle_low = take(6)
    outs = [take(n) for n in out_counts]
    dist, normed = take(2)
    grads = take(3)
    outward, narrow = take(2)
    wide = take(4)
    bufs = take(5 * len(counts))
    sems = take(5)
    derived = take(3)
    place = Place()
    run = Reduction(place, plans, items, outs, bufs, sems)
    run.begin()
    greet(place)
    run.begin_core()
    size = q.shape[0]

    def segment(axis):
        shape = (size, 1) if axis == 0 else (1, size)
        at = lax.broadcasted_iota(jnp.int32, shape, axis)
        code, end = jnp.zeros(shape, jnp.int32), 0
        for j in range(lengths.shape[1]):
            end = end + lengths[place.y, j]
            code = code + (end <= at).astype(jnp.int32)
        return code

    events = run.events()

    def tick(t, unused):
        def some(numbers):
            for number in numbers:
                events[number]()

        choose(t, list(range(len(BACK_TICKS))), [functools.partial(some, n) for n in BACK_TICKS])

        @pl.when(t < PAIRS)
        def attention():
            heads_backward(half, t, q, k, v, g, segment(0), segment(1), etable, *derived, dist)

        for i in range(3):

            @pl.when(t == PAIRS + i)
            def project():
                grads[i][...] = dotf(first[...], derived[i][...], CONTRACT_FIRST).astype(jnp.bfloat16)
                part = dotf(derived[i][...], weights[i][...], CONTRACT_LAST)
                normed[...] = part if i == 0 else normed[...] + part

        rest = PAIRS + 3

        @pl.when(t == rest)
        def outward_grad():
            outward[...] = dotf(attended[...], middle_low[...], CONTRACT_FIRST).astype(jnp.bfloat16)

        width = second.shape[1]

        @pl.when((t > rest) & (t <= rest + 4))
        def narrow_grad():
            at = pl.ds(pl.multiple_of((t - rest - 1) * width, 128), width)
            narrow[at] = dotf(act[:, at], branch_low[...], CONTRACT_FIRST).astype(jnp.bfloat16)

        for j in range(4):

            @pl.when(t == rest + 5 + j)
            def wide_grad():
                at = slice(j * width, (j + 1) * width)
                wide[j][...] = dotf(second[...], pre_low[:, at], CONTRACT_FIRST).astype(jnp.bfloat16)

        return unused

    lax.fori_loop(0, len(BACK_TICKS), tick, 0)
    run.end()


def reduce_with_attention(groups, joined, q, k, v, g, first, etable, lengths, weights, others):
    items, plans, scratch, out_groups = reduction_parts(groups, joined)
    flat = [i for group in items for i in group]
    out_shapes = [o for group in out_groups for o in group]
    counts = tuple(len(i) for i in items), tuple(len(o) for o in out_groups)
    vmem, hbm = pl.BlockSpec(memory_space=pltpu.VMEM), pl.BlockSpec(memory_space=pltpu.HBM)
    length, width = q.shape
    outs = pl.pallas_call(
        functools.partial(backward_kernel, plans, *counts, length - 1),
        out_shape=out_shapes
        + [
            jax.ShapeDtypeStruct((16, SPAN), jnp.float32),
            jax.ShapeDtypeStruct((length, width), jnp.float32),
        ]
        + [jax.ShapeDtypeStruct((width, width), jnp.bfloat16)] * 4
        + [jax.ShapeDtypeStruct((others[0].shape[1], width), jnp.bfloat16)]
        + [jax.ShapeDtypeStruct((width, width), jnp.bfloat16)] * 4,
        in_specs=[hbm] * len(flat)
        + [vmem] * 6
        + [pl.BlockSpec(memory_space=pltpu.SMEM)]
        + [vmem] * 9,
        out_specs=[vmem] * (len(out_shapes) + 11),
        scratch_shapes=scratch + [pltpu.VMEM((length, width), jnp.bfloat16)] * 3,
        compiler_params=pltpu.CompilerParams(
            collective_id=1, has_side_effects=True, vmem_limit_bytes=62 * 2**20
        ),
    )(*flat, q, k, v, g, first, etable, lengths, *weights, *others)
    count = len(out_shapes)
    return outs[:count], outs[count], outs[count + 1], outs[count + 2 :]


def finish_kernel(plans, counts, out_counts, *refs):
    refs = list(refs)
    take = lambda n: [refs.pop(0) for unused in range(n)]
    items = [take(n) for n in counts]
    small, halves = take(2)
    outs = [take(n) for n in out_counts]
    total, theirs = take(2)
    bufs = take(5 * len(counts))
    sems = take(5)
    near_in, far_in, subtotal, near_send, near_recv, far_send, far_recv = take(7)
    half_send, half_recv = take(2)
    place = Place()
    run = Reduction(place, plans, items, outs, bufs, sems)
    run.begin()
    greet_all(place)
    run.begin_core()
    half = pltpu.make_async_remote_copy(
        src_ref=halves.at[1 - place.y],
        dst_ref=theirs,
        send_sem=half_send.at[0],
        recv_sem=half_recv.at[0],
        device_id=place.device("y"),
        device_id_type=pl.DeviceIdType.MESH,
    )
    half.start()
    def near(number):
        return pltpu.make_async_remote_copy(
            src_ref=small,
            dst_ref=near_in.at[number - 1],
            send_sem=near_send.at[number - 1],
            recv_sem=near_recv.at[number - 1],
            device_id=place.flipped(number),
            device_id_type=pl.DeviceIdType.MESH,
        )

    def far(number):
        return pltpu.make_async_remote_copy(
            src_ref=subtotal,
            dst_ref=far_in.at[number - 1],
            send_sem=far_send.at[number - 1],
            recv_sem=far_recv.at[number - 1],
            device_id=place.along(number),
            device_id_type=pl.DeviceIdType.MESH,
        )

    for number in range(1, 8):
        near(number).start()
    for number, event in enumerate(run.events()):
        event()
        if number == 9:
            value = small[...]
            for other in range(1, 8):
                near(other).wait_recv()
                value = value + near_in[other - 1]
            subtotal[...] = value
            for other in range(1, CHAIN):
                far(other).start()
    value = subtotal[...]
    for other in range(1, CHAIN):
        far(other).wait_recv()
        value = value + far_in[other - 1]
    total[...] = value
    run.end()
    half.wait_recv()
    half.wait_send()
    for number in range(1, 8):
        near(number).wait_send()
    for number in range(1, CHAIN):
        far(number).wait_send()


def reduce_and_finish(groups, joined, small, halves):
    items, plans, scratch, out_groups = reduction_parts(groups, joined)
    flat = [i for group in items for i in group]
    out_shapes = [o for group in out_groups for o in group]
    counts = tuple(len(i) for i in items), tuple(len(o) for o in out_groups)
    vmem, hbm = pl.BlockSpec(memory_space=pltpu.VMEM), pl.BlockSpec(memory_space=pltpu.HBM)
    sems = pltpu.SemaphoreType.DMA
    lines = -(-small.shape[0] // 1024) * 8
    padded = jnp.pad(small, (0, lines * 128 - small.shape[0])).reshape(lines, 128)
    block = jax.ShapeDtypeStruct((lines, 128), jnp.float32)
    outs = pl.pallas_call(
        functools.partial(finish_kernel, plans, *counts),
        out_shape=out_shapes + [block, jax.ShapeDtypeStruct(halves.shape[1:], halves.dtype)],
        in_specs=[hbm] * len(flat) + [vmem] * 2,
        out_specs=[vmem] * (len(out_shapes) + 2),
        scratch_shapes=scratch
        + [pltpu.VMEM((n, lines, 128), jnp.float32) for n in (7, CHAIN - 1)]
        + [pltpu.VMEM((lines, 128), jnp.float32)]
        + [sems((n,)) for n in (7, 7, CHAIN - 1, CHAIN - 1, 1, 1)],
        compiler_params=pltpu.CompilerParams(
            collective_id=2, has_side_effects=True, vmem_limit_bytes=62 * 2**20
        ),
    )(*flat, padded, halves)
    return outs[:-2], outs[-2].reshape(-1)[: small.shape[0]], outs[-1]


class GatherStage:
    def __init__(self, place, streams, items, sems):
        self.place, self.streams, self.items = place, streams, items
        self.core_send, self.core_recv, self.local = sems

    def own_copy(self, k):
        a, own, out = self.items[k]
        p = self.place
        return pltpu.make_async_copy(own, out.at[:, p.z, p.x, p.c, p.y], self.local.at[a])

    def core_copy(self, k, number, arriving):
        a, own, out = self.items[k]
        z = GatherStream.z_of(self.streams[0], number)
        ref = out.at[:, z, :, 1 - self.place.c if arriving else self.place.c]
        return pltpu.make_async_remote_copy(
            src_ref=ref,
            dst_ref=ref,
            send_sem=self.core_send.at[a * 7 + number],
            recv_sem=self.core_recv.at[a * 7 + number],
            device_id=self.place.device("c"),
            device_id_type=pl.DeviceIdType.MESH,
        )

    def start(self):
        for k in range(len(self.items)):
            self.own_copy(k).start()
        for s in self.streams:
            s.u_copy(0).start()
            if s.kind == "A":
                self.chain_start(s)

    def chain_start(self, s):
        for up in (True, False):
            pl.when(s.sends_at(up, 1))(lambda: s.chain_copy(up, 1).start())

    def after_u(self):
        for k in range(len(self.items)):
            self.own_copy(k).wait()
        for s in self.streams:
            s.u_arrival(0).wait_recv()
            if s.kind == "B":
                self.chain_start(s)
            s.v_copy(0).start()

    def arrivals(self, step):
        def arrival(s, up, number):
            s.chain_arrival(up, step).wait_recv()
            if step < CHAIN - 1:
                pl.when(s.sends_at(up, step + 1))(lambda: s.chain_copy(up, step + 1).start())
            if s.kind == "A":
                s.u_copy(number).start()
            else:
                s.v_copy(number).start()

        for s in self.streams:
            each_arrival(s, step, functools.partial(arrival, s))

    def sides(self, step):
        def side(s, up, number):
            s.u_arrival(number).wait_recv()
            s.v_copy(number).start()

        for s in self.streams:
            if s.kind == "A":
                each_arrival(s, step, functools.partial(side, s))

    def finish(self, number):
        for s in self.streams:
            s.v_arrival(number).wait_recv()
        for k in range(len(self.items)):
            self.core_copy(k, number, False).start()

    def finishes(self, step):
        each_arrival(self.streams[0], step, lambda up, number: self.finish(number))

    def last(self):
        def one(up, number):
            for k in range(len(self.items)):
                self.core_copy(k, number, True).wait_recv()

        one(True, 0)
        for step in range(1, CHAIN):
            each_arrival(self.streams[0], step, one)

    def events(self):
        steps = range(1, CHAIN)
        moves = [
            act
            for step in steps
            for act in (functools.partial(self.arrivals, step), functools.partial(self.sides, step))
        ]
        ends = [functools.partial(self.finishes, step) for step in steps]
        return [self.start, self.after_u] + moves + [lambda: self.finish(0)] + ends + [self.last]

    def sent(self):
        def one(up, number):
            for k in range(len(self.items)):
                self.core_copy(k, number, False).wait_send()
            for s in self.streams:
                if s.kind == "A":
                    s.u_copy(number).wait_send()
                s.v_copy(number).wait_send()

        one(True, 0)
        for s in self.streams:
            if s.kind == "B":
                s.u_copy(0).wait_send()
            for step in range(1, CHAIN):
                for up in (True, False):
                    pl.when(s.sends_at(up, step))(lambda: s.chain_copy(up, step).wait_send())
        for step in range(1, CHAIN):
            each_arrival(self.streams[0], step, one)


class Weights(NamedTuple):
    eq: jax.Array
    ek: jax.Array
    ev: jax.Array
    eo: jax.Array
    ew: jax.Array
    en: jax.Array
    dq: jax.Array
    dk: jax.Array
    dv: jax.Array
    do: jax.Array
    cq: jax.Array
    ck: jax.Array
    cv: jax.Array
    co: jax.Array
    dw: jax.Array
    dn: jax.Array


class Rows(NamedTuple):
    x: jax.Array
    first: jax.Array
    q: jax.Array
    k: jax.Array
    v: jax.Array
    attended: jax.Array
    middle: jax.Array
    second: jax.Array
    output: jax.Array
    memory: jax.Array
    ck: jax.Array
    cv: jax.Array
    cotangent: jax.Array
    target: jax.Array
    own: jax.Array
    sq: jax.Array
    sk: jax.Array
    sv: jax.Array
    sattended: jax.Array
    tmiddle: jax.Array
    cross: jax.Array
    cq: jax.Array
    cattended: jax.Array
    crossed: jax.Array
    third: jax.Array
    doutput: jax.Array
    tcotangent: jax.Array


ROW_KINDS = (
    (True, False),
    (True, False),
    (True, False),
    (True, False),
    (True, False),
    (True, False),
    (True, True),
    (True, False),
    (True, True),
    (True, False),
    (True, False),
    (True, False),
    (True, False),
    (False, False),
    (False, False),
    (False, False),
    (False, False),
    (False, False),
    (False, False),
    (False, True),
    (False, False),
    (False, False),
    (False, False),
    (False, True),
    (False, False),
    (False, True),
    (False, False),
)
GROUP_ARRAYS = ((0, 1), (2, 3), (4,), (5, 6))
(
    TABLES, BEGIN, QKV, ATTEND, JOIN, FFN, CLOSE, SELF, SELF_ATTEND, CROSS, CROSS_ATTEND, CROSSED,
    DFFN, DCLOSE,
) = range(14)
TICKS = (
    (TABLES, ((0, 0),)),
    (BEGIN, (
        (0, 1), (0, 2), (0, 3), (0, 4), (1, 0), (1, 1), (0, 5), (0, 6), (0, 7), (0, 8), (0, 9),
        (1, 2), (0, 10), (0, 11), (1, 3), (0, 12),
    )),
    (QKV, ()),
    (ATTEND, ((1, 4),)),
    (ATTEND, ((2, 0), (2, 1), (1, 5))),
    (ATTEND, ((1, 6),)),
    (ATTEND, ((1, 7),)),
    (ATTEND, ((2, 2), (1, 8), (1, 9))),
    (ATTEND, ((2, 3), (1, 10))),
    (JOIN, ((1, 11), (2, 4), (3, 0), (3, 1), (1, 12))),
    (FFN, ((2, 5),)),
    (FFN, ((2, 6),)),
    (FFN, ((2, 7),)),
    (FFN, ((3, 2), (2, 8), (2, 9))),
    (CLOSE, ((3, 3), (2, 10))),
    (SELF, ((3, 4), (2, 11), (2, 12))),
    (SELF_ATTEND, ((3, 5),)),
    (CROSS, ((3, 6),)),
    (CROSS_ATTEND, ((3, 7), (3, 8))),
    (CROSS_ATTEND, ((3, 9),)),
    (CROSSED, ((3, 10),)),
    (DFFN, ((3, 11), (3, 12))),
    (DFFN, ()), (DFFN, ()), (DFFN, ()),
    (DCLOSE, ()),
)


def first_of(kind):
    return [k for k, unused in TICKS].index(kind)


def load_blocks(src, items, landing, sem, dst):
    height, width = landing.shape[-2:]
    copy = pltpu.make_async_copy(src.at[items], landing, sem)
    copy.start()
    copy.wait()

    def one(flat, unused):
        z, x, c = flat // 4, (flat // 2) % 2, flat % 2
        rows = pl.ds(pl.multiple_of(flat * 2 * height, 2 * height), 2 * height)
        for item in range(landing.shape[0]):
            pair = [landing[item, z, x, c, y].astype(jnp.float32) for y in range(2)]
            dst[item, rows] = jnp.concatenate(pair, axis=0).astype(dst.dtype)
        return unused

    lax.fori_loop(0, 4 * CHAIN, one, 0)


def matmul(left, right):
    return jnp.dot(left, right, preferred_element_type=jnp.float32)


def low(values):
    return values.astype(jnp.bfloat16)


def rms_of(values, gain):
    return (
        values * lax.rsqrt(jnp.mean(values * values, axis=-1, keepdims=True) + EPSILON) * gain
    )


def heads_forward(mode, half, pair, q_ref, k_ref, v_ref, o_ref, qc, kc, t_ref):
    lanes = pl.ds(pl.multiple_of(pair * 128, 128), 128)
    q2, k2, v2 = q_ref[:, lanes], k_ref[:, lanes], v_ref[:, lanes]
    allowed = allowed_of(mode, qc, kc, (q2.shape[0], k2.shape[0]))
    mixed = []
    for h in range(2):
        sl = slice(64 * h, 64 * h + 64)
        row = None if t_ref is None else t_ref[pl.ds(2 * pair + h, 1), :]
        p = probs_of(q2[:, sl], k2[:, sl], row, allowed, half)
        mixed.append(matmul(low(p), v2[:, sl]))
    o_ref[:, lanes] = low(jnp.concatenate(mixed, axis=1))


def forward_kernel(plans, *refs):
    refs = list(refs)
    take = lambda n: [refs.pop(0) for unused in range(n)]
    shards = Weights(*take(16))
    tile, halves_x, halves_t, halves_c, halves_tc = take(5)
    lengths, target_lengths, buckets, etable_in, dtable_in = take(5)
    w_sq, w_wide, w_narrow, w_dsq, w_dwide, w_dnarrow = take(6)
    row = Rows(*take(len(ROW_KINDS)))
    gains, etable, dtable, sums, pre_hbm, act_hbm, dpre, dact = take(8)
    stack_e, stack_d, stack_w, stack_dw, gbuf, branch, dbranch = take(7)
    send, recv, core_send, core_recv, local, load_sem, store_sem, swap_send, swap_recv = take(9)
    sq, wide, narrow, dwide, landing, pre, act = take(7)
    place = Place()
    mine = place.y
    half = row.x.shape[0] - 1

    for i in range(4):
        stack_e[i] = shards[i][...]
    for i in range(8):
        stack_d[i] = shards[6 + i][...]
    for j in range(4):
        columns = slice(j * stack_w.shape[2], (j + 1) * stack_w.shape[2])
        stack_w[j] = shards.ew[:, columns]
        stack_dw[j] = shards.dw[:, columns]
    owns = [stack_e, tile, stack_w, shards.en, stack_d, stack_dw, shards.dn]
    hbm = [w_sq, None, w_wide, w_narrow, w_dsq, w_dwide, w_dnarrow]
    full = [gbuf if out is None else out for out in hbm]
    stages = []
    for group in GROUP_ARRAYS:
        streams = [
            GatherStream(place, owns[a], full[a], third, kind, u, v, send.at[i], recv.at[i])
            for i, (a, third, kind, u, v) in enumerate(plans)
            if a in group
        ]
        items = [(a, owns[a], full[a]) for a in group]
        stages.append(GatherStage(place, streams, items, (core_send, core_recv, local)))

    def half_copy(number, halves, whole):
        size = halves.shape[1]
        return pltpu.make_async_remote_copy(
            src_ref=halves.at[1 - mine],
            dst_ref=whole.at[pl.ds(pl.multiple_of(mine * size, 64), size)],
            send_sem=swap_send.at[number],
            recv_sem=swap_recv.at[number],
            device_id=place.device("y"),
            device_id_type=pl.DeviceIdType.MESH,
        )

    swaps = [
        half_copy(0, halves_x, row.x),
        half_copy(1, halves_t, row.target),
        half_copy(2, halves_c, row.cotangent),
        half_copy(3, halves_tc, row.tcotangent),
    ]
    for halves, whole in (
        (halves_x, row.x),
        (halves_t, row.target),
        (halves_c, row.cotangent),
        (halves_tc, row.tcotangent),
    ):
        size = halves.shape[1]
        whole[pl.ds(pl.multiple_of(mine * size, 64), size)] = halves[mine]
    greet(place)

    count = lengths.shape[1]
    ends, total = [], 0
    for j in range(count):
        total = total + lengths[mine, j]
        ends.append(total)
    target_length = target_lengths[mine, 0]

    def codes(size, axis):
        shape = (size, 1) if axis == 0 else (1, size)
        at = lax.broadcasted_iota(jnp.int32, shape, axis)
        segment = jnp.zeros(shape, jnp.int32)
        for end in ends:
            segment = segment + (end <= at).astype(jnp.int32)
        return at, segment

    length, target_count = row.x.shape[0], row.target.shape[0]

    def mean_parts(kept, first, second, rows):
        keep = lax.broadcasted_iota(jnp.int32, (first.shape[0], 1), 0) < kept
        for i, value in enumerate((first, second)):
            total_square = jnp.sum(jnp.where(keep, value * value, 0.0))
            sums[rows + i : rows + i + 1, :] = jnp.full((1, 128), total_square, jnp.float32)
        sums[rows // 2 + 4 : rows // 2 + 5, :] = jnp.full((1, 128), kept.astype(jnp.float32))

    def load_narrow(src):
        return [
            pltpu.make_async_copy(
                src.at[0, z, x, c, y],
                narrow.at[pl.ds((((z * 2 + x) * 2 + c) * 2 + y) * src.shape[5], src.shape[5])],
                load_sem.at[0],
            )
            for z in range(CHAIN)
            for x in range(2)
            for c in range(2)
            for y in range(2)
        ]

    def narrow_loaded():
        pltpu.make_async_copy(narrow, narrow, load_sem.at[0]).wait()

    chunk = row.x.shape[1]
    chunks = wide.shape[0]

    def store(j, slot):
        columns = pl.ds(pl.multiple_of(j * chunk, 128), chunk)
        return (
            pltpu.make_async_copy(pre.at[slot], pre_hbm.at[:, columns], store_sem.at[0, slot]),
            pltpu.make_async_copy(act.at[slot], act_hbm.at[:, columns], store_sem.at[1, slot]),
        )

    def tick(t, unused):
        pieces = {}

        def at_tick(kind):
            def keep(act):
                pieces[kind] = act
                return act

            return keep

        def comm(events):
            for stage, number in events:
                stages[stage].events()[number]()

        choose(
            t, list(range(len(TICKS))), [functools.partial(comm, events) for unused, events in TICKS]
        )

        @at_tick(TABLES)
        def tables():
            swaps[0].start()
            swaps[1].start()
            for table_in, table in ((etable_in, etable), (dtable_in, dtable)):
                value = jnp.zeros(table.shape, jnp.float32)
                for b in range(BUCKETS):
                    value = value + jnp.where(buckets[...] == b, table_in[:, b : b + 1], 0.0)
                table[...] = value

        @at_tick(BEGIN)
        def begin():
            load_blocks(w_sq, slice(0, 4), landing, load_sem.at[1], sq)
            tiles = gbuf.at[0]
            value = jnp.zeros(gains.shape, jnp.float32)
            share = gains.shape[1] // (8 * CHAIN)
            for d in range(8 * CHAIN):
                z, x, c, y = d // 8, (d // 4) % 2, (d // 2) % 2, d % 2
                part = tiles[z, x, c, y].astype(jnp.float32)
                spread = jnp.concatenate(
                    [part, jnp.zeros((8, gains.shape[1] - 128), jnp.float32)], axis=1
                )
                value = value + (pltpu.roll(spread, share * d, 1) if d else spread)
            gains[...] = value
            swaps[0].wait_recv()
            swaps[1].wait_recv()
            row.first[...] = low(rms_of(row.x[...].astype(jnp.float32), value[0:1, :]))

        @at_tick(QKV)
        def project():
            for i, ref in enumerate((row.q, row.k, row.v)):
                ref[...] = low(matmul(row.first[...], sq[i]))

        @at_tick(ATTEND)
        def attention():
            heads_forward(
                "segment", half, t - first_of(ATTEND), row.q, row.k, row.v, row.attended,
                codes(length, 0)[1], codes(length, 1)[1], etable,
            )

        @at_tick(JOIN)
        def join():
            for copy in load_narrow(w_narrow):
                copy.start()
            value = row.x[...].astype(jnp.float32) + matmul(row.attended[...], sq[3])
            row.middle[...] = value
            row.second[...] = low(rms_of(value, gains[1:2, :]))
            load_blocks(w_wide, slice(0, 4), landing, load_sem.at[1], wide)
            narrow_loaded()

        @at_tick(FFN)
        def feedforward():
            j = t - first_of(FFN)
            slot = lax.rem(j, 2)

            @pl.when(j >= 2)
            def stored():
                for copy in store(j - 2, slot):
                    copy.wait()

            columns = pl.ds(pl.multiple_of(j * chunk, 128), chunk)
            value = matmul(row.second[...], wide[j])
            active = low(jax.nn.gelu(value, approximate=True))
            pre[slot] = value
            act[slot] = active
            for copy in store(j, slot):
                copy.start()
            part = matmul(active, narrow[columns, :])

            @pl.when(j == 0)
            def first_part():
                branch[...] = part

            @pl.when(j > 0)
            def more():
                branch[...] = branch[...] + part

        @at_tick(CLOSE)
        def close():
            value = row.middle[...] + branch[...]
            row.output[...] = value
            row.memory[...] = low(rms_of(value, gains[2:3, :]))
            mean_parts(total, value, branch[...], 0)
            swaps[2].start()
            swaps[3].start()
            for j in (chunks - 2, chunks - 1):
                for copy in store(j, j % 2):
                    copy.wait()

        @at_tick(SELF)
        def self_project():
            load_blocks(w_dsq, slice(0, 4), landing, load_sem.at[1], sq)
            load_blocks(w_dsq, slice(4, 8), landing, load_sem.at[1], wide)
            normed = low(rms_of(row.target[...].astype(jnp.float32), gains[3:4, :]))
            row.own[...] = normed
            for i, ref in enumerate((row.sq, row.sk, row.sv)):
                ref[...] = low(matmul(normed, sq[i]))
            row.ck[...] = low(matmul(row.memory[...], wide[1]))
            row.cv[...] = low(matmul(row.memory[...], wide[2]))

        def valid_code(size, axis, limit):
            return (codes(size, axis)[0] < limit).astype(jnp.int32)

        @at_tick(SELF_ATTEND)
        def self_attention():
            def one(pair, unused):
                heads_forward(
                    "causal", half, pair, row.sq, row.sk, row.sv, row.sattended,
                    valid_code(target_count, 0, target_length),
                    valid_code(target_count, 1, target_length), dtable,
                )
                return unused

            lax.fori_loop(0, PAIRS, one, 0)

        @at_tick(CROSS)
        def self_join():
            value = row.target[...].astype(jnp.float32) + matmul(row.sattended[...], sq[3])
            row.tmiddle[...] = value
            normed = low(rms_of(value, gains[4:5, :]))
            row.cross[...] = normed
            row.cq[...] = low(matmul(normed, wide[0]))

        @at_tick(CROSS_ATTEND)
        def cross_attention():
            def one(pair, unused):
                heads_forward(
                    "cross", half, pair, row.cq, row.ck, row.cv, row.cattended,
                    valid_code(target_count, 0, target_length), valid_code(length, 1, total), None,
                )
                return unused

            begin_pair = (t - first_of(CROSS_ATTEND)) * (PAIRS // 2)
            lax.fori_loop(begin_pair, begin_pair + PAIRS // 2, one, 0)

        @at_tick(CROSSED)
        def cross_join():
            value = row.tmiddle[...] + matmul(row.cattended[...], wide[3])
            row.crossed[...] = value
            row.third[...] = low(rms_of(value, gains[5:6, :]))

        @at_tick(DFFN)
        def decoder_feedforward():
            j = t - first_of(DFFN)

            @pl.when(j == 0)
            def decoder_load():
                for copy in load_narrow(w_dnarrow):
                    copy.start()
                load_blocks(w_dwide, slice(0, 4), landing, load_sem.at[1], dwide)
                narrow_loaded()

            columns = pl.ds(pl.multiple_of(j * chunk, 128), chunk)
            value = matmul(row.third[...], dwide[j])
            active = low(jax.nn.gelu(value, approximate=True))
            dpre[:, columns] = value
            dact[:, columns] = active
            part = matmul(active, narrow[columns, :])

            @pl.when(j == 0)
            def first_part():
                dbranch[...] = part

            @pl.when(j > 0)
            def more():
                dbranch[...] = dbranch[...] + part

        @at_tick(DCLOSE)
        def decoder_close():
            value = row.crossed[...] + dbranch[...]
            row.doutput[...] = value
            mean_parts(target_length, value, dbranch[...], 2)

        kinds = range(DCLOSE + 1)
        choose(t, [first_of(kind) for kind in kinds], [pieces[kind] for kind in kinds])
        return unused

    lax.fori_loop(0, len(TICKS), tick, 0)
    swaps[2].wait_recv()
    swaps[3].wait_recv()
    for copy in swaps:
        copy.wait_send()
    for stage in stages:
        stage.sent()


def forward(shards, tile, x, t, c, tc, lengths, target_lengths, buckets, etable, dtable):
    bf, f32 = jnp.bfloat16, jnp.float32
    sems = pltpu.SemaphoreType.DMA
    length, target_count, width = 2 * x.shape[1], 2 * t.shape[1], x.shape[2]
    height, hidden = shards.ew.shape
    fake = lambda *s: jax.ShapeDtypeStruct(s, bf)
    arrays = [
        fake(4, height, width), tile, fake(4, height, width), fake(1, hidden // (8 * CHAIN), width),
        fake(8, height, width), fake(4, height, width), fake(1, hidden // (8 * CHAIN), width),
    ]
    plans = plans_for(arrays)
    shape = lambda s, kind: jax.ShapeDtypeStruct(s, kind)
    rows = [
        shape((length if encoder else target_count, width), f32 if exact else bf)
        for encoder, exact in ROW_KINDS
    ]
    gathered = [
        shape((a.shape[0], CHAIN, 2, 2, 2) + a.shape[1:], bf)
        for i, a in enumerate(arrays)
        if i != 1
    ]
    more = [
        shape((8, width), f32), shape((16, SPAN), f32), shape((16, SPAN), f32), shape((8, 128), f32),
        shape((length, hidden), f32), shape((length, hidden), bf),
        shape((target_count, hidden), f32), shape((target_count, hidden), bf),
    ]
    vmem, hbm = pl.BlockSpec(memory_space=pltpu.VMEM), pl.BlockSpec(memory_space=pltpu.HBM)
    smem = pl.BlockSpec(memory_space=pltpu.SMEM)
    count = len(arrays)
    ordered = shards._replace(en=shards.en[None], dn=shards.dn[None])
    outs = pl.pallas_call(
        functools.partial(forward_kernel, plans),
        out_shape=gathered + rows + more,
        in_specs=[vmem] * 21 + [smem] * 2 + [vmem] * 3,
        out_specs=[hbm] * 6 + [vmem] * len(rows) + [vmem] * 4 + [hbm] * 2 + [vmem] * 2,
        scratch_shapes=[
            pltpu.VMEM((4, height, width), bf),
            pltpu.VMEM((8, height, width), bf),
            pltpu.VMEM((4, height, width), bf),
            pltpu.VMEM((4, height, width), bf),
            pltpu.VMEM((1, CHAIN, 2, 2, 2, 8, 128), bf),
            pltpu.VMEM((length, width), f32),
            pltpu.VMEM((target_count, width), f32),
            sems((len(plans), SLOTS)),
            sems((len(plans), SLOTS)),
            sems((count * 7,)),
            sems((count * 7,)),
            sems((count,)),
            sems((6,)),
            sems((2, 2)),
            sems((4,)),
            sems((4,)),
            pltpu.VMEM((4, width, width), bf),
            pltpu.VMEM((4, width, width), bf),
            pltpu.VMEM((hidden, width), bf),
            pltpu.VMEM((4, width, width), bf),
            pltpu.VMEM((4, CHAIN, 2, 2, 2, height, width), bf),
            pltpu.VMEM((2, length, width), f32),
            pltpu.VMEM((2, length, width), bf),
        ],
        compiler_params=pltpu.CompilerParams(
            collective_id=0, has_side_effects=True, vmem_limit_bytes=62 * 2**20
        ),
    )(*ordered, tile, x, t, c, tc, lengths, target_lengths, buckets, etable, dtable)
    whole = [o.reshape(o.shape[0], -1, o.shape[-1]) for o in outs[:6]]
    joined = [jnp.concatenate([whole[at][j] for j in range(4)], axis=1) for at in (1, 4)]
    weights = Weights(
        *[whole[0][i] for i in range(4)], joined[0], whole[2][0],
        *[whole[3][i] for i in range(8)], joined[1], whole[5][0],
    )
    rows_out = Rows(*outs[6 : 6 + len(rows)])
    gains, etable, dtable, sums, pre, act, dpre, dact = outs[6 + len(rows) :]
    kept = SimpleNamespace(
        **rows_out._asdict(), gains=gains, etable=etable, dtable=dtable, sums=sums, pre=pre, act=act,
        dpre=dpre, dact=dact,
    )
    return weights, kept


def whole_row(halves):
    mine = lax.axis_index("seq")
    keep = lax.dynamic_index_in_dim(halves, mine, 0, keepdims=False)
    other = lax.ppermute(
        lax.dynamic_index_in_dim(halves, 1 - mine, 0, keepdims=False), "seq", [(0, 1), (1, 0)]
    )
    first = jnp.where(mine == 0, keep, other)
    second = jnp.where(mine == 0, other, keep)
    return jnp.concatenate([first, second], axis=0)


def own_slots(row):
    mine = lax.axis_index("seq")
    half = row.shape[0] // 2
    sent = lax.dynamic_slice_in_dim(row, (1 - mine) * half, half, 0).astype(jnp.bfloat16)
    return placed_slots(row, lax.ppermute(sent, "seq", [(0, 1), (1, 0)]))


def placed_slots(row, other):
    mine = lax.axis_index("seq")
    half = row.shape[0] // 2
    keep = lax.dynamic_slice_in_dim(row, mine * half, half, 0)
    other = other.astype(row.dtype)
    return jnp.stack([jnp.where(mine == 0, keep, other), jnp.where(mine == 0, other, keep)])


def matmul_back(grads, weight):
    return dotf(grads, weight, CONTRACT_LAST)


def weight_grad(inputs, grads):
    return dotf(inputs, grads, CONTRACT_FIRST).astype(jnp.bfloat16)


def rms_scale(values, gain_vec):
    return (
        values * lax.rsqrt(jnp.mean(values * values, axis=-1, keepdims=True) + EPSILON) * gain_vec
    )


def gelu_float(values):
    return jax.nn.gelu(values, approximate=True)


def norm_back(values, gain_vec, upstream):
    unused_value, pullback = jax.vjp(rms_scale, values, gain_vec)
    return pullback(upstream)


def widen_grad_of(near, normed, pre_low):
    if not near:
        return weight_grad(normed, pre_low)
    chunk = pre_low.shape[1] // 4
    return [weight_grad(normed, pre_low[:, j * chunk : (j + 1) * chunk]) for j in range(4)]


def feedforward_back(near, normed, pre_values, active, widen, narrow, upstream):
    branch_low = low(upstream)
    narrow_grad = weight_grad(active, branch_low)
    active_grad = matmul_back(branch_low, narrow)
    unused_value, gelu_pull = jax.vjp(gelu_float, pre_values)
    pre_low = low(gelu_pull(active_grad)[0])
    return (matmul_back(pre_low, widen), widen_grad_of(near, normed, pre_low), narrow_grad, pre_low)


def selector_of(buckets):
    ids = jnp.arange(BUCKETS, dtype=jnp.int32)
    return (buckets[:, None] == ids[None, :]).astype(jnp.float32)


def distance_table(table_in, buckets):
    by_distance = jnp.einsum(
        "db,bh->hd", selector_of(buckets), table_in, precision=HIGHEST_PRECISION
    )
    return jnp.pad(by_distance, ((0, 4), (0, SPAN - by_distance.shape[1])))


def by_pair(table):
    return table[:HEADS].reshape(PAIRS, 2, SPAN)


def table_grad(selector, by_distance):
    flat = by_distance.reshape(-1, SPAN)[:HEADS, : selector.shape[0]]
    return jnp.einsum("db,hd->bh", selector, flat, precision=HIGHEST_PRECISION)


def forward_plain(w, gains, x, t, c, tc, lengths_row, target_length, buckets, encoder_table_in, decoder_table_in):
    kept = SimpleNamespace(x=x, target=t, cotangent=c, tcotangent=tc)
    half = x.shape[0] - 1
    encoder_codes, self_codes, cross_codes, valid, target_valid = row_codes(
        lengths_row, target_length, x.shape[0], t.shape[0]
    )
    etable = distance_table(encoder_table_in, buckets)
    dtable = distance_table(decoder_table_in, buckets)
    gain = [gains[i] for i in range(6)]
    residual = x.astype(jnp.float32)
    kept.first = low(rms_scale(residual, gain[0]))
    kept.q, kept.k, kept.v = [low(matmul(kept.first, weight)) for weight in (w.eq, w.ek, w.ev)]
    kept.attended = attn_fwd(
        "segment", half, kept.q, kept.k, kept.v, *encoder_codes, by_pair(etable)
    )
    kept.middle = residual + matmul(kept.attended, w.eo)
    kept.second = low(rms_scale(kept.middle, gain[1]))
    kept.pre = matmul(kept.second, w.ew)
    kept.act = low(gelu_float(kept.pre))
    branch = matmul(kept.act, w.en)
    kept.output = kept.middle + branch
    kept.memory = low(rms_scale(kept.output, gain[2]))
    target = t.astype(jnp.float32)
    kept.own = low(rms_scale(target, gain[3]))
    kept.sq, kept.sk, kept.sv = [low(matmul(kept.own, weight)) for weight in (w.dq, w.dk, w.dv)]
    kept.sattended = attn_fwd(
        "causal", half, kept.sq, kept.sk, kept.sv, *self_codes, by_pair(dtable)
    )
    kept.tmiddle = target + matmul(kept.sattended, w.do)
    kept.cross = low(rms_scale(kept.tmiddle, gain[4]))
    kept.cq = low(matmul(kept.cross, w.cq))
    kept.ck = low(matmul(kept.memory, w.ck))
    kept.cv = low(matmul(kept.memory, w.cv))
    kept.cattended = attn_fwd(
        "cross", half, kept.cq, kept.ck, kept.cv, *cross_codes, None
    )
    kept.crossed = kept.tmiddle + matmul(kept.cattended, w.co)
    kept.third = low(rms_scale(kept.crossed, gain[5]))
    kept.dpre = matmul(kept.third, w.dw)
    kept.dact = low(gelu_float(kept.dpre))
    decoder_branch = matmul(kept.dact, w.dn)
    kept.doutput = kept.crossed + decoder_branch
    kept.gains, kept.etable, kept.dtable = gains, etable, dtable
    keep, target_keep = valid[:, None], target_valid[:, None]
    sums = jnp.stack(
        [
            jnp.sum(jnp.where(keep, kept.output * kept.output, 0.0)),
            jnp.sum(jnp.where(keep, branch * branch, 0.0)),
            jnp.sum(jnp.where(target_keep, kept.doutput * kept.doutput, 0.0)),
            jnp.sum(jnp.where(target_keep, decoder_branch * decoder_branch, 0.0)),
            jnp.sum(valid.astype(jnp.float32)),
            jnp.sum(target_valid.astype(jnp.float32)),
        ]
    )
    kept.sums = sums[:, None]
    return kept


def row_codes(lengths_row, target_length, encoder_length, decoder_length):
    positions = jnp.arange(encoder_length, dtype=jnp.int32)
    target_positions = jnp.arange(decoder_length, dtype=jnp.int32)
    order = jnp.arange(lengths_row.shape[0], dtype=jnp.int32)
    ends = jnp.sum(jnp.where(order[None, :] <= order[:, None], lengths_row[None, :], 0), axis=1)
    segment = jnp.sum((ends[None, :] <= positions[:, None]).astype(jnp.int32), axis=1)
    valid = positions < jnp.sum(lengths_row)
    target_valid = target_positions < target_length
    column = lambda code: code.astype(jnp.int32)[:, None]
    line = lambda code: code.astype(jnp.int32)[None, :]
    return (
        (column(segment), line(segment)),
        (column(target_valid), line(target_valid)),
        (column(target_valid), line(valid)),
        valid,
        target_valid,
    )


def backward(near, w, kept, lengths_row, target_length, buckets, all_lengths):
    half = kept.x.shape[0] - 1
    encoder_codes, self_codes, cross_codes, unused_valid, unused_target = row_codes(
        lengths_row, target_length, kept.x.shape[0], kept.target.shape[0]
    )
    selector = selector_of(buckets)
    encoder_table, decoder_table = by_pair(kept.etable), by_pair(kept.dtable)
    first_gain, second_gain, final_gain, self_gain, cross_gain, third_gain = [
        kept.gains[i] for i in range(6)
    ]
    residual, target = kept.x.astype(jnp.float32), kept.target.astype(jnp.float32)
    first_normed, second_normed = kept.first, kept.second
    queries, keys, values, attended = kept.q, kept.k, kept.v, kept.attended
    middle, output, memory, pre, active = (
        kept.middle, kept.output, kept.memory, kept.pre, kept.act
    )
    self_normed, cross_normed, third_normed = kept.own, kept.cross, kept.third
    self_queries, self_keys, self_values = kept.sq, kept.sk, kept.sv
    cross_queries, cross_keys, cross_values = kept.cq, kept.ck, kept.cv
    self_attended, cross_attended = kept.sattended, kept.cattended
    target_middle, crossed = kept.tmiddle, kept.crossed
    decoder_pre, decoder_active = kept.dpre, kept.dact
    encoder_cotangent, decoder_cotangent = kept.cotangent, kept.tcotangent
    grads = SimpleNamespace()
    upstream = decoder_cotangent.astype(jnp.float32)
    normed_grad, grads.dw, grads.dn, unused_low = feedforward_back(
        near, third_normed, decoder_pre, decoder_active, w.dw, w.dn, upstream
    )
    part, third_gain_grad = norm_back(crossed, third_gain, normed_grad)
    crossed_grad = upstream + part

    crossed_low = low(crossed_grad)
    grads.co = weight_grad(cross_attended, crossed_low)
    mixed_grad = low(matmul_back(crossed_low, w.co))
    query_low, key_low, value_low = attn_bwd(
        "cross", half, cross_queries, cross_keys, cross_values, mixed_grad, *cross_codes, None
    )
    grads.cq = weight_grad(cross_normed, query_low)
    grads.ck = weight_grad(memory, key_low)
    grads.cv = weight_grad(memory, value_low)
    memory_grad = matmul_back(key_low, w.ck) + matmul_back(value_low, w.cv)
    part, cross_gain_grad = norm_back(target_middle, cross_gain, matmul_back(query_low, w.cq))
    middle_grad = crossed_grad + part

    middle_low = low(middle_grad)
    grads.do = weight_grad(self_attended, middle_low)
    mixed_grad = low(matmul_back(middle_low, w.do))
    query_low, key_low, value_low, decoder_distance = attn_bwd(
        "causal", half, self_queries, self_keys, self_values, mixed_grad, *self_codes, decoder_table
    )
    grads.dq = weight_grad(self_normed, query_low)
    grads.dk = weight_grad(self_normed, key_low)
    grads.dv = weight_grad(self_normed, value_low)
    normed_grad = (
        matmul_back(query_low, w.dq)
        + matmul_back(key_low, w.dk)
        + matmul_back(value_low, w.dv)
    )
    part, self_gain_grad = norm_back(target, self_gain, normed_grad)
    decoder_input_grad = middle_grad + part

    part, final_gain_grad = norm_back(output, final_gain, memory_grad)
    output_grad = encoder_cotangent.astype(jnp.float32) + part
    normed_grad, grads.ew, grads.en, pre_low = feedforward_back(
        near, second_normed, pre, active, w.ew, w.en, output_grad
    )
    part, second_gain_grad = norm_back(middle, second_gain, normed_grad)
    encoder_middle_grad = output_grad + part

    middle_low = low(encoder_middle_grad)
    grads.eo = weight_grad(attended, middle_low)
    mixed_grad = low(matmul_back(middle_low, w.eo))
    reduced = None
    if near:
        made, encoder_distance, normed_grad, weight_grads = reduce_with_attention(
            [[grads.dq, grads.dk, grads.dv, grads.do, grads.cq, grads.ck, grads.cv, grads.co]], (False,), queries, keys, values, mixed_grad, first_normed, kept.etable,
            all_lengths, (w.eq, w.ek, w.ev),
            (active, pre_low, second_normed, low(output_grad), attended, middle_low),
        )
        reduced = [made[0][i] for i in range(8)] + scatter_feedforward(grads.dw, grads.dn)
        grads.eq, grads.ek, grads.ev, grads.eo, grads.en = weight_grads[:5]
        grads.ew = weight_grads[5:]
    else:
        query_low, key_low, value_low, encoder_distance = attn_bwd(
            "segment", half, queries, keys, values, mixed_grad, *encoder_codes, encoder_table
        )
        grads.eq = weight_grad(first_normed, query_low)
        grads.ek = weight_grad(first_normed, key_low)
        grads.ev = weight_grad(first_normed, value_low)
        normed_grad = (
            matmul_back(query_low, w.eq)
            + matmul_back(key_low, w.ek)
            + matmul_back(value_low, w.ev)
        )
    part, first_gain_grad = norm_back(residual, first_gain, normed_grad)
    encoder_input_grad = encoder_middle_grad + part

    small = jnp.concatenate(
        [
            first_gain_grad,
            second_gain_grad,
            final_gain_grad,
            self_gain_grad,
            cross_gain_grad,
            third_gain_grad,
            table_grad(selector, encoder_distance).reshape(-1),
            table_grad(selector, decoder_distance).reshape(-1),
            kept.sums[:6, 0],
        ]
    )
    return (output, kept.doutput, encoder_input_grad, decoder_input_grad, grads, small, reduced)


def scatter_feedforward(wide, narrow):
    count = lax.axis_size("rows") * lax.axis_size("seq")
    width = narrow.shape[1]
    parts = [grad.reshape(count, -1, width) for grad in [*wide, narrow]]
    whole = jnp.concatenate(parts, axis=1).reshape(-1, width)
    mine = lax.psum_scatter(whole, BOTH, scatter_dimension=0, tiled=True).astype(jnp.float32)
    share = parts[0].shape[1]
    pieces = [mine[j * share : (j + 1) * share] for j in range(4)]
    return [jnp.concatenate(pieces, axis=1), mine[4 * share :]]


WEIGHT_ARGS = (6, 7, 8, 9, 12, 13, 16, 17, 18, 19, 22, 23, 24, 25, 27, 28)
GAIN_ARGS = (5, 11, 14, 15, 21, 26)
WEIGHT_OUTS = (5, 6, 7, 8, 11, 12, 15, 16, 17, 18, 21, 22, 23, 24, 26, 27)
GAIN_OUTS = (4, 10, 13, 14, 20, 25)


def body(near, *args):
    row_count = lax.axis_size("rows") * lax.axis_size("seq")
    me = lax.axis_index("rows") * lax.axis_size("seq") + lax.axis_index("seq")
    seq_index = lax.axis_index("seq")
    shards = Weights(*[args[i] for i in WEIGHT_ARGS])
    own_gains = jnp.stack([args[i] for i in GAIN_ARGS])
    lengths_row = lax.dynamic_index_in_dim(args[2], seq_index, 0, keepdims=False)
    target_length = lax.dynamic_index_in_dim(args[3], seq_index, 0, keepdims=False)
    if near:
        tile = jnp.pad(own_gains, ((0, 2), (0, 128 - own_gains.shape[1])))[None]
        tables = [jnp.pad(args[i].T, ((0, 4), (0, 0))) for i in (10, 20)]
        line = jnp.pad(args[4], (0, SPAN - args[4].shape[0]), constant_values=-1)[None]
        weights, kept = forward(
            shards, tile, args[0], args[1], args[29], args[30], args[2], args[3][:, None], line, *tables
        )
    else:
        gains = lax.all_gather(own_gains, BOTH, axis=1, tiled=True).astype(jnp.float32)
        weights = Weights(*[lax.all_gather(shard, BOTH, axis=0, tiled=True) for shard in shards])
        rows = [whole_row(args[i]) for i in (0, 1, 29, 30)]
        kept = forward_plain(
            weights, gains, *rows, lengths_row, target_length, args[4], args[10], args[20]
        )
    output, decoder_output, encoder_input_grad, decoder_input_grad, grads, small, decoder_reduced = backward(
        near, weights, kept, lengths_row, target_length, args[4], args[2]
    )
    outs = [None] * 29
    for i, value in ((0, output), (1, decoder_output), (3, decoder_input_grad)):
        outs[i] = own_slots(value)
    if near:
        g = grads
        halves = low(encoder_input_grad).reshape((2, -1) + encoder_input_grad.shape[1:])
        made, small, other = reduce_and_finish(
            [[g.eq, g.ek, g.ev, g.eo], list(g.ew), [g.en]], (False, True, True), small, halves
        )
        reduced = [made[0][i] for i in range(4)] + list(made[1:]) + decoder_reduced
        outs[2] = placed_slots(encoder_input_grad, other)
    else:
        g = grads
        every = Weights(
            g.eq, g.ek, g.ev, g.eo, g.ew, g.en, g.dq, g.dk, g.dv, g.do, g.cq, g.ck, g.cv, g.co, g.dw, g.dn
        )
        reduced = [
            lax.psum_scatter(grad.astype(jnp.float32), BOTH, scatter_dimension=0, tiled=True)
            for grad in every
        ]
        small = lax.psum(small, BOTH)
        outs[2] = own_slots(encoder_input_grad)
    for i, value in zip(WEIGHT_OUTS, reduced):
        outs[i] = value
    feature_count = args[0].shape[2]
    share = feature_count // row_count
    for number, i in enumerate(GAIN_OUTS):
        outs[i] = lax.dynamic_slice_in_dim(small, number * feature_count + me * share, share)
    offset = 6 * feature_count
    size = BUCKETS * HEADS
    outs[9] = small[offset : offset + size].reshape(BUCKETS, HEADS)
    outs[19] = small[offset + size : offset + 2 * size].reshape(BUCKETS, HEADS)
    sums = small[offset + 2 * size :]
    divisors = jnp.stack([sums[4], sums[4], sums[5], sums[5]]) * feature_count
    outs[28] = jnp.sqrt(sums[:4] / divisors)
    return tuple(outs)


def solution(mesh):
    row_spec = P("rows", "seq", None)
    matrix = P(BOTH, None)
    vector = P(BOTH)
    in_specs = [row_spec, row_spec, P("rows", None), P("rows"), P()] + [None] * 26
    in_specs[10] = in_specs[20] = P()
    in_specs[29] = in_specs[30] = row_spec
    for i in GAIN_ARGS:
        in_specs[i] = vector
    for i in WEIGHT_ARGS:
        in_specs[i] = matrix
    out_specs = [row_spec] * 4 + [None] * 25
    out_specs[9] = out_specs[19] = out_specs[28] = P()
    for i in GAIN_OUTS:
        out_specs[i] = vector
    for i in WEIGHT_OUTS:
        out_specs[i] = matrix
    near = mesh.shape["rows"] == 4 * CHAIN and mesh.shape["seq"] == 2
    return jax.shard_map(
        functools.partial(body, near),
        mesh=mesh,
        in_specs=tuple(in_specs),
        out_specs=tuple(out_specs),
        check_vma=False,
    )
```
